256 devices in a mesh: freq: 8 (over z), lat: 8 (over x, y_hi), lon: 4 (over y_lo, core).
Axes of the slice: x: 4, y: 4 (y_hi: 2, y_lo: 2; y = y_hi * 2 + y_lo), z: 8, core: 2. Of those that a mesh axis runs over, the one named last changes fastest.
Arguments:
- direction: float32 [3, 32, 1024, 2048], P(None, 'freq', 'lat', 'lon'), may hold values from -6 to 6
- base_flow: float32 [2, 32, 1024, 2048], P(None, 'freq', 'lat', 'lon'), may hold values from -2 to 2
- water_depth: float32 [1024, 2048], P('lat', 'lon'), may hold values from 0.5 to 2
- drag_factor: float32 [1024, 2048], P('lat', 'lon'), may hold values from 0.2 to 2
- wet_mask: int32 [1024, 2048], P('lat', 'lon'), may hold values 0 or 1
Outputs:
- result: float32 [3, 32, 1024, 2048], P(None, 'freq', 'lat', 'lon')
The draws below stay inside these ranges and needn't reach their ends.
All inputs are finite; a program needn't handle non-finite values. No bound on the sum of `wet_mask` on one device may be relied on, other than what follows from the above.
Results may differ from the reference program's by a relative error of at most 0.000071.
Values sent between devices are 32-bit elements; how exact they have to be, the bound alone decides.
A program may use at most 128 MiB of HBM per device.

```python
import math
import jax
import jax.numpy as jnp
from jax import lax

NCON = 16
NTIME = 256
NLAT = 1024
NLON = 2048


def set_ends(result, own_key, least, largest):
    shape = result.shape
    place = [jax.random.randint(jax.random.fold_in(own_key, axis), (), 0, shape[axis]) for axis in range(len(shape))]
    result = result.at[tuple(place)].set(least)
    longest = shape.index(max(shape))
    place[longest] = (place[longest] + 1) % shape[longest]
    return result.at[tuple(place)].set(largest)


def levels(own_key, shape, pieces, least, largest):
    def one(position, shards_of):
        draws = jax.random.uniform(jax.random.fold_in(jax.random.fold_in(own_key, 6), position), (shards_of,), jnp.float32, least / len(pieces), largest / len(pieces))
        return jnp.repeat(jnp.exp(draws), shape[position] // shards_of).reshape((-1,) + (1,) * (len(shape) - position - 1))

    gain = one(*pieces[0])
    for cut in pieces[1:]:
        gain = gain * one(*cut)
    return gain


def scatter_about(stream_key, dims, scale, bound, pieces=(), kind=jnp.bfloat16):
    entries = jax.random.normal(stream_key, dims, jnp.float32) * scale
    if len(pieces) > 0:
        entries = levels(stream_key, dims, pieces, -0.22, 0.18) * entries
    return jnp.clip(entries, min=-bound, max=bound).astype(kind)


def setup_inputs(seed: int = 0) -> dict:
    keys = jax.random.split(jax.random.key(seed), 6)
    return {
        "direction": scatter_about(keys[0], (3, 2 * NCON, NLAT, NLON), 1.0, 6.0, ((1, 8), (2, 8), (3, 4)), jnp.float32),
        "base_flow": scatter_about(keys[1], (2, 2 * NCON, NLAT, NLON), 0.3, 2.0, ((1, 8), (2, 8), (3, 4)), jnp.float32),
        "water_depth": jnp.clip(jnp.exp(math.log(2.0) - 1.3862944 * jax.random.uniform(keys[2], (NLAT, NLON), jnp.float32) ** levels(keys[2], (NLAT, NLON), ((0, 8), (1, 4)), -0.2, 0.2)), 0.5, 2.0),
        "drag_factor": jnp.clip(jnp.exp(math.log(2.0) - 2.3025851 * jax.random.uniform(keys[3], (NLAT, NLON), jnp.float32) ** levels(keys[3], (NLAT, NLON), ((0, 8), (1, 4)), -0.2, 0.2)), 0.2, 2.0),
        "wet_mask": set_ends((jax.random.randint(keys[4], (NLAT, NLON), 0, 4) < 3).astype(jnp.int32), jax.random.fold_in(keys[4], 1), 0, 1),
    }


LINEAR_DRAG = 0.5
GRAVITY = 1.0
OMEGA_STEP = 0.25
SPEED_SOFT = 0.01

def samples_table(sample_count, constituents):
    sample_index = jnp.arange(sample_count, dtype=jnp.int32)
    harmonic = jnp.arange(1, constituents + 1, dtype=jnp.int32)
    wrapped_turns = sample_index[:, None] * harmonic[None, :] % sample_count
    phase_angle = wrapped_turns.astype(jnp.float32) * (2.0 * math.pi / sample_count)
    table = jnp.stack([jnp.cos(phase_angle), jnp.sin(phase_angle)], axis=2)
    return table.reshape(sample_count, 2 * constituents)

def rotation_of(row_index, total_rows):
    return 0.5 + (row_index.astype(jnp.float32) + 0.5) / total_rows

def tendency(values, angular):
    cos_sin = values.reshape((values.shape[0] // 2, 2) + values.shape[1:])
    moved = jnp.stack([angular * cos_sin[:, 1], -angular * cos_sin[:, 0]], axis=1)
    return moved.reshape(values.shape)

def linear_residual(extended, tile_rows, tile_cols, angular, rotation):

    def neighbour(plane, row_step, col_step):
        return extended[plane, :, 1 + row_step:1 + row_step + tile_rows, 1 + col_step:1 + col_step + tile_cols]
    height = neighbour(0, 0, 0)
    east = neighbour(1, 0, 0)
    north = neighbour(2, 0, 0)
    res_height = tendency(height, angular) + neighbour(3, 0, 0) - neighbour(3, 0, -1) + neighbour(4, 0, 0) - neighbour(4, -1, 0)
    north_mean = 0.25 * (north + neighbour(2, 0, 1) + neighbour(2, -1, 0) + neighbour(2, -1, 1))
    east_mean = 0.25 * (east + neighbour(1, 0, -1) + neighbour(1, 1, 0) + neighbour(1, 1, -1))
    res_east = tendency(east, angular) + LINEAR_DRAG * east - rotation * north_mean + GRAVITY * (neighbour(0, 0, 1) - height)
    res_north = tendency(north, angular) + LINEAR_DRAG * north + rotation * east_mean + GRAVITY * (neighbour(0, 1, 0) - height)
    return jnp.stack([res_height, res_east, res_north])

def friction_row(row_block, drag_row, table):
    highest = lax.Precision.HIGHEST
    series = jnp.einsum('tc,fcn->ftn', table, row_block, precision=highest)
    base_east, base_north, step_east, step_north = (series[0], series[1], series[2], series[3])
    magnitude = jnp.sqrt(base_east * base_east + base_north * base_north + SPEED_SOFT)
    projected = (base_east * step_east + base_north * step_north) / magnitude
    force_east = drag_row * (magnitude * step_east + base_east * projected)
    force_north = drag_row * (magnitude * step_north + base_north * projected)
    forces = jnp.stack([force_east, force_north])
    analysed = jnp.einsum('tc,ftn->fcn', table, forces, precision=highest) * (2.0 / table.shape[0])
    drag_rate = drag_row * lax.optimization_barrier(jnp.mean(magnitude, axis=0))
    return (analysed, drag_rate)

def precondition(residual, angular, rotation, drag_rate):
    shaped = residual.reshape((3, residual.shape[1] // 2, 2) + residual.shape[2:])
    cos_part = shaped[:, :, 0]
    sin_part = shaped[:, :, 1]
    height_cos = -sin_part[0] / angular
    height_sin = cos_part[0] / angular
    real_rate = drag_rate + LINEAR_DRAG
    det_real = real_rate * real_rate - angular * angular + rotation * rotation
    det_imag = 2.0 * real_rate * angular
    det_norm = det_real * det_real + det_imag * det_imag
    inv_real = det_real / det_norm
    inv_imag = -det_imag / det_norm
    east_re = cos_part[1]
    east_im = -sin_part[1]
    north_re = cos_part[2]
    north_im = -sin_part[2]
    num_east_re = real_rate * east_re - angular * east_im + rotation * north_re
    num_east_im = real_rate * east_im + angular * east_re + rotation * north_im
    num_north_re = -rotation * east_re + real_rate * north_re - angular * north_im
    num_north_im = -rotation * east_im + real_rate * north_im + angular * north_re
    east_out_re = num_east_re * inv_real - num_east_im * inv_imag
    east_out_im = num_east_re * inv_imag + num_east_im * inv_real
    north_out_re = num_north_re * inv_real - num_north_im * inv_imag
    north_out_im = num_north_re * inv_imag + num_north_im * inv_real
    cosines = jnp.stack([height_cos, east_out_re, north_out_re])
    sines = jnp.stack([height_sin, -east_out_im, -north_out_im])
    return jnp.stack([cosines, sines], axis=2).reshape(residual.shape)

def extend_grid(planes):
    wrapped = jnp.concatenate([planes[..., -1:], planes, planes[..., :1]], axis=-1)
    return jnp.pad(wrapped, ((0, 0), (0, 0), (1, 1), (0, 0)))

def reference(direction, base_flow, water_depth, drag_factor, wet_mask):
    wet_cells = wet_mask.astype(jnp.float32)
    height = direction[0] * wet_cells
    east = direction[1] * wet_cells
    north = direction[2] * wet_cells
    planes = jnp.stack([height, east, north, water_depth * east, water_depth * north])
    extended = extend_grid(planes)
    angular = OMEGA_STEP * jnp.arange(1, NCON + 1, dtype=jnp.float32)
    rotation = rotation_of(jnp.arange(NLAT, dtype=jnp.int32), NLAT)
    linear_part = linear_residual(extended, NLAT, NLON, angular[:, None, None], rotation[:, None])
    table = samples_table(NTIME, NCON)
    flows = jnp.concatenate([base_flow, jnp.stack([east, north])], axis=0)

    def one_row(items):
        return friction_row(items[0], items[1], table)
    friction, drag_rate = lax.map(one_row, (jnp.moveaxis(flows, 2, 0), drag_factor))
    friction = jnp.moveaxis(friction, 0, 2)
    residual = (linear_part + jnp.concatenate([jnp.zeros_like(friction[:1]), friction], axis=0)) * wet_cells
    return precondition(residual, angular[:, None, None], rotation[:, None], drag_rate)
```

```python
import math

import jax
import jax.numpy as jnp
from jax import lax
from jax.sharding import PartitionSpec as P

NCON = 16
NTIME = 256


LINEAR_DRAG = 0.5
GRAVITY = 1.0
OMEGA_STEP = 0.25
SPEED_SOFT = 0.01


def extended_2(block, sides, width):
    for axis, dim in sides:
        count = lax.axis_size(axis)
        forward = [(i, i + 1) for i in range(count - 1)]
        forward.append((count - 1, 0))
        backward = [(target, source) for source, target in forward]
        low = lax.ppermute(
            lax.slice_in_dim(block, block.shape[dim] - width, None, axis=dim), axis, forward
        )
        high = lax.ppermute(lax.slice_in_dim(block, 0, width, axis=dim), axis, backward)
        block = jnp.concatenate([low, block, high], axis=dim)
    return block


def samples_table(sample_count, constituents):
    sample_index = jnp.arange(sample_count, dtype=jnp.int32)
    harmonic = jnp.arange(1, constituents + 1, dtype=jnp.int32)
    wrapped_turns = sample_index[:, None] * harmonic[None, :] % sample_count
    phase_angle = wrapped_turns.astype(jnp.float32) * (2.0 * math.pi / sample_count)
    table = jnp.stack([jnp.cos(phase_angle), jnp.sin(phase_angle)], axis=2)
    return table.reshape(sample_count, 2 * constituents)


def rotation_of(row_index, total_rows):
    return 0.5 + (row_index.astype(jnp.float32) + 0.5) / total_rows


def tendency(values, angular):
    cos_sin = values.reshape((values.shape[0] // 2, 2) + values.shape[1:])
    moved = jnp.stack([angular * cos_sin[:, 1], -angular * cos_sin[:, 0]], axis=1)
    return moved.reshape(values.shape)


def linear_residual(extended, tile_rows, tile_cols, angular, rotation):

    def neighbour(plane, row_step, col_step):
        return extended[
            plane,
            :,
            1 + row_step : 1 + row_step + tile_rows,
            1 + col_step : 1 + col_step + tile_cols,
        ]

    height = neighbour(0, 0, 0)
    east = neighbour(1, 0, 0)
    north = neighbour(2, 0, 0)
    res_height = (
        tendency(height, angular)
        + neighbour(3, 0, 0)
        - neighbour(3, 0, -1)
        + neighbour(4, 0, 0)
        - neighbour(4, -1, 0)
    )
    north_mean = 0.25 * (north + neighbour(2, 0, 1) + neighbour(2, -1, 0) + neighbour(2, -1, 1))
    east_mean = 0.25 * (east + neighbour(1, 0, -1) + neighbour(1, 1, 0) + neighbour(1, 1, -1))
    res_east = (
        tendency(east, angular)
        + LINEAR_DRAG * east
        - rotation * north_mean
        + GRAVITY * (neighbour(0, 0, 1) - height)
    )
    res_north = (
        tendency(north, angular)
        + LINEAR_DRAG * north
        + rotation * east_mean
        + GRAVITY * (neighbour(0, 1, 0) - height)
    )
    return jnp.stack([res_height, res_east, res_north])


def friction_row(row_block, drag_row, table):
    highest = lax.Precision.HIGHEST
    series = jnp.einsum("tc,fcn->ftn", table, row_block, precision=highest)
    base_east, base_north, step_east, step_north = (series[0], series[1], series[2], series[3])
    magnitude = jnp.sqrt(base_east * base_east + base_north * base_north + SPEED_SOFT)
    projected = (base_east * step_east + base_north * step_north) / magnitude
    force_east = drag_row * (magnitude * step_east + base_east * projected)
    force_north = drag_row * (magnitude * step_north + base_north * projected)
    forces = jnp.stack([force_east, force_north])
    analysed = jnp.einsum("tc,ftn->fcn", table, forces, precision=highest) * (2.0 / table.shape[0])
    drag_rate = drag_row * jnp.mean(magnitude, axis=0)
    return (analysed, drag_rate)


def precondition(residual, angular, rotation, drag_rate):
    shaped = residual.reshape((3, residual.shape[1] // 2, 2) + residual.shape[2:])
    cos_part = shaped[:, :, 0]
    sin_part = shaped[:, :, 1]
    height_cos = -sin_part[0] / angular
    height_sin = cos_part[0] / angular
    real_rate = drag_rate + LINEAR_DRAG
    det_real = real_rate * real_rate - angular * angular + rotation * rotation
    det_imag = 2.0 * real_rate * angular
    det_norm = det_real * det_real + det_imag * det_imag
    inv_real = det_real / det_norm
    inv_imag = -det_imag / det_norm
    east_re = cos_part[1]
    east_im = -sin_part[1]
    north_re = cos_part[2]
    north_im = -sin_part[2]
    num_east_re = real_rate * east_re - angular * east_im + rotation * north_re
    num_east_im = real_rate * east_im + angular * east_re + rotation * north_im
    num_north_re = -rotation * east_re + real_rate * north_re - angular * north_im
    num_north_im = -rotation * east_im + real_rate * north_im + angular * north_re
    east_out_re = num_east_re * inv_real - num_east_im * inv_imag
    east_out_im = num_east_re * inv_imag + num_east_im * inv_real
    north_out_re = num_north_re * inv_real - num_north_im * inv_imag
    north_out_im = num_north_re * inv_imag + num_north_im * inv_real
    cosines = jnp.stack([height_cos, east_out_re, north_out_re])
    sines = jnp.stack([height_sin, -east_out_im, -north_out_im])
    return jnp.stack([cosines, sines], axis=2).reshape(residual.shape)


def friction_band(flows_band, drag_band, table):
    highest = lax.Precision.HIGHEST
    fields, coefs, rows, cols = flows_band.shape
    block = flows_band.reshape(fields, coefs, rows * cols)
    series = jnp.einsum("tc,fcn->ftn", table, block, precision=highest)
    base_east, base_north, step_east, step_north = (series[0], series[1], series[2], series[3])
    drag_row = drag_band.reshape(1, rows * cols)
    magnitude = jnp.sqrt(base_east * base_east + base_north * base_north + SPEED_SOFT)
    projected = (base_east * step_east + base_north * step_north) / magnitude
    force_east = drag_row * (magnitude * step_east + base_east * projected)
    force_north = drag_row * (magnitude * step_north + base_north * projected)
    forces = jnp.stack([force_east, force_north])
    analysed = jnp.einsum("tc,ftn->fcn", table, forces, precision=highest) * (2.0 / table.shape[0])
    drag_rate = drag_row[0] * lax.optimization_barrier(jnp.mean(magnitude, axis=0))
    return analysed.reshape(2, coefs, rows, cols), drag_rate.reshape(rows, cols)


def local(direction, base_flow, water_depth, drag_factor, wet_mask):
    local_coefs = direction.shape[1]
    tile_rows = direction.shape[2]
    tile_cols = direction.shape[3]
    groups = lax.axis_size("freq")
    member = lax.axis_index("freq")
    band_rows = tile_rows // groups
    lat_place = lax.axis_index("lat")
    lat_count = lax.axis_size("lat")
    total_rows = tile_rows * lat_count
    wet_cells = wet_mask.astype(jnp.float32)
    height = direction[0] * wet_cells
    east = direction[1] * wet_cells
    north = direction[2] * wet_cells
    flows = jnp.concatenate([base_flow, jnp.stack([east, north])], axis=0)
    flows_band = lax.all_to_all(flows, "freq", split_axis=2, concat_axis=1, tiled=True)
    planes = jnp.stack([height, east, north, water_depth * east, water_depth * north])
    extended = extended_2(planes, (("lat", 2), ("lon", 3)), 1)
    rim_keep = jnp.ones((tile_rows + 2,), jnp.float32)
    rim_keep = rim_keep.at[0].set(jnp.where(lat_place == 0, 0.0, 1.0))
    rim_keep = rim_keep.at[tile_rows + 1].set(jnp.where(lat_place == lat_count - 1, 0.0, 1.0))
    extended = extended * rim_keep[:, None]
    local_count = local_coefs // 2
    first_con = member * local_count
    angular_local = OMEGA_STEP * (first_con + jnp.arange(local_count, dtype=jnp.int32) + 1).astype(
        jnp.float32
    )
    row_global = lat_place * tile_rows + jnp.arange(tile_rows, dtype=jnp.int32)
    rotation = rotation_of(row_global, total_rows)
    linear_part = linear_residual(
        extended, tile_rows, tile_cols, angular_local[:, None, None], rotation[:, None]
    )
    table = samples_table(NTIME, NCON)
    band_start = member * band_rows
    drag_band = lax.dynamic_slice_in_dim(drag_factor, band_start, band_rows, 0)
    analysed_band, drag_rate_band = friction_band(flows_band, drag_band, table)
    friction = lax.all_to_all(analysed_band, "freq", split_axis=1, concat_axis=2, tiled=True)
    drag_rate = lax.all_gather(drag_rate_band, "freq", axis=0, tiled=True)
    residual = (
        linear_part + jnp.concatenate([jnp.zeros_like(friction[:1]), friction], axis=0)
    ) * wet_cells
    return precondition(residual, angular_local[:, None, None], rotation[:, None], drag_rate)


def solution(mesh):
    placed = (
        P(None, "freq", "lat", "lon"),
        P(None, "freq", "lat", "lon"),
        P("lat", "lon"),
        P("lat", "lon"),
        P("lat", "lon"),
    )
    return jax.shard_map(
        local, mesh=mesh, in_specs=placed, out_specs=P(None, "freq", "lat", "lon"), check_vma=False
    )
```

```python
import functools
import math

import jax
import jax.numpy as jnp
from jax import lax
from jax.experimental import pallas as pl
from jax.experimental.pallas import tpu as pltpu
from jax.sharding import PartitionSpec as P

NCON = 16
NTIME = 256


LINEAR_DRAG = 0.5
GRAVITY = 1.0
OMEGA_STEP = 0.25
SPEED_SOFT = 0.01


def extended_2(block, sides, width):
    for axis, dim in sides:
        count = lax.axis_size(axis)
        forward = [(i, i + 1) for i in range(count - 1)]
        forward.append((count - 1, 0))
        backward = [(target, source) for source, target in forward]
        low = lax.ppermute(
            lax.slice_in_dim(block, block.shape[dim] - width, None, axis=dim), axis, forward
        )
        high = lax.ppermute(lax.slice_in_dim(block, 0, width, axis=dim), axis, backward)
        block = jnp.concatenate([low, block, high], axis=dim)
    return block


def samples_table(sample_count, constituents):
    sample_index = jnp.arange(sample_count, dtype=jnp.int32)
    harmonic = jnp.arange(1, constituents + 1, dtype=jnp.int32)
    wrapped_turns = sample_index[:, None] * harmonic[None, :] % sample_count
    phase_angle = wrapped_turns.astype(jnp.float32) * (2.0 * math.pi / sample_count)
    table = jnp.stack([jnp.cos(phase_angle), jnp.sin(phase_angle)], axis=2)
    return table.reshape(sample_count, 2 * constituents)


def rotation_of(row_index, total_rows):
    return 0.5 + (row_index.astype(jnp.float32) + 0.5) / total_rows


def tendency(values, angular):
    cos_sin = values.reshape((values.shape[0] // 2, 2) + values.shape[1:])
    moved = jnp.stack([angular * cos_sin[:, 1], -angular * cos_sin[:, 0]], axis=1)
    return moved.reshape(values.shape)


def linear_residual(extended, tile_rows, tile_cols, angular, rotation):

    def neighbour(plane, row_step, col_step):
        return extended[
            plane,
            :,
            1 + row_step : 1 + row_step + tile_rows,
            1 + col_step : 1 + col_step + tile_cols,
        ]

    height = neighbour(0, 0, 0)
    east = neighbour(1, 0, 0)
    north = neighbour(2, 0, 0)
    res_height = (
        tendency(height, angular)
        + neighbour(3, 0, 0)
        - neighbour(3, 0, -1)
        + neighbour(4, 0, 0)
        - neighbour(4, -1, 0)
    )
    north_mean = 0.25 * (north + neighbour(2, 0, 1) + neighbour(2, -1, 0) + neighbour(2, -1, 1))
    east_mean = 0.25 * (east + neighbour(1, 0, -1) + neighbour(1, 1, 0) + neighbour(1, 1, -1))
    res_east = (
        tendency(east, angular)
        + LINEAR_DRAG * east
        - rotation * north_mean
        + GRAVITY * (neighbour(0, 0, 1) - height)
    )
    res_north = (
        tendency(north, angular)
        + LINEAR_DRAG * north
        + rotation * east_mean
        + GRAVITY * (neighbour(0, 1, 0) - height)
    )
    return jnp.stack([res_height, res_east, res_north])


def friction_row(row_block, drag_row, table):
    highest = lax.Precision.HIGHEST
    series = jnp.einsum("tc,fcn->ftn", table, row_block, precision=highest)
    base_east, base_north, step_east, step_north = (series[0], series[1], series[2], series[3])
    magnitude = jnp.sqrt(base_east * base_east + base_north * base_north + SPEED_SOFT)
    projected = (base_east * step_east + base_north * step_north) / magnitude
    force_east = drag_row * (magnitude * step_east + base_east * projected)
    force_north = drag_row * (magnitude * step_north + base_north * projected)
    forces = jnp.stack([force_east, force_north])
    analysed = jnp.einsum("tc,ftn->fcn", table, forces, precision=highest) * (2.0 / table.shape[0])
    drag_rate = drag_row * jnp.mean(magnitude, axis=0)
    return (analysed, drag_rate)


def precondition(residual, angular, rotation, drag_rate):
    shaped = residual.reshape((3, residual.shape[1] // 2, 2) + residual.shape[2:])
    cos_part = shaped[:, :, 0]
    sin_part = shaped[:, :, 1]
    height_cos = -sin_part[0] / angular
    height_sin = cos_part[0] / angular
    real_rate = drag_rate + LINEAR_DRAG
    det_real = real_rate * real_rate - angular * angular + rotation * rotation
    det_imag = 2.0 * real_rate * angular
    det_norm = det_real * det_real + det_imag * det_imag
    inv_real = det_real / det_norm
    inv_imag = -det_imag / det_norm
    east_re = cos_part[1]
    east_im = -sin_part[1]
    north_re = cos_part[2]
    north_im = -sin_part[2]
    num_east_re = real_rate * east_re - angular * east_im + rotation * north_re
    num_east_im = real_rate * east_im + angular * east_re + rotation * north_im
    num_north_re = -rotation * east_re + real_rate * north_re - angular * north_im
    num_north_im = -rotation * east_im + real_rate * north_im + angular * north_re
    east_out_re = num_east_re * inv_real - num_east_im * inv_imag
    east_out_im = num_east_re * inv_imag + num_east_im * inv_real
    north_out_re = num_north_re * inv_real - num_north_im * inv_imag
    north_out_im = num_north_re * inv_imag + num_north_im * inv_real
    cosines = jnp.stack([height_cos, east_out_re, north_out_re])
    sines = jnp.stack([height_sin, -east_out_im, -north_out_im])
    return jnp.stack([cosines, sines], axis=2).reshape(residual.shape)


def friction_kernel(groups, table_ref, table_t_ref, flows_ref, drag_ref, out_ref):
    highest = lax.Precision.HIGHEST
    table = table_ref[...]

    def synth(field):
        return jnp.dot(
            table, flows_ref[field], precision=highest, preferred_element_type=jnp.float32
        )

    base_east, base_north, step_east, step_north = synth(0), synth(1), synth(2), synth(3)
    drag_row = drag_ref[...]
    magnitude = jnp.sqrt(base_east * base_east + base_north * base_north + SPEED_SOFT)
    projected = (base_east * step_east + base_north * step_north) / magnitude
    force_east = drag_row * (magnitude * step_east + base_east * projected)
    force_north = drag_row * (magnitude * step_north + base_north * projected)
    table_t = table_t_ref[...]
    scale = 2.0 / table.shape[0]
    analysed_east = (
        jnp.dot(table_t, force_east, precision=highest, preferred_element_type=jnp.float32) * scale
    )
    analysed_north = (
        jnp.dot(table_t, force_north, precision=highest, preferred_element_type=jnp.float32)
        * scale
    )
    drag_rate = drag_row * jnp.mean(magnitude, axis=0, keepdims=True)
    per = table.shape[1] // groups
    for group in range(groups):
        out_ref[group, 0:per, :] = analysed_east[group * per : (group + 1) * per]
        out_ref[group, per : 2 * per, :] = analysed_north[group * per : (group + 1) * per]
        out_ref[group, 2 * per : 2 * per + 1, :] = drag_rate


def friction_band(flows_band, drag_band, table, groups, block=512):
    fields, coefs, cells = flows_band.shape
    per = coefs // groups
    table_t = jnp.transpose(table)
    return pl.pallas_call(
        functools.partial(friction_kernel, groups),
        grid=(cells // block,),
        in_specs=[
            pl.BlockSpec(table.shape, lambda i: (0, 0)),
            pl.BlockSpec(table_t.shape, lambda i: (0, 0)),
            pl.BlockSpec((fields, coefs, block), lambda i: (0, 0, i)),
            pl.BlockSpec((1, block), lambda i: (0, i)),
        ],
        out_specs=pl.BlockSpec((groups, 2 * per + 1, block), lambda i: (0, 0, i)),
        out_shape=jax.ShapeDtypeStruct((groups, 2 * per + 1, cells), jnp.float32),
        compiler_params=pltpu.CompilerParams(vmem_limit_bytes=48 * 1024 * 1024),
    )(table, table_t, flows_band, drag_band)


def local(direction, base_flow, water_depth, drag_factor, wet_mask):
    local_coefs = direction.shape[1]
    tile_rows = direction.shape[2]
    tile_cols = direction.shape[3]
    groups = lax.axis_size("freq")
    member = lax.axis_index("freq")
    band_rows = tile_rows // groups
    band_cells = band_rows * tile_cols
    lat_place = lax.axis_index("lat")
    lat_count = lax.axis_size("lat")
    total_rows = tile_rows * lat_count
    wet_cells = wet_mask.astype(jnp.float32)
    height = direction[0] * wet_cells
    east = direction[1] * wet_cells
    north = direction[2] * wet_cells
    flows = jnp.concatenate([base_flow, jnp.stack([east, north])], axis=0)
    flows = jnp.moveaxis(flows.reshape(4, local_coefs, groups, band_cells), 2, 0)
    flows_band = lax.all_to_all(flows, "freq", split_axis=0, concat_axis=2, tiled=True)
    flows_band = flows_band.reshape(4, local_coefs * groups, band_cells)
    planes = jnp.stack([height, east, north, water_depth * east, water_depth * north])
    extended = extended_2(planes, (("lat", 2), ("lon", 3)), 1)
    rim_keep = jnp.ones((tile_rows + 2,), jnp.float32)
    rim_keep = rim_keep.at[0].set(jnp.where(lat_place == 0, 0.0, 1.0))
    rim_keep = rim_keep.at[tile_rows + 1].set(jnp.where(lat_place == lat_count - 1, 0.0, 1.0))
    extended = extended * rim_keep[:, None]
    local_count = local_coefs // 2
    first_con = member * local_count
    angular_local = OMEGA_STEP * (first_con + jnp.arange(local_count, dtype=jnp.int32) + 1).astype(
        jnp.float32
    )
    row_global = lat_place * tile_rows + jnp.arange(tile_rows, dtype=jnp.int32)
    rotation = rotation_of(row_global, total_rows)
    linear_part = linear_residual(
        extended, tile_rows, tile_cols, angular_local[:, None, None], rotation[:, None]
    )
    flows_band, linear_part = lax.optimization_barrier((flows_band, linear_part))
    table = samples_table(NTIME, NCON)
    band_start = member * band_rows
    drag_band = lax.dynamic_slice_in_dim(drag_factor, band_start, band_rows, 0)
    packed = friction_band(flows_band, drag_band.reshape(1, band_cells), table, groups)
    back = lax.all_to_all(packed, "freq", split_axis=0, concat_axis=0, tiled=True)
    back = back.reshape(groups, 2 * local_coefs + 1, band_rows, tile_cols)
    back = jnp.moveaxis(back, 0, 1).reshape(2 * local_coefs + 1, tile_rows, tile_cols)
    friction = back[: 2 * local_coefs].reshape(2, local_coefs, tile_rows, tile_cols)
    drag_rate = back[2 * local_coefs]
    residual = (
        linear_part + jnp.concatenate([jnp.zeros_like(friction[:1]), friction], axis=0)
    ) * wet_cells
    return precondition(residual, angular_local[:, None, None], rotation[:, None], drag_rate)


def solution(mesh):
    placed = (
        P(None, "freq", "lat", "lon"),
        P(None, "freq", "lat", "lon"),
        P("lat", "lon"),
        P("lat", "lon"),
        P("lat", "lon"),
    )
    return jax.shard_map(
        local, mesh=mesh, in_specs=placed, out_specs=P(None, "freq", "lat", "lon"), check_vma=False
    )
```

```python
import functools
import math

import jax
import jax.numpy as jnp
from jax import lax
from jax.experimental import pallas as pl
from jax.experimental.pallas import tpu as pltpu
from jax.sharding import PartitionSpec as P

NCON = 16
NTIME = 256


LINEAR_DRAG = 0.5
GRAVITY = 1.0
OMEGA_STEP = 0.25
SPEED_SOFT = 0.01


def extended_2(block, sides, width):
    for axis, dim in sides:
        count = lax.axis_size(axis)
        forward = [(i, i + 1) for i in range(count - 1)]
        forward.append((count - 1, 0))
        backward = [(target, source) for source, target in forward]
        low = lax.ppermute(
            lax.slice_in_dim(block, block.shape[dim] - width, None, axis=dim), axis, forward
        )
        high = lax.ppermute(lax.slice_in_dim(block, 0, width, axis=dim), axis, backward)
        block = jnp.concatenate([low, block, high], axis=dim)
    return block


def samples_table(sample_count, constituents):
    sample_index = jnp.arange(sample_count, dtype=jnp.int32)
    harmonic = jnp.arange(1, constituents + 1, dtype=jnp.int32)
    wrapped_turns = sample_index[:, None] * harmonic[None, :] % sample_count
    phase_angle = wrapped_turns.astype(jnp.float32) * (2.0 * math.pi / sample_count)
    table = jnp.stack([jnp.cos(phase_angle), jnp.sin(phase_angle)], axis=2)
    return table.reshape(sample_count, 2 * constituents)


def rotation_of(row_index, total_rows):
    return 0.5 + (row_index.astype(jnp.float32) + 0.5) / total_rows


def tendency(values, angular):
    cos_sin = values.reshape((values.shape[0] // 2, 2) + values.shape[1:])
    moved = jnp.stack([angular * cos_sin[:, 1], -angular * cos_sin[:, 0]], axis=1)
    return moved.reshape(values.shape)


def linear_residual(extended, tile_rows, tile_cols, angular, rotation):

    def neighbour(plane, row_step, col_step):
        return extended[
            plane,
            :,
            1 + row_step : 1 + row_step + tile_rows,
            1 + col_step : 1 + col_step + tile_cols,
        ]

    height = neighbour(0, 0, 0)
    east = neighbour(1, 0, 0)
    north = neighbour(2, 0, 0)
    res_height = (
        tendency(height, angular)
        + neighbour(3, 0, 0)
        - neighbour(3, 0, -1)
        + neighbour(4, 0, 0)
        - neighbour(4, -1, 0)
    )
    north_mean = 0.25 * (north + neighbour(2, 0, 1) + neighbour(2, -1, 0) + neighbour(2, -1, 1))
    east_mean = 0.25 * (east + neighbour(1, 0, -1) + neighbour(1, 1, 0) + neighbour(1, 1, -1))
    res_east = (
        tendency(east, angular)
        + LINEAR_DRAG * east
        - rotation * north_mean
        + GRAVITY * (neighbour(0, 0, 1) - height)
    )
    res_north = (
        tendency(north, angular)
        + LINEAR_DRAG * north
        + rotation * east_mean
        + GRAVITY * (neighbour(0, 1, 0) - height)
    )
    return jnp.stack([res_height, res_east, res_north])


def friction_row(row_block, drag_row, table):
    highest = lax.Precision.HIGHEST
    series = jnp.einsum("tc,fcn->ftn", table, row_block, precision=highest)
    base_east, base_north, step_east, step_north = (series[0], series[1], series[2], series[3])
    magnitude = jnp.sqrt(base_east * base_east + base_north * base_north + SPEED_SOFT)
    projected = (base_east * step_east + base_north * step_north) / magnitude
    force_east = drag_row * (magnitude * step_east + base_east * projected)
    force_north = drag_row * (magnitude * step_north + base_north * projected)
    forces = jnp.stack([force_east, force_north])
    analysed = jnp.einsum("tc,ftn->fcn", table, forces, precision=highest) * (2.0 / table.shape[0])
    drag_rate = drag_row * jnp.mean(magnitude, axis=0)
    return (analysed, drag_rate)


def precondition(residual, angular, rotation, drag_rate):
    shaped = residual.reshape((3, residual.shape[1] // 2, 2) + residual.shape[2:])
    cos_part = shaped[:, :, 0]
    sin_part = shaped[:, :, 1]
    height_cos = -sin_part[0] / angular
    height_sin = cos_part[0] / angular
    real_rate = drag_rate + LINEAR_DRAG
    det_real = real_rate * real_rate - angular * angular + rotation * rotation
    det_imag = 2.0 * real_rate * angular
    det_norm = det_real * det_real + det_imag * det_imag
    inv_real = det_real / det_norm
    inv_imag = -det_imag / det_norm
    east_re = cos_part[1]
    east_im = -sin_part[1]
    north_re = cos_part[2]
    north_im = -sin_part[2]
    num_east_re = real_rate * east_re - angular * east_im + rotation * north_re
    num_east_im = real_rate * east_im + angular * east_re + rotation * north_im
    num_north_re = -rotation * east_re + real_rate * north_re - angular * north_im
    num_north_im = -rotation * east_im + real_rate * north_im + angular * north_re
    east_out_re = num_east_re * inv_real - num_east_im * inv_imag
    east_out_im = num_east_re * inv_imag + num_east_im * inv_real
    north_out_re = num_north_re * inv_real - num_north_im * inv_imag
    north_out_im = num_north_re * inv_imag + num_north_im * inv_real
    cosines = jnp.stack([height_cos, east_out_re, north_out_re])
    sines = jnp.stack([height_sin, -east_out_im, -north_out_im])
    return jnp.stack([cosines, sines], axis=2).reshape(residual.shape)


def split_three(values):
    high = values.astype(jnp.bfloat16)
    rest = values - high.astype(jnp.float32)
    middle = rest.astype(jnp.bfloat16)
    low = (rest - middle.astype(jnp.float32)).astype(jnp.bfloat16)
    return high, middle, low


def friction_kernel(
    groups, stacked_ref, table_t_ref, flows_ref, drag_ref, out_ref, rate_ref, parts_ref
):
    highest = lax.Precision.HIGHEST
    stacked = stacked_ref[...]
    coefs = flows_ref.shape[1]

    def synth(field):
        high, middle, low = split_three(flows_ref[field])
        for slot, part in enumerate((high, middle, high, low, high, middle)):
            parts_ref[slot * coefs : (slot + 1) * coefs, :] = part
        return jnp.dot(stacked, parts_ref[...], preferred_element_type=jnp.float32)

    base_east, base_north, step_east, step_north = synth(0), synth(1), synth(2), synth(3)
    drag_row = drag_ref[...]
    magnitude = jnp.sqrt(base_east * base_east + base_north * base_north + SPEED_SOFT)
    projected = (base_east * step_east + base_north * step_north) / magnitude
    force_east = drag_row * (magnitude * step_east + base_east * projected)
    force_north = drag_row * (magnitude * step_north + base_north * projected)
    table_t = table_t_ref[...]
    scale = 2.0 / stacked.shape[0]
    analysed_east = (
        jnp.dot(table_t, force_east, precision=highest, preferred_element_type=jnp.float32) * scale
    )
    analysed_north = (
        jnp.dot(table_t, force_north, precision=highest, preferred_element_type=jnp.float32)
        * scale
    )
    rate_ref[...] = drag_row * jnp.mean(magnitude, axis=0, keepdims=True)
    per = coefs // groups
    for group in range(groups):
        out_ref[group, 0:per, :] = analysed_east[group * per : (group + 1) * per]
        out_ref[group, per : 2 * per, :] = analysed_north[group * per : (group + 1) * per]


def friction_band(flows_band, drag_band, table, groups, block=512):
    fields, coefs, cells = flows_band.shape
    per = coefs // groups
    table_t = jnp.transpose(table)
    high = lax.reduce_precision(table, exponent_bits=8, mantissa_bits=7)
    rest = table - high
    middle = lax.reduce_precision(rest, exponent_bits=8, mantissa_bits=7)
    low = lax.reduce_precision(rest - middle, exponent_bits=8, mantissa_bits=7)
    stacked = jnp.concatenate([high, middle, middle, high, low, high], axis=1)
    stacked = stacked.astype(jnp.bfloat16)
    return pl.pallas_call(
        functools.partial(friction_kernel, groups),
        grid=(cells // block,),
        in_specs=[
            pl.BlockSpec(stacked.shape, lambda i: (0, 0)),
            pl.BlockSpec(table_t.shape, lambda i: (0, 0)),
            pl.BlockSpec((fields, coefs, block), lambda i: (0, 0, i)),
            pl.BlockSpec((1, block), lambda i: (0, i)),
        ],
        out_specs=[
            pl.BlockSpec((groups, 2 * per, block), lambda i: (0, 0, i)),
            pl.BlockSpec((1, block), lambda i: (0, i)),
        ],
        out_shape=[
            jax.ShapeDtypeStruct((groups, 2 * per, cells), jnp.float32),
            jax.ShapeDtypeStruct((1, cells), jnp.float32),
        ],
        scratch_shapes=[pltpu.VMEM((6 * coefs, block), jnp.bfloat16)],
        compiler_params=pltpu.CompilerParams(vmem_limit_bytes=48 * 1024 * 1024),
    )(stacked, table_t, flows_band, drag_band)


def local(direction, base_flow, water_depth, drag_factor, wet_mask):
    local_coefs = direction.shape[1]
    tile_rows = direction.shape[2]
    tile_cols = direction.shape[3]
    groups = lax.axis_size("freq")
    member = lax.axis_index("freq")
    band_rows = tile_rows // groups
    band_cells = band_rows * tile_cols
    lat_place = lax.axis_index("lat")
    lat_count = lax.axis_size("lat")
    total_rows = tile_rows * lat_count
    wet_cells = wet_mask.astype(jnp.float32)
    height = direction[0] * wet_cells
    east = direction[1] * wet_cells
    north = direction[2] * wet_cells
    flows = jnp.concatenate([base_flow, jnp.stack([east, north])], axis=0)
    flows = jnp.moveaxis(flows.reshape(4, local_coefs, groups, band_cells), 2, 0)
    flows_band = lax.all_to_all(flows, "freq", split_axis=0, concat_axis=2, tiled=True)
    flows_band = flows_band.reshape(4, local_coefs * groups, band_cells)
    planes = jnp.stack([height, east, north, water_depth * east, water_depth * north])
    extended = extended_2(planes, (("lat", 2), ("lon", 3)), 1)
    rim_keep = jnp.ones((tile_rows + 2,), jnp.float32)
    rim_keep = rim_keep.at[0].set(jnp.where(lat_place == 0, 0.0, 1.0))
    rim_keep = rim_keep.at[tile_rows + 1].set(jnp.where(lat_place == lat_count - 1, 0.0, 1.0))
    extended = extended * rim_keep[:, None]
    local_count = local_coefs // 2
    first_con = member * local_count
    angular_local = OMEGA_STEP * (first_con + jnp.arange(local_count, dtype=jnp.int32) + 1).astype(
        jnp.float32
    )
    row_global = lat_place * tile_rows + jnp.arange(tile_rows, dtype=jnp.int32)
    rotation = rotation_of(row_global, total_rows)
    linear_part = linear_residual(
        extended, tile_rows, tile_cols, angular_local[:, None, None], rotation[:, None]
    )
    flows_band, linear_part = lax.optimization_barrier((flows_band, linear_part))
    table = samples_table(NTIME, NCON)
    band_start = member * band_rows
    drag_band = lax.dynamic_slice_in_dim(drag_factor, band_start, band_rows, 0)
    packed, rate = friction_band(flows_band, drag_band.reshape(1, band_cells), table, groups)
    back = lax.all_to_all(packed, "freq", split_axis=0, concat_axis=0, tiled=True)
    back = back.reshape(groups, 2 * local_coefs, band_rows, tile_cols)
    back = jnp.moveaxis(back, 0, 1).reshape(2, local_coefs, tile_rows, tile_cols)
    friction = back
    rate = jnp.broadcast_to(rate.reshape(1, band_rows, tile_cols), (groups, band_rows, tile_cols))
    drag_rate = lax.all_to_all(rate, "freq", split_axis=0, concat_axis=0, tiled=True)
    drag_rate = drag_rate.reshape(tile_rows, tile_cols)
    residual = (
        linear_part + jnp.concatenate([jnp.zeros_like(friction[:1]), friction], axis=0)
    ) * wet_cells
    return precondition(residual, angular_local[:, None, None], rotation[:, None], drag_rate)


def solution(mesh):
    placed = (
        P(None, "freq", "lat", "lon"),
        P(None, "freq", "lat", "lon"),
        P("lat", "lon"),
        P("lat", "lon"),
        P("lat", "lon"),
    )
    return jax.shard_map(
        local, mesh=mesh, in_specs=placed, out_specs=P(None, "freq", "lat", "lon"), check_vma=False
    )
```

```python
import functools
import math

import jax
import jax.numpy as jnp
from jax import lax
from jax.experimental import pallas as pl
from jax.experimental.pallas import tpu as pltpu
from jax.sharding import PartitionSpec as P

NCON = 16
NTIME = 256


LINEAR_DRAG = 0.5
GRAVITY = 1.0
OMEGA_STEP = 0.25
SPEED_SOFT = 0.01


def extended_2(block, sides, width):
    for axis, dim in sides:
        count = lax.axis_size(axis)
        forward = [(i, i + 1) for i in range(count - 1)]
        forward.append((count - 1, 0))
        backward = [(target, source) for source, target in forward]
        low = lax.ppermute(
            lax.slice_in_dim(block, block.shape[dim] - width, None, axis=dim), axis, forward
        )
        high = lax.ppermute(lax.slice_in_dim(block, 0, width, axis=dim), axis, backward)
        block = jnp.concatenate([low, block, high], axis=dim)
    return block


def samples_table(sample_count, constituents):
    sample_index = jnp.arange(sample_count, dtype=jnp.int32)
    harmonic = jnp.arange(1, constituents + 1, dtype=jnp.int32)
    wrapped_turns = sample_index[:, None] * harmonic[None, :] % sample_count
    phase_angle = wrapped_turns.astype(jnp.float32) * (2.0 * math.pi / sample_count)
    table = jnp.stack([jnp.cos(phase_angle), jnp.sin(phase_angle)], axis=2)
    return table.reshape(sample_count, 2 * constituents)


def rotation_of(row_index, total_rows):
    return 0.5 + (row_index.astype(jnp.float32) + 0.5) / total_rows


def tendency(values, angular):
    cos_sin = values.reshape((values.shape[0] // 2, 2) + values.shape[1:])
    moved = jnp.stack([angular * cos_sin[:, 1], -angular * cos_sin[:, 0]], axis=1)
    return moved.reshape(values.shape)


def linear_residual(extended, tile_rows, tile_cols, angular, rotation):

    def neighbour(plane, row_step, col_step):
        return extended[
            plane,
            :,
            1 + row_step : 1 + row_step + tile_rows,
            1 + col_step : 1 + col_step + tile_cols,
        ]

    height = neighbour(0, 0, 0)
    east = neighbour(1, 0, 0)
    north = neighbour(2, 0, 0)
    res_height = (
        tendency(height, angular)
        + neighbour(3, 0, 0)
        - neighbour(3, 0, -1)
        + neighbour(4, 0, 0)
        - neighbour(4, -1, 0)
    )
    north_mean = 0.25 * (north + neighbour(2, 0, 1) + neighbour(2, -1, 0) + neighbour(2, -1, 1))
    east_mean = 0.25 * (east + neighbour(1, 0, -1) + neighbour(1, 1, 0) + neighbour(1, 1, -1))
    res_east = (
        tendency(east, angular)
        + LINEAR_DRAG * east
        - rotation * north_mean
        + GRAVITY * (neighbour(0, 0, 1) - height)
    )
    res_north = (
        tendency(north, angular)
        + LINEAR_DRAG * north
        + rotation * east_mean
        + GRAVITY * (neighbour(0, 1, 0) - height)
    )
    return jnp.stack([res_height, res_east, res_north])


def friction_row(row_block, drag_row, table):
    highest = lax.Precision.HIGHEST
    series = jnp.einsum("tc,fcn->ftn", table, row_block, precision=highest)
    base_east, base_north, step_east, step_north = (series[0], series[1], series[2], series[3])
    magnitude = jnp.sqrt(base_east * base_east + base_north * base_north + SPEED_SOFT)
    projected = (base_east * step_east + base_north * step_north) / magnitude
    force_east = drag_row * (magnitude * step_east + base_east * projected)
    force_north = drag_row * (magnitude * step_north + base_north * projected)
    forces = jnp.stack([force_east, force_north])
    analysed = jnp.einsum("tc,ftn->fcn", table, forces, precision=highest) * (2.0 / table.shape[0])
    drag_rate = drag_row * jnp.mean(magnitude, axis=0)
    return (analysed, drag_rate)


def precondition(residual, angular, rotation, drag_rate):
    shaped = residual.reshape((3, residual.shape[1] // 2, 2) + residual.shape[2:])
    cos_part = shaped[:, :, 0]
    sin_part = shaped[:, :, 1]
    height_cos = -sin_part[0] / angular
    height_sin = cos_part[0] / angular
    real_rate = drag_rate + LINEAR_DRAG
    det_real = real_rate * real_rate - angular * angular + rotation * rotation
    det_imag = 2.0 * real_rate * angular
    det_norm = det_real * det_real + det_imag * det_imag
    inv_real = det_real / det_norm
    inv_imag = -det_imag / det_norm
    east_re = cos_part[1]
    east_im = -sin_part[1]
    north_re = cos_part[2]
    north_im = -sin_part[2]
    num_east_re = real_rate * east_re - angular * east_im + rotation * north_re
    num_east_im = real_rate * east_im + angular * east_re + rotation * north_im
    num_north_re = -rotation * east_re + real_rate * north_re - angular * north_im
    num_north_im = -rotation * east_im + real_rate * north_im + angular * north_re
    east_out_re = num_east_re * inv_real - num_east_im * inv_imag
    east_out_im = num_east_re * inv_imag + num_east_im * inv_real
    north_out_re = num_north_re * inv_real - num_north_im * inv_imag
    north_out_im = num_north_re * inv_imag + num_north_im * inv_real
    cosines = jnp.stack([height_cos, east_out_re, north_out_re])
    sines = jnp.stack([height_sin, -east_out_im, -north_out_im])
    return jnp.stack([cosines, sines], axis=2).reshape(residual.shape)


def split_three(values):
    high = values.astype(jnp.bfloat16)
    rest = values - high.astype(jnp.float32)
    middle = rest.astype(jnp.bfloat16)
    low = (rest - middle.astype(jnp.float32)).astype(jnp.bfloat16)
    return high, middle, low


def friction_kernel(
    groups, stacked_ref, table_t_ref, flows_ref, drag_ref, out_ref, rate_ref, gather_ref, parts_ref
):
    highest = lax.Precision.HIGHEST
    stacked = stacked_ref[...]
    coefs = gather_ref.shape[0]
    per = coefs // groups

    def synth(field):
        for source in range(groups):
            gather_ref[source * per : (source + 1) * per, :] = flows_ref[
                source, field * per : (field + 1) * per, :
            ]
        high, middle, low = split_three(gather_ref[...])
        for slot, part in enumerate((high, middle, high, low, high, middle)):
            parts_ref[slot * coefs : (slot + 1) * coefs, :] = part
        return jnp.dot(stacked, parts_ref[...], preferred_element_type=jnp.float32)

    base_east, base_north, step_east, step_north = synth(0), synth(1), synth(2), synth(3)
    drag_row = drag_ref[...]
    magnitude = jnp.sqrt(base_east * base_east + base_north * base_north + SPEED_SOFT)
    projected = (base_east * step_east + base_north * step_north) / magnitude
    force_east = drag_row * (magnitude * step_east + base_east * projected)
    force_north = drag_row * (magnitude * step_north + base_north * projected)
    table_t = table_t_ref[...]
    scale = 2.0 / stacked.shape[0]
    analysed_east = (
        jnp.dot(table_t, force_east, precision=highest, preferred_element_type=jnp.float32) * scale
    )
    analysed_north = (
        jnp.dot(table_t, force_north, precision=highest, preferred_element_type=jnp.float32)
        * scale
    )
    rate_ref[...] = drag_row * jnp.mean(magnitude, axis=0, keepdims=True)
    for group in range(groups):
        out_ref[group, 0:per, :] = analysed_east[group * per : (group + 1) * per]
        out_ref[group, per : 2 * per, :] = analysed_north[group * per : (group + 1) * per]


def friction_band(flows_band, drag_band, table, block):
    groups, rows_in, cells = flows_band.shape
    coefs = table.shape[1]
    per = coefs // groups
    table_t = jnp.transpose(table)
    high = lax.reduce_precision(table, exponent_bits=8, mantissa_bits=7)
    rest = table - high
    middle = lax.reduce_precision(rest, exponent_bits=8, mantissa_bits=7)
    low = lax.reduce_precision(rest - middle, exponent_bits=8, mantissa_bits=7)
    stacked = jnp.concatenate([high, middle, middle, high, low, high], axis=1)
    stacked = stacked.astype(jnp.bfloat16)
    steps = cells // block
    return pl.pallas_call(
        functools.partial(friction_kernel, groups),
        grid=(steps,),
        in_specs=[
            pl.BlockSpec(stacked.shape, lambda i: (0, 0)),
            pl.BlockSpec(table_t.shape, lambda i: (0, 0)),
            pl.BlockSpec((groups, rows_in, block), lambda i: (0, 0, i)),
            pl.BlockSpec((1, block), lambda i: (0, i)),
        ],
        out_specs=[
            pl.BlockSpec((groups, 2 * per, block), lambda i: (0, 0, i)),
            pl.BlockSpec((pl.Squeezed(), 1, block), lambda i: (i, 0, 0)),
        ],
        out_shape=[
            jax.ShapeDtypeStruct((groups, 2 * per, cells), jnp.float32),
            jax.ShapeDtypeStruct((steps, 1, block), jnp.float32),
        ],
        scratch_shapes=[
            pltpu.VMEM((coefs, block), jnp.float32),
            pltpu.VMEM((6 * coefs, block), jnp.bfloat16),
        ],
        compiler_params=pltpu.CompilerParams(vmem_limit_bytes=48 * 1024 * 1024),
    )(stacked, table_t, flows_band, drag_band)


def local(direction, base_flow, water_depth, drag_factor, wet_mask, pieces=2):
    local_coefs = direction.shape[1]
    tile_rows = direction.shape[2]
    tile_cols = direction.shape[3]
    groups = lax.axis_size("freq")
    member = lax.axis_index("freq")
    band_rows = tile_rows // groups
    piece_rows = band_rows // pieces
    piece_cells = piece_rows * tile_cols
    lat_place = lax.axis_index("lat")
    lat_count = lax.axis_size("lat")
    total_rows = tile_rows * lat_count
    wet_cells = wet_mask.astype(jnp.float32)
    height = direction[0] * wet_cells
    east = direction[1] * wet_cells
    north = direction[2] * wet_cells
    flows = jnp.concatenate([base_flow, jnp.stack([east, north])], axis=0)
    flows = flows.reshape(4 * local_coefs, groups, pieces, piece_rows, tile_cols)
    table = samples_table(NTIME, NCON)
    band_start = member * band_rows
    drag_band = lax.dynamic_slice_in_dim(drag_factor, band_start, band_rows, 0)
    drag_band = drag_band.reshape(pieces, 1, piece_cells)
    sent = []
    for piece in range(pieces):
        payload = jnp.moveaxis(flows[:, :, piece], 1, 0).reshape(groups, 4 * local_coefs, piece_cells)
        sent.append(lax.all_to_all(payload, "freq", split_axis=0, concat_axis=0, tiled=True))
    planes = jnp.stack([height, east, north, water_depth * east, water_depth * north])
    extended = extended_2(planes, (("lat", 2), ("lon", 3)), 1)
    rim_keep = jnp.ones((tile_rows + 2,), jnp.float32)
    rim_keep = rim_keep.at[0].set(jnp.where(lat_place == 0, 0.0, 1.0))
    rim_keep = rim_keep.at[tile_rows + 1].set(jnp.where(lat_place == lat_count - 1, 0.0, 1.0))
    extended = extended * rim_keep[:, None]
    local_count = local_coefs // 2
    first_con = member * local_count
    angular_local = OMEGA_STEP * (first_con + jnp.arange(local_count, dtype=jnp.int32) + 1).astype(
        jnp.float32
    )
    row_global = lat_place * tile_rows + jnp.arange(tile_rows, dtype=jnp.int32)
    rotation = rotation_of(row_global, total_rows)
    linear_part = linear_residual(
        extended, tile_rows, tile_cols, angular_local[:, None, None], rotation[:, None]
    )
    frictions, rates = [], []
    for piece in range(pieces):
        packed, rate = friction_band(sent[piece], drag_band[piece], table, tile_cols)
        rate = jnp.broadcast_to(
            rate.reshape(1, 1, piece_cells).reshape(1, 2 * local_coefs, piece_cells // (2 * local_coefs)),
            (groups, 2 * local_coefs, piece_cells // (2 * local_coefs)),
        )
        payload = jnp.concatenate([packed, rate], axis=2)
        back = lax.all_to_all(payload, "freq", split_axis=0, concat_axis=0, tiled=True)
        frictions.append(
            back[:, :, :piece_cells].reshape(groups, 2 * local_coefs, piece_rows, tile_cols)
        )
        rates.append(back[:, :, piece_cells:].reshape(groups, piece_rows, tile_cols))
    friction = jnp.stack(frictions, axis=2)
    friction = jnp.moveaxis(friction, 0, 1).reshape(2, local_coefs, tile_rows, tile_cols)
    drag_rate = jnp.stack(rates, axis=1).reshape(tile_rows, tile_cols)
    residual = (
        linear_part + jnp.concatenate([jnp.zeros_like(friction[:1]), friction], axis=0)
    ) * wet_cells
    return precondition(residual, angular_local[:, None, None], rotation[:, None], drag_rate)


def solution(mesh):
    placed = (
        P(None, "freq", "lat", "lon"),
        P(None, "freq", "lat", "lon"),
        P("lat", "lon"),
        P("lat", "lon"),
        P("lat", "lon"),
    )
    return jax.shard_map(
        local, mesh=mesh, in_specs=placed, out_specs=P(None, "freq", "lat", "lon"), check_vma=False
    )
```

```python
import functools
import math

import jax
import jax.numpy as jnp
from jax import lax
from jax.experimental import pallas as pl
from jax.experimental.pallas import tpu as pltpu
from jax.sharding import PartitionSpec as P

NCON = 16
NTIME = 256


LINEAR_DRAG = 0.5
GRAVITY = 1.0
OMEGA_STEP = 0.25
SPEED_SOFT = 0.01


def extended_2(block, sides, width):
    for axis, dim in sides:
        count = lax.axis_size(axis)
        forward = [(i, i + 1) for i in range(count - 1)]
        forward.append((count - 1, 0))
        backward = [(target, source) for source, target in forward]
        low = lax.ppermute(
            lax.slice_in_dim(block, block.shape[dim] - width, None, axis=dim), axis, forward
        )
        high = lax.ppermute(lax.slice_in_dim(block, 0, width, axis=dim), axis, backward)
        block = jnp.concatenate([low, block, high], axis=dim)
    return block


def samples_table(sample_count, constituents):
    sample_index = jnp.arange(sample_count, dtype=jnp.int32)
    harmonic = jnp.arange(1, constituents + 1, dtype=jnp.int32)
    wrapped_turns = sample_index[:, None] * harmonic[None, :] % sample_count
    phase_angle = wrapped_turns.astype(jnp.float32) * (2.0 * math.pi / sample_count)
    table = jnp.stack([jnp.cos(phase_angle), jnp.sin(phase_angle)], axis=2)
    return table.reshape(sample_count, 2 * constituents)


def rotation_of(row_index, total_rows):
    return 0.5 + (row_index.astype(jnp.float32) + 0.5) / total_rows


def tendency(values, angular):
    cos_sin = values.reshape((values.shape[0] // 2, 2) + values.shape[1:])
    moved = jnp.stack([angular * cos_sin[:, 1], -angular * cos_sin[:, 0]], axis=1)
    return moved.reshape(values.shape)


def linear_residual(extended, tile_rows, tile_cols, angular, rotation):

    def neighbour(plane, row_step, col_step):
        return extended[
            plane,
            :,
            1 + row_step : 1 + row_step + tile_rows,
            1 + col_step : 1 + col_step + tile_cols,
        ]

    height = neighbour(0, 0, 0)
    east = neighbour(1, 0, 0)
    north = neighbour(2, 0, 0)
    res_height = (
        tendency(height, angular)
        + neighbour(3, 0, 0)
        - neighbour(3, 0, -1)
        + neighbour(4, 0, 0)
        - neighbour(4, -1, 0)
    )
    north_mean = 0.25 * (north + neighbour(2, 0, 1) + neighbour(2, -1, 0) + neighbour(2, -1, 1))
    east_mean = 0.25 * (east + neighbour(1, 0, -1) + neighbour(1, 1, 0) + neighbour(1, 1, -1))
    res_east = (
        tendency(east, angular)
        + LINEAR_DRAG * east
        - rotation * north_mean
        + GRAVITY * (neighbour(0, 0, 1) - height)
    )
    res_north = (
        tendency(north, angular)
        + LINEAR_DRAG * north
        + rotation * east_mean
        + GRAVITY * (neighbour(0, 1, 0) - height)
    )
    return jnp.stack([res_height, res_east, res_north])


def friction_row(row_block, drag_row, table):
    highest = lax.Precision.HIGHEST
    series = jnp.einsum("tc,fcn->ftn", table, row_block, precision=highest)
    base_east, base_north, step_east, step_north = (series[0], series[1], series[2], series[3])
    magnitude = jnp.sqrt(base_east * base_east + base_north * base_north + SPEED_SOFT)
    projected = (base_east * step_east + base_north * step_north) / magnitude
    force_east = drag_row * (magnitude * step_east + base_east * projected)
    force_north = drag_row * (magnitude * step_north + base_north * projected)
    forces = jnp.stack([force_east, force_north])
    analysed = jnp.einsum("tc,ftn->fcn", table, forces, precision=highest) * (2.0 / table.shape[0])
    drag_rate = drag_row * jnp.mean(magnitude, axis=0)
    return (analysed, drag_rate)


def precondition(residual, angular, rotation, drag_rate):
    shaped = residual.reshape((3, residual.shape[1] // 2, 2) + residual.shape[2:])
    cos_part = shaped[:, :, 0]
    sin_part = shaped[:, :, 1]
    height_cos = -sin_part[0] / angular
    height_sin = cos_part[0] / angular
    real_rate = drag_rate + LINEAR_DRAG
    det_real = real_rate * real_rate - angular * angular + rotation * rotation
    det_imag = 2.0 * real_rate * angular
    det_norm = det_real * det_real + det_imag * det_imag
    inv_real = det_real / det_norm
    inv_imag = -det_imag / det_norm
    east_re = cos_part[1]
    east_im = -sin_part[1]
    north_re = cos_part[2]
    north_im = -sin_part[2]
    num_east_re = real_rate * east_re - angular * east_im + rotation * north_re
    num_east_im = real_rate * east_im + angular * east_re + rotation * north_im
    num_north_re = -rotation * east_re + real_rate * north_re - angular * north_im
    num_north_im = -rotation * east_im + real_rate * north_im + angular * north_re
    east_out_re = num_east_re * inv_real - num_east_im * inv_imag
    east_out_im = num_east_re * inv_imag + num_east_im * inv_real
    north_out_re = num_north_re * inv_real - num_north_im * inv_imag
    north_out_im = num_north_re * inv_imag + num_north_im * inv_real
    cosines = jnp.stack([height_cos, east_out_re, north_out_re])
    sines = jnp.stack([height_sin, -east_out_im, -north_out_im])
    return jnp.stack([cosines, sines], axis=2).reshape(residual.shape)


def split_three(values):
    high = values.astype(jnp.bfloat16)
    rest = values - high.astype(jnp.float32)
    middle = rest.astype(jnp.bfloat16)
    low = (rest - middle.astype(jnp.float32)).astype(jnp.bfloat16)
    return high, middle, low


def friction_kernel(
    groups, stacked_ref, table_t_ref, flows_ref, drag_ref, out_ref, rate_ref, gather_ref, parts_ref
):
    highest = lax.Precision.HIGHEST
    stacked = stacked_ref[...]
    coefs = gather_ref.shape[0]
    per = coefs // groups

    def synth(field):
        for source in range(groups):
            gather_ref[source * per : (source + 1) * per, :] = flows_ref[
                source, field * per : (field + 1) * per, :
            ]
        high, middle, low = split_three(gather_ref[...])
        for slot, part in enumerate((high, middle, high, low, high, middle)):
            parts_ref[slot * coefs : (slot + 1) * coefs, :] = part
        return jnp.dot(stacked, parts_ref[...], preferred_element_type=jnp.float32)

    base_east, base_north, step_east, step_north = synth(0), synth(1), synth(2), synth(3)
    drag_row = drag_ref[...]
    magnitude = jnp.sqrt(base_east * base_east + base_north * base_north + SPEED_SOFT)
    projected = (base_east * step_east + base_north * step_north) / magnitude
    force_east = drag_row * (magnitude * step_east + base_east * projected)
    force_north = drag_row * (magnitude * step_north + base_north * projected)
    table_t = table_t_ref[...]
    scale = 2.0 / stacked.shape[0]
    analysed_east = (
        jnp.dot(table_t, force_east, precision=highest, preferred_element_type=jnp.float32) * scale
    )
    analysed_north = (
        jnp.dot(table_t, force_north, precision=highest, preferred_element_type=jnp.float32)
        * scale
    )
    rate_ref[...] = drag_row * jnp.mean(magnitude, axis=0, keepdims=True)
    for group in range(groups):
        out_ref[group, 0:per, :] = analysed_east[group * per : (group + 1) * per]
        out_ref[group, per : 2 * per, :] = analysed_north[group * per : (group + 1) * per]


def friction_band(flows_band, drag_band, table, block):
    groups, rows_in, cells = flows_band.shape
    coefs = table.shape[1]
    per = coefs // groups
    table_t = jnp.transpose(table)
    high = lax.reduce_precision(table, exponent_bits=8, mantissa_bits=7)
    rest = table - high
    middle = lax.reduce_precision(rest, exponent_bits=8, mantissa_bits=7)
    low = lax.reduce_precision(rest - middle, exponent_bits=8, mantissa_bits=7)
    stacked = jnp.concatenate([high, middle, middle, high, low, high], axis=1)
    stacked = stacked.astype(jnp.bfloat16)
    steps = cells // block
    return pl.pallas_call(
        functools.partial(friction_kernel, groups),
        grid=(steps,),
        in_specs=[
            pl.BlockSpec(stacked.shape, lambda i: (0, 0)),
            pl.BlockSpec(table_t.shape, lambda i: (0, 0)),
            pl.BlockSpec((groups, rows_in, block), lambda i: (0, 0, i)),
            pl.BlockSpec((1, block), lambda i: (0, i)),
        ],
        out_specs=[
            pl.BlockSpec((groups, 2 * per, block), lambda i: (0, 0, i)),
            pl.BlockSpec((pl.Squeezed(), 1, block), lambda i: (i, 0, 0)),
        ],
        out_shape=[
            jax.ShapeDtypeStruct((groups, 2 * per, cells), jnp.float32),
            jax.ShapeDtypeStruct((steps, 1, block), jnp.float32),
        ],
        scratch_shapes=[
            pltpu.VMEM((coefs, block), jnp.float32),
            pltpu.VMEM((6 * coefs, block), jnp.bfloat16),
        ],
        compiler_params=pltpu.CompilerParams(vmem_limit_bytes=48 * 1024 * 1024),
    )(stacked, table_t, flows_band, drag_band)


def local(direction, base_flow, water_depth, drag_factor, wet_mask, pieces=2):
    local_coefs = direction.shape[1]
    tile_rows = direction.shape[2]
    tile_cols = direction.shape[3]
    groups = lax.axis_size("freq")
    member = lax.axis_index("freq")
    band_rows = tile_rows // groups
    piece_rows = band_rows // pieces
    piece_cells = piece_rows * tile_cols
    lat_place = lax.axis_index("lat")
    lat_count = lax.axis_size("lat")
    total_rows = tile_rows * lat_count
    wet_cells = wet_mask.astype(jnp.float32)
    height = direction[0] * wet_cells
    east = direction[1] * wet_cells
    north = direction[2] * wet_cells
    flows = jnp.concatenate([base_flow, jnp.stack([east, north])], axis=0)
    flows = flows.reshape(4 * local_coefs, groups, pieces, piece_rows, tile_cols)
    table = samples_table(NTIME, NCON)
    band_start = member * band_rows
    drag_band = lax.dynamic_slice_in_dim(drag_factor, band_start, band_rows, 0)
    drag_band = drag_band.reshape(pieces, 1, piece_cells)
    payloads = [
        jnp.moveaxis(flows[:, :, piece], 1, 0).reshape(groups, 4 * local_coefs, piece_cells)
        for piece in range(pieces)
    ]
    sent = [lax.all_to_all(payloads[0], "freq", split_axis=0, concat_axis=0, tiled=True)]
    planes = jnp.stack([height, east, north, water_depth * east, water_depth * north])
    extended = extended_2(planes, (("lat", 2), ("lon", 3)), 1)
    rim_keep = jnp.ones((tile_rows + 2,), jnp.float32)
    rim_keep = rim_keep.at[0].set(jnp.where(lat_place == 0, 0.0, 1.0))
    rim_keep = rim_keep.at[tile_rows + 1].set(jnp.where(lat_place == lat_count - 1, 0.0, 1.0))
    extended = extended * rim_keep[:, None]
    local_count = local_coefs // 2
    first_con = member * local_count
    angular_local = OMEGA_STEP * (first_con + jnp.arange(local_count, dtype=jnp.int32) + 1).astype(
        jnp.float32
    )
    row_global = lat_place * tile_rows + jnp.arange(tile_rows, dtype=jnp.int32)
    rotation = rotation_of(row_global, total_rows)
    linear_part = linear_residual(
        extended, tile_rows, tile_cols, angular_local[:, None, None], rotation[:, None]
    )
    later = lax.optimization_barrier((payloads[1:], linear_part))
    linear_part = later[1]
    for payload in later[0]:
        sent.append(lax.all_to_all(payload, "freq", split_axis=0, concat_axis=0, tiled=True))
    shape_piece = (groups, pieces, piece_rows, tile_cols)
    linear_part = linear_part.reshape(3, local_coefs, *shape_piece)
    wet_piece = wet_cells.reshape(shape_piece)
    rotation_piece = rotation.reshape(groups, pieces, piece_rows, 1)
    results = []
    for piece in range(pieces):
        packed, rate = friction_band(sent[piece], drag_band[piece], table, tile_cols)
        rate = jnp.broadcast_to(
            rate.reshape(1, 1, piece_cells).reshape(1, 2 * local_coefs, piece_cells // (2 * local_coefs)),
            (groups, 2 * local_coefs, piece_cells // (2 * local_coefs)),
        )
        payload = jnp.concatenate([packed, rate], axis=2)
        back = lax.all_to_all(payload, "freq", split_axis=0, concat_axis=0, tiled=True)
        friction = back[:, :, :piece_cells].reshape(groups, 2, local_coefs, piece_rows, tile_cols)
        friction = jnp.moveaxis(friction, 0, 2)
        drag_rate = back[:, :, piece_cells:].reshape(groups, piece_rows, tile_cols)
        linear_piece = linear_part[:, :, :, piece]
        residual = (
            linear_piece + jnp.concatenate([jnp.zeros_like(friction[:1]), friction], axis=0)
        ) * wet_piece[:, piece]
        results.append(
            precondition(
                residual,
                angular_local[:, None, None, None],
                rotation_piece[:, piece],
                drag_rate,
            )
        )
    return jnp.stack(results, axis=3).reshape(3, local_coefs, tile_rows, tile_cols)


def solution(mesh):
    placed = (
        P(None, "freq", "lat", "lon"),
        P(None, "freq", "lat", "lon"),
        P("lat", "lon"),
        P("lat", "lon"),
        P("lat", "lon"),
    )
    return jax.shard_map(
        local, mesh=mesh, in_specs=placed, out_specs=P(None, "freq", "lat", "lon"), check_vma=False
    )
```

```python
import functools
import math

import jax
import jax.numpy as jnp
from jax import lax
from jax.experimental import pallas as pl
from jax.experimental.pallas import tpu as pltpu
from jax.sharding import PartitionSpec as P

NCON = 16
NTIME = 256


LINEAR_DRAG = 0.5
GRAVITY = 1.0
OMEGA_STEP = 0.25
SPEED_SOFT = 0.01


def extended_2(block, sides, width):
    for axis, dim in sides:
        count = lax.axis_size(axis)
        forward = [(i, i + 1) for i in range(count - 1)]
        forward.append((count - 1, 0))
        backward = [(target, source) for source, target in forward]
        low = lax.ppermute(
            lax.slice_in_dim(block, block.shape[dim] - width, None, axis=dim), axis, forward
        )
        high = lax.ppermute(lax.slice_in_dim(block, 0, width, axis=dim), axis, backward)
        block = jnp.concatenate([low, block, high], axis=dim)
    return block


def samples_table(sample_count, constituents):
    sample_index = jnp.arange(sample_count, dtype=jnp.int32)
    harmonic = jnp.arange(1, constituents + 1, dtype=jnp.int32)
    wrapped_turns = sample_index[:, None] * harmonic[None, :] % sample_count
    phase_angle = wrapped_turns.astype(jnp.float32) * (2.0 * math.pi / sample_count)
    table = jnp.stack([jnp.cos(phase_angle), jnp.sin(phase_angle)], axis=2)
    return table.reshape(sample_count, 2 * constituents)


def rotation_of(row_index, total_rows):
    return 0.5 + (row_index.astype(jnp.float32) + 0.5) / total_rows


def tendency(values, angular):
    cos_sin = values.reshape((values.shape[0] // 2, 2) + values.shape[1:])
    moved = jnp.stack([angular * cos_sin[:, 1], -angular * cos_sin[:, 0]], axis=1)
    return moved.reshape(values.shape)


def linear_residual(extended, tile_rows, tile_cols, angular, rotation):

    def neighbour(plane, row_step, col_step):
        return extended[
            plane,
            :,
            1 + row_step : 1 + row_step + tile_rows,
            1 + col_step : 1 + col_step + tile_cols,
        ]

    height = neighbour(0, 0, 0)
    east = neighbour(1, 0, 0)
    north = neighbour(2, 0, 0)
    res_height = (
        tendency(height, angular)
        + neighbour(3, 0, 0)
        - neighbour(3, 0, -1)
        + neighbour(4, 0, 0)
        - neighbour(4, -1, 0)
    )
    north_mean = 0.25 * (north + neighbour(2, 0, 1) + neighbour(2, -1, 0) + neighbour(2, -1, 1))
    east_mean = 0.25 * (east + neighbour(1, 0, -1) + neighbour(1, 1, 0) + neighbour(1, 1, -1))
    res_east = (
        tendency(east, angular)
        + LINEAR_DRAG * east
        - rotation * north_mean
        + GRAVITY * (neighbour(0, 0, 1) - height)
    )
    res_north = (
        tendency(north, angular)
        + LINEAR_DRAG * north
        + rotation * east_mean
        + GRAVITY * (neighbour(0, 1, 0) - height)
    )
    return jnp.stack([res_height, res_east, res_north])


def friction_row(row_block, drag_row, table):
    highest = lax.Precision.HIGHEST
    series = jnp.einsum("tc,fcn->ftn", table, row_block, precision=highest)
    base_east, base_north, step_east, step_north = (series[0], series[1], series[2], series[3])
    magnitude = jnp.sqrt(base_east * base_east + base_north * base_north + SPEED_SOFT)
    projected = (base_east * step_east + base_north * step_north) / magnitude
    force_east = drag_row * (magnitude * step_east + base_east * projected)
    force_north = drag_row * (magnitude * step_north + base_north * projected)
    forces = jnp.stack([force_east, force_north])
    analysed = jnp.einsum("tc,ftn->fcn", table, forces, precision=highest) * (2.0 / table.shape[0])
    drag_rate = drag_row * jnp.mean(magnitude, axis=0)
    return (analysed, drag_rate)


def precondition(residual, angular, rotation, drag_rate):
    shaped = residual.reshape((3, residual.shape[1] // 2, 2) + residual.shape[2:])
    cos_part = shaped[:, :, 0]
    sin_part = shaped[:, :, 1]
    height_cos = -sin_part[0] / angular
    height_sin = cos_part[0] / angular
    real_rate = drag_rate + LINEAR_DRAG
    det_real = real_rate * real_rate - angular * angular + rotation * rotation
    det_imag = 2.0 * real_rate * angular
    det_norm = det_real * det_real + det_imag * det_imag
    inv_real = det_real / det_norm
    inv_imag = -det_imag / det_norm
    east_re = cos_part[1]
    east_im = -sin_part[1]
    north_re = cos_part[2]
    north_im = -sin_part[2]
    num_east_re = real_rate * east_re - angular * east_im + rotation * north_re
    num_east_im = real_rate * east_im + angular * east_re + rotation * north_im
    num_north_re = -rotation * east_re + real_rate * north_re - angular * north_im
    num_north_im = -rotation * east_im + real_rate * north_im + angular * north_re
    east_out_re = num_east_re * inv_real - num_east_im * inv_imag
    east_out_im = num_east_re * inv_imag + num_east_im * inv_real
    north_out_re = num_north_re * inv_real - num_north_im * inv_imag
    north_out_im = num_north_re * inv_imag + num_north_im * inv_real
    cosines = jnp.stack([height_cos, east_out_re, north_out_re])
    sines = jnp.stack([height_sin, -east_out_im, -north_out_im])
    return jnp.stack([cosines, sines], axis=2).reshape(residual.shape)


def split_three(values):
    high = values.astype(jnp.bfloat16)
    rest = values - high.astype(jnp.float32)
    middle = rest.astype(jnp.bfloat16)
    low = (rest - middle.astype(jnp.float32)).astype(jnp.bfloat16)
    return high, middle, low


def friction_kernel(
    groups, stacked_ref, table_t_ref, flows_ref, drag_ref, out_ref, rate_ref, gather_ref, parts_ref
):
    highest = lax.Precision.HIGHEST
    stacked = stacked_ref[...]
    coefs = gather_ref.shape[0]
    per = coefs // groups

    def synth(field):
        for source in range(groups):
            gather_ref[source * per : (source + 1) * per, :] = flows_ref[
                source, field * per : (field + 1) * per, :
            ]
        high, middle, low = split_three(gather_ref[...])
        for slot, part in enumerate((high, middle, high, low, high, middle)):
            parts_ref[slot * coefs : (slot + 1) * coefs, :] = part
        return jnp.dot(stacked, parts_ref[...], preferred_element_type=jnp.float32)

    base_east, base_north, step_east, step_north = synth(0), synth(1), synth(2), synth(3)
    drag_row = drag_ref[...]
    magnitude = jnp.sqrt(base_east * base_east + base_north * base_north + SPEED_SOFT)
    projected = (base_east * step_east + base_north * step_north) / magnitude
    force_east = drag_row * (magnitude * step_east + base_east * projected)
    force_north = drag_row * (magnitude * step_north + base_north * projected)
    table_t = table_t_ref[...]
    scale = 2.0 / stacked.shape[0]
    analysed_east = (
        jnp.dot(table_t, force_east, precision=highest, preferred_element_type=jnp.float32) * scale
    )
    analysed_north = (
        jnp.dot(table_t, force_north, precision=highest, preferred_element_type=jnp.float32)
        * scale
    )
    rate_ref[...] = drag_row * jnp.mean(magnitude, axis=0, keepdims=True)
    for group in range(groups):
        out_ref[group, 0:per, :] = analysed_east[group * per : (group + 1) * per]
        out_ref[group, per : 2 * per, :] = analysed_north[group * per : (group + 1) * per]


def friction_band(flows_band, drag_band, table, block):
    groups, rows_in, cells = flows_band.shape
    coefs = table.shape[1]
    per = coefs // groups
    table_t = jnp.transpose(table)
    high = lax.reduce_precision(table, exponent_bits=8, mantissa_bits=7)
    rest = table - high
    middle = lax.reduce_precision(rest, exponent_bits=8, mantissa_bits=7)
    low = lax.reduce_precision(rest - middle, exponent_bits=8, mantissa_bits=7)
    stacked = jnp.concatenate([high, middle, middle, high, low, high], axis=1)
    stacked = stacked.astype(jnp.bfloat16)
    steps = cells // block
    return pl.pallas_call(
        functools.partial(friction_kernel, groups),
        grid=(steps,),
        in_specs=[
            pl.BlockSpec(stacked.shape, lambda i: (0, 0)),
            pl.BlockSpec(table_t.shape, lambda i: (0, 0)),
            pl.BlockSpec((groups, rows_in, block), lambda i: (0, 0, i)),
            pl.BlockSpec((1, block), lambda i: (0, i)),
        ],
        out_specs=[
            pl.BlockSpec((groups, 2 * per, block), lambda i: (0, 0, i)),
            pl.BlockSpec((pl.Squeezed(), 1, block), lambda i: (i, 0, 0)),
        ],
        out_shape=[
            jax.ShapeDtypeStruct((groups, 2 * per, cells), jnp.float32),
            jax.ShapeDtypeStruct((steps, 1, block), jnp.float32),
        ],
        scratch_shapes=[
            pltpu.VMEM((coefs, block), jnp.float32),
            pltpu.VMEM((6 * coefs, block), jnp.bfloat16),
        ],
        compiler_params=pltpu.CompilerParams(vmem_limit_bytes=48 * 1024 * 1024),
    )(stacked, table_t, flows_band, drag_band)


MESH = pl.DeviceIdType.MESH


def friction_block(groups, stacked, table_t, flows_ref, drag_row, offset, width, gather_ref, parts_ref):
    coefs = gather_ref.shape[0]
    per = coefs // groups
    cells = pl.ds(offset, width)

    def synth(field):
        for source in range(groups):
            gather_ref[source * per : (source + 1) * per, :] = flows_ref[
                source, field * per : (field + 1) * per, cells
            ]
        high, middle, low = split_three(gather_ref[...])
        for slot, part in enumerate((high, middle, high, low, high, middle)):
            parts_ref[slot * coefs : (slot + 1) * coefs, :] = part
        return jnp.dot(stacked, parts_ref[...], preferred_element_type=jnp.float32)

    highest = lax.Precision.HIGHEST
    base_east, base_north, step_east, step_north = synth(0), synth(1), synth(2), synth(3)
    magnitude = jnp.sqrt(base_east * base_east + base_north * base_north + SPEED_SOFT)
    projected = (base_east * step_east + base_north * step_north) / magnitude
    force_east = drag_row * (magnitude * step_east + base_east * projected)
    force_north = drag_row * (magnitude * step_north + base_north * projected)
    scale = 2.0 / stacked.shape[0]
    analysed_east = (
        jnp.dot(table_t, force_east, precision=highest, preferred_element_type=jnp.float32) * scale
    )
    analysed_north = (
        jnp.dot(table_t, force_north, precision=highest, preferred_element_type=jnp.float32)
        * scale
    )
    drag_rate = drag_row * jnp.mean(magnitude, axis=0, keepdims=True)
    return analysed_east, analysed_north, drag_rate


def exchange_kernel(
    groups,
    width,
    stacked_ref,
    table_t_ref,
    first_ref,
    second_ref,
    drag_ref,
    back_first_ref,
    back_second_ref,
    arrived,
    results,
    landed,
    gather_ref,
    parts_ref,
    send_sems,
    recv_sems,
    local_sems,
):
    me = lax.axis_index("freq")
    lat = lax.axis_index("lat")
    lon = lax.axis_index("lon")
    cells = first_ref.shape[2]
    coefs = gather_ref.shape[0]
    per = coefs // groups
    blocks = cells // width

    barrier = pltpu.get_barrier_semaphore()
    for distance in range(1, groups):
        peer = lax.rem(me + distance, groups)
        pl.semaphore_signal(barrier, inc=1, device_id=(peer, lat, lon), device_id_type=MESH)
    pl.semaphore_wait(barrier, groups - 1)

    def exchange(phase, source_of, target_of):
        copies = []
        for distance in range(1, groups):
            peer = lax.rem(me + distance, groups)
            copy = pltpu.make_async_remote_copy(
                src_ref=source_of(peer),
                dst_ref=target_of(me),
                send_sem=send_sems.at[phase, distance],
                recv_sem=recv_sems.at[phase, distance],
                device_id=(peer, lat, lon),
                device_id_type=MESH,
            )
            copy.start()
            copies.append(copy)
        local = pltpu.make_async_copy(source_of(me), target_of(me), local_sems.at[phase])
        local.start()
        return copies, local

    def wait_arrivals(phase, source_of, target_of):
        for distance in range(1, groups):
            sender = lax.rem(me + groups - distance, groups)
            pltpu.make_async_remote_copy(
                src_ref=source_of(sender),
                dst_ref=target_of(sender),
                send_sem=send_sems.at[phase, distance],
                recv_sem=recv_sems.at[phase, distance],
                device_id=(sender, lat, lon),
                device_id_type=MESH,
            ).wait_recv()

    sending = [exchange(0, lambda g: second_ref.at[g], lambda g: arrived.at[g])]
    stacked = stacked_ref[...]
    table_t = table_t_ref[...]

    def compute(piece, flows_ref):
        def block(index, carry):
            offset = pl.multiple_of(index * width, width)
            drag_row = drag_ref[piece, :, pl.ds(offset, width)]
            east, north, rate = friction_block(
                groups, stacked, table_t, flows_ref, drag_row, offset, width, gather_ref, parts_ref
            )
            for group in range(groups):
                results[piece, group, 0:per, pl.ds(offset, width)] = east[
                    group * per : (group + 1) * per
                ]
                results[piece, group, per : 2 * per, pl.ds(offset, width)] = north[
                    group * per : (group + 1) * per
                ]
                results[piece, group, pl.ds(index, 1), pl.ds(cells, width)] = rate
            return carry

        lax.fori_loop(0, blocks, block, 0)

    compute(0, first_ref)
    sending.append(exchange(1, lambda g: results.at[0, g], lambda g: landed.at[0, g]))
    wait_arrivals(0, lambda g: second_ref.at[g], lambda g: arrived.at[g])
    sending[0][1].wait()
    compute(1, arrived)
    sending.append(exchange(2, lambda g: results.at[1, g], lambda g: landed.at[1, g]))
    for copies, local in sending:
        for copy in copies:
            copy.wait_send()
    sending[1][1].wait()
    sending[2][1].wait()
    wait_arrivals(1, lambda g: results.at[0, g], lambda g: landed.at[0, g])
    wait_arrivals(2, lambda g: results.at[1, g], lambda g: landed.at[1, g])
    back_first_ref[...] = landed[0]
    back_second_ref[...] = landed[1]


def exchange_friction(first, second, drag_band, table, width):
    groups, rows_in, cells = first.shape
    coefs = table.shape[1]
    per = coefs // groups
    table_t = jnp.transpose(table)
    high = lax.reduce_precision(table, exponent_bits=8, mantissa_bits=7)
    rest = table - high
    middle = lax.reduce_precision(rest, exponent_bits=8, mantissa_bits=7)
    low = lax.reduce_precision(rest - middle, exponent_bits=8, mantissa_bits=7)
    stacked = jnp.concatenate([high, middle, middle, high, low, high], axis=1)
    stacked = stacked.astype(jnp.bfloat16)
    returned = (groups, 2 * per, cells + cells // (2 * per))
    vmem = pl.BlockSpec(memory_space=pltpu.VMEM)
    return pl.pallas_call(
        functools.partial(exchange_kernel, groups, width),
        in_specs=[vmem] * 5,
        out_specs=[vmem, vmem],
        out_shape=[jax.ShapeDtypeStruct(returned, jnp.float32)] * 2,
        scratch_shapes=[
            pltpu.VMEM(first.shape, jnp.float32),
            pltpu.VMEM((2,) + returned, jnp.float32),
            pltpu.VMEM((2,) + returned, jnp.float32),
            pltpu.VMEM((coefs, width), jnp.float32),
            pltpu.VMEM((6 * coefs, width), jnp.bfloat16),
            pltpu.SemaphoreType.DMA((3, groups)),
            pltpu.SemaphoreType.DMA((3, groups)),
            pltpu.SemaphoreType.DMA((3,)),
        ],
        compiler_params=pltpu.CompilerParams(
            collective_id=0, has_side_effects=True, vmem_limit_bytes=60 * 1024 * 1024
        ),
    )(stacked, table_t, first, second, drag_band)


def local(direction, base_flow, water_depth, drag_factor, wet_mask, pieces=2):
    local_coefs = direction.shape[1]
    tile_rows = direction.shape[2]
    tile_cols = direction.shape[3]
    groups = lax.axis_size("freq")
    member = lax.axis_index("freq")
    band_rows = tile_rows // groups
    piece_rows = band_rows // pieces
    piece_cells = piece_rows * tile_cols
    lat_place = lax.axis_index("lat")
    lat_count = lax.axis_size("lat")
    total_rows = tile_rows * lat_count
    wet_cells = wet_mask.astype(jnp.float32)
    height = direction[0] * wet_cells
    east = direction[1] * wet_cells
    north = direction[2] * wet_cells
    flows = jnp.concatenate([base_flow, jnp.stack([east, north])], axis=0)
    flows = flows.reshape(4 * local_coefs, groups, pieces, piece_rows, tile_cols)
    table = samples_table(NTIME, NCON)
    band_start = member * band_rows
    drag_band = lax.dynamic_slice_in_dim(drag_factor, band_start, band_rows, 0)
    drag_band = drag_band.reshape(pieces, 1, piece_cells)
    payloads = [
        jnp.moveaxis(flows[:, :, piece], 1, 0).reshape(groups, 4 * local_coefs, piece_cells)
        for piece in range(pieces)
    ]
    sent = [lax.all_to_all(payloads[0], "freq", split_axis=0, concat_axis=0, tiled=True)]
    planes = jnp.stack([height, east, north, water_depth * east, water_depth * north])
    extended = extended_2(planes, (("lat", 2), ("lon", 3)), 1)
    rim_keep = jnp.ones((tile_rows + 2,), jnp.float32)
    rim_keep = rim_keep.at[0].set(jnp.where(lat_place == 0, 0.0, 1.0))
    rim_keep = rim_keep.at[tile_rows + 1].set(jnp.where(lat_place == lat_count - 1, 0.0, 1.0))
    extended = extended * rim_keep[:, None]
    local_count = local_coefs // 2
    first_con = member * local_count
    angular_local = OMEGA_STEP * (first_con + jnp.arange(local_count, dtype=jnp.int32) + 1).astype(
        jnp.float32
    )
    row_global = lat_place * tile_rows + jnp.arange(tile_rows, dtype=jnp.int32)
    rotation = rotation_of(row_global, total_rows)
    linear_part = linear_residual(
        extended, tile_rows, tile_cols, angular_local[:, None, None], rotation[:, None]
    )
    later = lax.optimization_barrier((payloads[1], linear_part))
    linear_part = later[1]
    shape_piece = (groups, pieces, piece_rows, tile_cols)
    linear_part = linear_part.reshape(3, local_coefs, *shape_piece)
    wet_piece = wet_cells.reshape(shape_piece)
    rotation_piece = rotation.reshape(groups, pieces, piece_rows, 1)
    backs = exchange_friction(sent[0], later[0], drag_band, table, tile_cols)
    results = []
    for piece in range(pieces):
        back = backs[piece]
        friction = back[:, :, :piece_cells].reshape(groups, 2, local_coefs, piece_rows, tile_cols)
        friction = jnp.moveaxis(friction, 0, 2)
        drag_rate = back[:, :, piece_cells:].reshape(groups, piece_rows, tile_cols)
        linear_piece = linear_part[:, :, :, piece]
        residual = (
            linear_piece + jnp.concatenate([jnp.zeros_like(friction[:1]), friction], axis=0)
        ) * wet_piece[:, piece]
        results.append(
            precondition(
                residual,
                angular_local[:, None, None, None],
                rotation_piece[:, piece],
                drag_rate,
            )
        )
    return jnp.stack(results, axis=3).reshape(3, local_coefs, tile_rows, tile_cols)


def solution(mesh):
    placed = (
        P(None, "freq", "lat", "lon"),
        P(None, "freq", "lat", "lon"),
        P("lat", "lon"),
        P("lat", "lon"),
        P("lat", "lon"),
    )
    return jax.shard_map(
        local, mesh=mesh, in_specs=placed, out_specs=P(None, "freq", "lat", "lon"), check_vma=False
    )
```

```python
import functools
import math

import jax
import jax.numpy as jnp
from jax import lax
from jax.experimental import pallas as pl
from jax.experimental.pallas import tpu as pltpu
from jax.sharding import PartitionSpec as P

NCON = 16
NTIME = 256


LINEAR_DRAG = 0.5
GRAVITY = 1.0
OMEGA_STEP = 0.25
SPEED_SOFT = 0.01


def extended_2(block, sides, width):
    for axis, dim in sides:
        count = lax.axis_size(axis)
        forward = [(i, i + 1) for i in range(count - 1)]
        forward.append((count - 1, 0))
        backward = [(target, source) for source, target in forward]
        low = lax.ppermute(
            lax.slice_in_dim(block, block.shape[dim] - width, None, axis=dim), axis, forward
        )
        high = lax.ppermute(lax.slice_in_dim(block, 0, width, axis=dim), axis, backward)
        block = jnp.concatenate([low, block, high], axis=dim)
    return block


def samples_table(sample_count, constituents):
    sample_index = jnp.arange(sample_count, dtype=jnp.int32)
    harmonic = jnp.arange(1, constituents + 1, dtype=jnp.int32)
    wrapped_turns = sample_index[:, None] * harmonic[None, :] % sample_count
    phase_angle = wrapped_turns.astype(jnp.float32) * (2.0 * math.pi / sample_count)
    table = jnp.stack([jnp.cos(phase_angle), jnp.sin(phase_angle)], axis=2)
    return table.reshape(sample_count, 2 * constituents)


def rotation_of(row_index, total_rows):
    return 0.5 + (row_index.astype(jnp.float32) + 0.5) / total_rows


def tendency(values, angular):
    cos_sin = values.reshape((values.shape[0] // 2, 2) + values.shape[1:])
    moved = jnp.stack([angular * cos_sin[:, 1], -angular * cos_sin[:, 0]], axis=1)
    return moved.reshape(values.shape)


def linear_residual(extended, tile_rows, tile_cols, angular, rotation):

    def neighbour(plane, row_step, col_step):
        return extended[
            plane,
            :,
            1 + row_step : 1 + row_step + tile_rows,
            1 + col_step : 1 + col_step + tile_cols,
        ]

    height = neighbour(0, 0, 0)
    east = neighbour(1, 0, 0)
    north = neighbour(2, 0, 0)
    res_height = (
        tendency(height, angular)
        + neighbour(3, 0, 0)
        - neighbour(3, 0, -1)
        + neighbour(4, 0, 0)
        - neighbour(4, -1, 0)
    )
    north_mean = 0.25 * (north + neighbour(2, 0, 1) + neighbour(2, -1, 0) + neighbour(2, -1, 1))
    east_mean = 0.25 * (east + neighbour(1, 0, -1) + neighbour(1, 1, 0) + neighbour(1, 1, -1))
    res_east = (
        tendency(east, angular)
        + LINEAR_DRAG * east
        - rotation * north_mean
        + GRAVITY * (neighbour(0, 0, 1) - height)
    )
    res_north = (
        tendency(north, angular)
        + LINEAR_DRAG * north
        + rotation * east_mean
        + GRAVITY * (neighbour(0, 1, 0) - height)
    )
    return jnp.stack([res_height, res_east, res_north])


def friction_row(row_block, drag_row, table):
    highest = lax.Precision.HIGHEST
    series = jnp.einsum("tc,fcn->ftn", table, row_block, precision=highest)
    base_east, base_north, step_east, step_north = (series[0], series[1], series[2], series[3])
    magnitude = jnp.sqrt(base_east * base_east + base_north * base_north + SPEED_SOFT)
    projected = (base_east * step_east + base_north * step_north) / magnitude
    force_east = drag_row * (magnitude * step_east + base_east * projected)
    force_north = drag_row * (magnitude * step_north + base_north * projected)
    forces = jnp.stack([force_east, force_north])
    analysed = jnp.einsum("tc,ftn->fcn", table, forces, precision=highest) * (2.0 / table.shape[0])
    drag_rate = drag_row * jnp.mean(magnitude, axis=0)
    return (analysed, drag_rate)


def precondition(residual, angular, rotation, drag_rate):
    shaped = residual.reshape((3, residual.shape[1] // 2, 2) + residual.shape[2:])
    cos_part = shaped[:, :, 0]
    sin_part = shaped[:, :, 1]
    height_cos = -sin_part[0] / angular
    height_sin = cos_part[0] / angular
    real_rate = drag_rate + LINEAR_DRAG
    det_real = real_rate * real_rate - angular * angular + rotation * rotation
    det_imag = 2.0 * real_rate * angular
    det_norm = det_real * det_real + det_imag * det_imag
    inv_real = det_real / det_norm
    inv_imag = -det_imag / det_norm
    east_re = cos_part[1]
    east_im = -sin_part[1]
    north_re = cos_part[2]
    north_im = -sin_part[2]
    num_east_re = real_rate * east_re - angular * east_im + rotation * north_re
    num_east_im = real_rate * east_im + angular * east_re + rotation * north_im
    num_north_re = -rotation * east_re + real_rate * north_re - angular * north_im
    num_north_im = -rotation * east_im + real_rate * north_im + angular * north_re
    east_out_re = num_east_re * inv_real - num_east_im * inv_imag
    east_out_im = num_east_re * inv_imag + num_east_im * inv_real
    north_out_re = num_north_re * inv_real - num_north_im * inv_imag
    north_out_im = num_north_re * inv_imag + num_north_im * inv_real
    cosines = jnp.stack([height_cos, east_out_re, north_out_re])
    sines = jnp.stack([height_sin, -east_out_im, -north_out_im])
    return jnp.stack([cosines, sines], axis=2).reshape(residual.shape)


def split_three(values):
    high = values.astype(jnp.bfloat16)
    rest = values - high.astype(jnp.float32)
    middle = rest.astype(jnp.bfloat16)
    low = (rest - middle.astype(jnp.float32)).astype(jnp.bfloat16)
    return high, middle, low


def friction_kernel(
    groups, stacked_ref, table_t_ref, flows_ref, drag_ref, out_ref, rate_ref, gather_ref, parts_ref
):
    highest = lax.Precision.HIGHEST
    stacked = stacked_ref[...]
    coefs = gather_ref.shape[0]
    per = coefs // groups

    def synth(field):
        for source in range(groups):
            gather_ref[source * per : (source + 1) * per, :] = flows_ref[
                source, field * per : (field + 1) * per, :
            ]
        high, middle, low = split_three(gather_ref[...])
        for slot, part in enumerate((high, middle, high, low, high, middle)):
            parts_ref[slot * coefs : (slot + 1) * coefs, :] = part
        return jnp.dot(stacked, parts_ref[...], preferred_element_type=jnp.float32)

    base_east, base_north, step_east, step_north = synth(0), synth(1), synth(2), synth(3)
    drag_row = drag_ref[...]
    magnitude = jnp.sqrt(base_east * base_east + base_north * base_north + SPEED_SOFT)
    projected = (base_east * step_east + base_north * step_north) / magnitude
    force_east = drag_row * (magnitude * step_east + base_east * projected)
    force_north = drag_row * (magnitude * step_north + base_north * projected)
    table_t = table_t_ref[...]
    scale = 2.0 / stacked.shape[0]
    analysed_east = (
        jnp.dot(table_t, force_east, precision=highest, preferred_element_type=jnp.float32) * scale
    )
    analysed_north = (
        jnp.dot(table_t, force_north, precision=highest, preferred_element_type=jnp.float32)
        * scale
    )
    rate_ref[...] = drag_row * jnp.mean(magnitude, axis=0, keepdims=True)
    for group in range(groups):
        out_ref[group, 0:per, :] = analysed_east[group * per : (group + 1) * per]
        out_ref[group, per : 2 * per, :] = analysed_north[group * per : (group + 1) * per]


def friction_band(flows_band, drag_band, table, block):
    groups, rows_in, cells = flows_band.shape
    coefs = table.shape[1]
    per = coefs // groups
    table_t = jnp.transpose(table)
    high = lax.reduce_precision(table, exponent_bits=8, mantissa_bits=7)
    rest = table - high
    middle = lax.reduce_precision(rest, exponent_bits=8, mantissa_bits=7)
    low = lax.reduce_precision(rest - middle, exponent_bits=8, mantissa_bits=7)
    stacked = jnp.concatenate([high, middle, middle, high, low, high], axis=1)
    stacked = stacked.astype(jnp.bfloat16)
    steps = cells // block
    return pl.pallas_call(
        functools.partial(friction_kernel, groups),
        grid=(steps,),
        in_specs=[
            pl.BlockSpec(stacked.shape, lambda i: (0, 0)),
            pl.BlockSpec(table_t.shape, lambda i: (0, 0)),
            pl.BlockSpec((groups, rows_in, block), lambda i: (0, 0, i)),
            pl.BlockSpec((1, block), lambda i: (0, i)),
        ],
        out_specs=[
            pl.BlockSpec((groups, 2 * per, block), lambda i: (0, 0, i)),
            pl.BlockSpec((pl.Squeezed(), 1, block), lambda i: (i, 0, 0)),
        ],
        out_shape=[
            jax.ShapeDtypeStruct((groups, 2 * per, cells), jnp.float32),
            jax.ShapeDtypeStruct((steps, 1, block), jnp.float32),
        ],
        scratch_shapes=[
            pltpu.VMEM((coefs, block), jnp.float32),
            pltpu.VMEM((6 * coefs, block), jnp.bfloat16),
        ],
        compiler_params=pltpu.CompilerParams(vmem_limit_bytes=48 * 1024 * 1024),
    )(stacked, table_t, flows_band, drag_band)


MESH = pl.DeviceIdType.MESH


def friction_block(groups, stacked, table_t, flows_ref, drag_row, offset, width, gather_ref, parts_ref):
    coefs = gather_ref.shape[0]
    per = coefs // groups
    cells = pl.ds(offset, width)

    def synth(field):
        for source in range(groups):
            gather_ref[source * per : (source + 1) * per, :] = flows_ref[
                source, field * per : (field + 1) * per, cells
            ]
        high, middle, low = split_three(gather_ref[...])
        for slot, part in enumerate((high, middle, high, low, high, middle)):
            parts_ref[slot * coefs : (slot + 1) * coefs, :] = part
        return jnp.dot(stacked, parts_ref[...], preferred_element_type=jnp.float32)

    highest = lax.Precision.HIGHEST
    base_east, base_north, step_east, step_north = synth(0), synth(1), synth(2), synth(3)
    magnitude = jnp.sqrt(base_east * base_east + base_north * base_north + SPEED_SOFT)
    projected = (base_east * step_east + base_north * step_north) / magnitude
    force_east = drag_row * (magnitude * step_east + base_east * projected)
    force_north = drag_row * (magnitude * step_north + base_north * projected)
    scale = 2.0 / stacked.shape[0]
    analysed_east = (
        jnp.dot(table_t, force_east, precision=highest, preferred_element_type=jnp.float32) * scale
    )
    analysed_north = (
        jnp.dot(table_t, force_north, precision=highest, preferred_element_type=jnp.float32)
        * scale
    )
    drag_rate = drag_row * jnp.mean(magnitude, axis=0, keepdims=True)
    return analysed_east, analysed_north, drag_rate


def exchange_kernel(
    groups,
    width,
    stacked_ref,
    table_t_ref,
    first_ref,
    second_ref,
    drag_ref,
    back_first_ref,
    back_second_ref,
    arrived,
    results,
    landed,
    gather_ref,
    parts_ref,
    send_sems,
    recv_sems,
    local_sems,
):
    me = lax.axis_index("freq")
    lat = lax.axis_index("lat")
    lon = lax.axis_index("lon")
    cells = first_ref.shape[2]
    coefs = gather_ref.shape[0]
    per = coefs // groups
    blocks = cells // width

    barrier = pltpu.get_barrier_semaphore()
    for distance in range(1, groups):
        peer = lax.rem(me + distance, groups)
        pl.semaphore_signal(barrier, inc=1, device_id=(peer, lat, lon), device_id_type=MESH)
    pl.semaphore_wait(barrier, groups - 1)

    def exchange(phase, source_of, target_of):
        copies = []
        for distance in range(1, groups):
            peer = lax.rem(me + distance, groups)
            copy = pltpu.make_async_remote_copy(
                src_ref=source_of(peer),
                dst_ref=target_of(me),
                send_sem=send_sems.at[phase, distance],
                recv_sem=recv_sems.at[phase, distance],
                device_id=(peer, lat, lon),
                device_id_type=MESH,
            )
            copy.start()
            copies.append(copy)
        local = pltpu.make_async_copy(source_of(me), target_of(me), local_sems.at[phase])
        local.start()
        return copies, local

    def wait_arrivals(phase, source_of, target_of):
        for distance in range(1, groups):
            sender = lax.rem(me + groups - distance, groups)
            pltpu.make_async_remote_copy(
                src_ref=source_of(sender),
                dst_ref=target_of(sender),
                send_sem=send_sems.at[phase, distance],
                recv_sem=recv_sems.at[phase, distance],
                device_id=(sender, lat, lon),
                device_id_type=MESH,
            ).wait_recv()

    sending = [exchange(0, lambda g: second_ref.at[g], lambda g: arrived.at[g])]
    stacked = stacked_ref[...]
    table_t = table_t_ref[...]

    def compute(piece, flows_ref, first_block, last_block):
        def block(index, carry):
            offset = pl.multiple_of(index * width, width)
            drag_row = drag_ref[piece, :, pl.ds(offset, width)]
            east, north, rate = friction_block(
                groups, stacked, table_t, flows_ref, drag_row, offset, width, gather_ref, parts_ref
            )
            for group in range(groups):
                results[piece, group, 0:per, pl.ds(offset, width)] = east[
                    group * per : (group + 1) * per
                ]
                results[piece, group, per : 2 * per, pl.ds(offset, width)] = north[
                    group * per : (group + 1) * per
                ]
                results[piece, group, pl.ds(index, 1), pl.ds(cells, width)] = rate
            return carry

        lax.fori_loop(first_block, last_block, block, 0)

    half = blocks // 2
    early = pl.ds(0, half * width)
    late = pl.ds(half * width, cells + cells // (2 * per) - half * width)
    compute(0, first_ref, 0, blocks)
    sending.append(exchange(1, lambda g: results.at[0, g], lambda g: landed.at[0, g]))
    wait_arrivals(0, lambda g: second_ref.at[g], lambda g: arrived.at[g])
    sending[0][1].wait()
    compute(1, arrived, 0, half)
    sending.append(
        exchange(2, lambda g: results.at[1, g, :, early], lambda g: landed.at[1, g, :, early])
    )
    compute(1, arrived, half, blocks)
    sending.append(
        exchange(3, lambda g: results.at[1, g, :, late], lambda g: landed.at[1, g, :, late])
    )
    for copies, local in sending:
        for copy in copies:
            copy.wait_send()
    for copies, local in sending[1:]:
        local.wait()
    wait_arrivals(1, lambda g: results.at[0, g], lambda g: landed.at[0, g])
    wait_arrivals(2, lambda g: results.at[1, g, :, early], lambda g: landed.at[1, g, :, early])
    wait_arrivals(3, lambda g: results.at[1, g, :, late], lambda g: landed.at[1, g, :, late])
    back_first_ref[...] = landed[0]
    back_second_ref[...] = landed[1]


def exchange_friction(first, second, drag_band, table, width):
    groups, rows_in, cells = first.shape
    coefs = table.shape[1]
    per = coefs // groups
    table_t = jnp.transpose(table)
    high = lax.reduce_precision(table, exponent_bits=8, mantissa_bits=7)
    rest = table - high
    middle = lax.reduce_precision(rest, exponent_bits=8, mantissa_bits=7)
    low = lax.reduce_precision(rest - middle, exponent_bits=8, mantissa_bits=7)
    stacked = jnp.concatenate([high, middle, middle, high, low, high], axis=1)
    stacked = stacked.astype(jnp.bfloat16)
    returned = (groups, 2 * per, cells + cells // (2 * per))
    vmem = pl.BlockSpec(memory_space=pltpu.VMEM)
    return pl.pallas_call(
        functools.partial(exchange_kernel, groups, width),
        in_specs=[vmem] * 5,
        out_specs=[vmem, vmem],
        out_shape=[jax.ShapeDtypeStruct(returned, jnp.float32)] * 2,
        scratch_shapes=[
            pltpu.VMEM(first.shape, jnp.float32),
            pltpu.VMEM((2,) + returned, jnp.float32),
            pltpu.VMEM((2,) + returned, jnp.float32),
            pltpu.VMEM((coefs, width), jnp.float32),
            pltpu.VMEM((6 * coefs, width), jnp.bfloat16),
            pltpu.SemaphoreType.DMA((4, groups)),
            pltpu.SemaphoreType.DMA((4, groups)),
            pltpu.SemaphoreType.DMA((4,)),
        ],
        compiler_params=pltpu.CompilerParams(
            collective_id=0, has_side_effects=True, vmem_limit_bytes=60 * 1024 * 1024
        ),
    )(stacked, table_t, first, second, drag_band)


def local(direction, base_flow, water_depth, drag_factor, wet_mask, pieces=2):
    local_coefs = direction.shape[1]
    tile_rows = direction.shape[2]
    tile_cols = direction.shape[3]
    groups = lax.axis_size("freq")
    member = lax.axis_index("freq")
    band_rows = tile_rows // groups
    piece_rows = band_rows // pieces
    piece_cells = piece_rows * tile_cols
    lat_place = lax.axis_index("lat")
    lat_count = lax.axis_size("lat")
    total_rows = tile_rows * lat_count
    wet_cells = wet_mask.astype(jnp.float32)
    height = direction[0] * wet_cells
    east = direction[1] * wet_cells
    north = direction[2] * wet_cells
    flows = jnp.concatenate([base_flow, jnp.stack([east, north])], axis=0)
    flows = flows.reshape(4 * local_coefs, groups, pieces, piece_rows, tile_cols)
    table = samples_table(NTIME, NCON)
    band_start = member * band_rows
    drag_band = lax.dynamic_slice_in_dim(drag_factor, band_start, band_rows, 0)
    drag_band = drag_band.reshape(pieces, 1, piece_cells)
    payloads = [
        jnp.moveaxis(flows[:, :, piece], 1, 0).reshape(groups, 4 * local_coefs, piece_cells)
        for piece in range(pieces)
    ]
    sent = [lax.all_to_all(payloads[0], "freq", split_axis=0, concat_axis=0, tiled=True)]
    planes = jnp.stack([height, east, north, water_depth * east, water_depth * north])
    extended = extended_2(planes, (("lat", 2), ("lon", 3)), 1)
    rim_keep = jnp.ones((tile_rows + 2,), jnp.float32)
    rim_keep = rim_keep.at[0].set(jnp.where(lat_place == 0, 0.0, 1.0))
    rim_keep = rim_keep.at[tile_rows + 1].set(jnp.where(lat_place == lat_count - 1, 0.0, 1.0))
    extended = extended * rim_keep[:, None]
    local_count = local_coefs // 2
    first_con = member * local_count
    angular_local = OMEGA_STEP * (first_con + jnp.arange(local_count, dtype=jnp.int32) + 1).astype(
        jnp.float32
    )
    row_global = lat_place * tile_rows + jnp.arange(tile_rows, dtype=jnp.int32)
    rotation = rotation_of(row_global, total_rows)
    linear_part = linear_residual(
        extended, tile_rows, tile_cols, angular_local[:, None, None], rotation[:, None]
    )
    later = lax.optimization_barrier((payloads[1], linear_part))
    linear_part = later[1]
    shape_piece = (groups, pieces, piece_rows, tile_cols)
    linear_part = linear_part.reshape(3, local_coefs, *shape_piece)
    wet_piece = wet_cells.reshape(shape_piece)
    rotation_piece = rotation.reshape(groups, pieces, piece_rows, 1)
    backs = exchange_friction(sent[0], later[0], drag_band, table, tile_cols)
    results = []
    for piece in range(pieces):
        back = backs[piece]
        friction = back[:, :, :piece_cells].reshape(groups, 2, local_coefs, piece_rows, tile_cols)
        friction = jnp.moveaxis(friction, 0, 2)
        drag_rate = back[:, :, piece_cells:].reshape(groups, piece_rows, tile_cols)
        linear_piece = linear_part[:, :, :, piece]
        residual = (
            linear_piece + jnp.concatenate([jnp.zeros_like(friction[:1]), friction], axis=0)
        ) * wet_piece[:, piece]
        results.append(
            precondition(
                residual,
                angular_local[:, None, None, None],
                rotation_piece[:, piece],
                drag_rate,
            )
        )
    return jnp.stack(results, axis=3).reshape(3, local_coefs, tile_rows, tile_cols)


def solution(mesh):
    placed = (
        P(None, "freq", "lat", "lon"),
        P(None, "freq", "lat", "lon"),
        P("lat", "lon"),
        P("lat", "lon"),
        P("lat", "lon"),
    )
    return jax.shard_map(
        local, mesh=mesh, in_specs=placed, out_specs=P(None, "freq", "lat", "lon"), check_vma=False
    )
```

```python
import functools
import math

import jax
import jax.numpy as jnp
from jax import lax
from jax.experimental import pallas as pl
from jax.experimental.pallas import tpu as pltpu
from jax.sharding import PartitionSpec as P

NCON = 16
NTIME = 256


LINEAR_DRAG = 0.5
GRAVITY = 1.0
OMEGA_STEP = 0.25
SPEED_SOFT = 0.01


def extended_2(block, sides, width):
    for axis, dim in sides:
        count = lax.axis_size(axis)
        forward = [(i, i + 1) for i in range(count - 1)]
        forward.append((count - 1, 0))
        backward = [(target, source) for source, target in forward]
        low = lax.ppermute(
            lax.slice_in_dim(block, block.shape[dim] - width, None, axis=dim), axis, forward
        )
        high = lax.ppermute(lax.slice_in_dim(block, 0, width, axis=dim), axis, backward)
        block = jnp.concatenate([low, block, high], axis=dim)
    return block


def samples_table(sample_count, constituents):
    sample_index = jnp.arange(sample_count, dtype=jnp.int32)
    harmonic = jnp.arange(1, constituents + 1, dtype=jnp.int32)
    wrapped_turns = sample_index[:, None] * harmonic[None, :] % sample_count
    phase_angle = wrapped_turns.astype(jnp.float32) * (2.0 * math.pi / sample_count)
    table = jnp.stack([jnp.cos(phase_angle), jnp.sin(phase_angle)], axis=2)
    return table.reshape(sample_count, 2 * constituents)


def rotation_of(row_index, total_rows):
    return 0.5 + (row_index.astype(jnp.float32) + 0.5) / total_rows


def tendency(values, angular):
    cos_sin = values.reshape((values.shape[0] // 2, 2) + values.shape[1:])
    moved = jnp.stack([angular * cos_sin[:, 1], -angular * cos_sin[:, 0]], axis=1)
    return moved.reshape(values.shape)


def linear_residual(extended, tile_rows, tile_cols, angular, rotation):

    def neighbour(plane, row_step, col_step):
        return extended[
            plane,
            :,
            1 + row_step : 1 + row_step + tile_rows,
            1 + col_step : 1 + col_step + tile_cols,
        ]

    height = neighbour(0, 0, 0)
    east = neighbour(1, 0, 0)
    north = neighbour(2, 0, 0)
    res_height = (
        tendency(height, angular)
        + neighbour(3, 0, 0)
        - neighbour(3, 0, -1)
        + neighbour(4, 0, 0)
        - neighbour(4, -1, 0)
    )
    north_mean = 0.25 * (north + neighbour(2, 0, 1) + neighbour(2, -1, 0) + neighbour(2, -1, 1))
    east_mean = 0.25 * (east + neighbour(1, 0, -1) + neighbour(1, 1, 0) + neighbour(1, 1, -1))
    res_east = (
        tendency(east, angular)
        + LINEAR_DRAG * east
        - rotation * north_mean
        + GRAVITY * (neighbour(0, 0, 1) - height)
    )
    res_north = (
        tendency(north, angular)
        + LINEAR_DRAG * north
        + rotation * east_mean
        + GRAVITY * (neighbour(0, 1, 0) - height)
    )
    return jnp.stack([res_height, res_east, res_north])


def friction_row(row_block, drag_row, table):
    highest = lax.Precision.HIGHEST
    series = jnp.einsum("tc,fcn->ftn", table, row_block, precision=highest)
    base_east, base_north, step_east, step_north = (series[0], series[1], series[2], series[3])
    magnitude = jnp.sqrt(base_east * base_east + base_north * base_north + SPEED_SOFT)
    projected = (base_east * step_east + base_north * step_north) / magnitude
    force_east = drag_row * (magnitude * step_east + base_east * projected)
    force_north = drag_row * (magnitude * step_north + base_north * projected)
    forces = jnp.stack([force_east, force_north])
    analysed = jnp.einsum("tc,ftn->fcn", table, forces, precision=highest) * (2.0 / table.shape[0])
    drag_rate = drag_row * jnp.mean(magnitude, axis=0)
    return (analysed, drag_rate)


def precondition(residual, angular, rotation, drag_rate):
    shaped = residual.reshape((3, residual.shape[1] // 2, 2) + residual.shape[2:])
    cos_part = shaped[:, :, 0]
    sin_part = shaped[:, :, 1]
    height_cos = -sin_part[0] / angular
    height_sin = cos_part[0] / angular
    real_rate = drag_rate + LINEAR_DRAG
    det_real = real_rate * real_rate - angular * angular + rotation * rotation
    det_imag = 2.0 * real_rate * angular
    det_norm = det_real * det_real + det_imag * det_imag
    inv_real = det_real / det_norm
    inv_imag = -det_imag / det_norm
    east_re = cos_part[1]
    east_im = -sin_part[1]
    north_re = cos_part[2]
    north_im = -sin_part[2]
    num_east_re = real_rate * east_re - angular * east_im + rotation * north_re
    num_east_im = real_rate * east_im + angular * east_re + rotation * north_im
    num_north_re = -rotation * east_re + real_rate * north_re - angular * north_im
    num_north_im = -rotation * east_im + real_rate * north_im + angular * north_re
    east_out_re = num_east_re * inv_real - num_east_im * inv_imag
    east_out_im = num_east_re * inv_imag + num_east_im * inv_real
    north_out_re = num_north_re * inv_real - num_north_im * inv_imag
    north_out_im = num_north_re * inv_imag + num_north_im * inv_real
    cosines = jnp.stack([height_cos, east_out_re, north_out_re])
    sines = jnp.stack([height_sin, -east_out_im, -north_out_im])
    return jnp.stack([cosines, sines], axis=2).reshape(residual.shape)


def split_three(values):
    high = values.astype(jnp.bfloat16)
    rest = values - high.astype(jnp.float32)
    middle = rest.astype(jnp.bfloat16)
    low = (rest - middle.astype(jnp.float32)).astype(jnp.bfloat16)
    return high, middle, low


def friction_kernel(
    groups, stacked_ref, table_t_ref, flows_ref, drag_ref, out_ref, rate_ref, gather_ref, parts_ref
):
    highest = lax.Precision.HIGHEST
    stacked = stacked_ref[...]
    coefs = gather_ref.shape[0]
    per = coefs // groups

    def synth(field):
        for source in range(groups):
            gather_ref[source * per : (source + 1) * per, :] = flows_ref[
                source, field * per : (field + 1) * per, :
            ]
        high, middle, low = split_three(gather_ref[...])
        for slot, part in enumerate((high, middle, high, low, high, middle)):
            parts_ref[slot * coefs : (slot + 1) * coefs, :] = part
        return jnp.dot(stacked, parts_ref[...], preferred_element_type=jnp.float32)

    base_east, base_north, step_east, step_north = synth(0), synth(1), synth(2), synth(3)
    drag_row = drag_ref[...]
    magnitude = jnp.sqrt(base_east * base_east + base_north * base_north + SPEED_SOFT)
    projected = (base_east * step_east + base_north * step_north) / magnitude
    force_east = drag_row * (magnitude * step_east + base_east * projected)
    force_north = drag_row * (magnitude * step_north + base_north * projected)
    table_t = table_t_ref[...]
    scale = 2.0 / stacked.shape[0]
    analysed_east = (
        jnp.dot(table_t, force_east, precision=highest, preferred_element_type=jnp.float32) * scale
    )
    analysed_north = (
        jnp.dot(table_t, force_north, precision=highest, preferred_element_type=jnp.float32)
        * scale
    )
    rate_ref[...] = drag_row * jnp.mean(magnitude, axis=0, keepdims=True)
    for group in range(groups):
        out_ref[group, 0:per, :] = analysed_east[group * per : (group + 1) * per]
        out_ref[group, per : 2 * per, :] = analysed_north[group * per : (group + 1) * per]


def friction_band(flows_band, drag_band, table, block):
    groups, rows_in, cells = flows_band.shape
    coefs = table.shape[1]
    per = coefs // groups
    table_t = jnp.transpose(table)
    high = lax.reduce_precision(table, exponent_bits=8, mantissa_bits=7)
    rest = table - high
    middle = lax.reduce_precision(rest, exponent_bits=8, mantissa_bits=7)
    low = lax.reduce_precision(rest - middle, exponent_bits=8, mantissa_bits=7)
    stacked = jnp.concatenate([high, middle, middle, high, low, high], axis=1)
    stacked = stacked.astype(jnp.bfloat16)
    steps = cells // block
    return pl.pallas_call(
        functools.partial(friction_kernel, groups),
        grid=(steps,),
        in_specs=[
            pl.BlockSpec(stacked.shape, lambda i: (0, 0)),
            pl.BlockSpec(table_t.shape, lambda i: (0, 0)),
            pl.BlockSpec((groups, rows_in, block), lambda i: (0, 0, i)),
            pl.BlockSpec((1, block), lambda i: (0, i)),
        ],
        out_specs=[
            pl.BlockSpec((groups, 2 * per, block), lambda i: (0, 0, i)),
            pl.BlockSpec((pl.Squeezed(), 1, block), lambda i: (i, 0, 0)),
        ],
        out_shape=[
            jax.ShapeDtypeStruct((groups, 2 * per, cells), jnp.float32),
            jax.ShapeDtypeStruct((steps, 1, block), jnp.float32),
        ],
        scratch_shapes=[
            pltpu.VMEM((coefs, block), jnp.float32),
            pltpu.VMEM((6 * coefs, block), jnp.bfloat16),
        ],
        compiler_params=pltpu.CompilerParams(vmem_limit_bytes=48 * 1024 * 1024),
    )(stacked, table_t, flows_band, drag_band)


MESH = pl.DeviceIdType.MESH


def friction_block(groups, stacked, table_t, flows_ref, drag_row, offset, width, gather_ref, parts_ref):
    coefs = gather_ref.shape[0]
    per = coefs // groups
    cells = pl.ds(offset, width)

    def synth(field):
        for source in range(groups):
            gather_ref[source * per : (source + 1) * per, :] = flows_ref[
                source, field * per : (field + 1) * per, cells
            ]
        high, middle, low = split_three(gather_ref[...])
        for slot, part in enumerate((high, middle, high, low, high, middle)):
            parts_ref[slot * coefs : (slot + 1) * coefs, :] = part
        return jnp.dot(stacked, parts_ref[...], preferred_element_type=jnp.float32)

    highest = lax.Precision.HIGHEST
    base_east, base_north, step_east, step_north = synth(0), synth(1), synth(2), synth(3)
    magnitude = jnp.sqrt(base_east * base_east + base_north * base_north + SPEED_SOFT)
    projected = (base_east * step_east + base_north * step_north) / magnitude
    force_east = drag_row * (magnitude * step_east + base_east * projected)
    force_north = drag_row * (magnitude * step_north + base_north * projected)
    scale = 2.0 / stacked.shape[0]
    analysed_east = (
        jnp.dot(table_t, force_east, precision=highest, preferred_element_type=jnp.float32) * scale
    )
    analysed_north = (
        jnp.dot(table_t, force_north, precision=highest, preferred_element_type=jnp.float32)
        * scale
    )
    drag_rate = drag_row * jnp.mean(magnitude, axis=0, keepdims=True)
    return analysed_east, analysed_north, drag_rate


def exchange_kernel(
    groups,
    width,
    stacked_first_ref,
    stacked_ref,
    table_t_ref,
    first_ref,
    second_ref,
    drag_ref,
    back_first_ref,
    back_second_ref,
    arrived,
    results,
    landed,
    gather_ref,
    parts_ref,
    send_sems,
    recv_sems,
    local_sems,
):
    me = lax.axis_index("freq")
    lat = lax.axis_index("lat")
    lon = lax.axis_index("lon")
    cells = first_ref.shape[2]
    coefs = gather_ref.shape[0]
    per = coefs // groups
    blocks = cells // width

    barrier = pltpu.get_barrier_semaphore()
    for distance in range(1, groups):
        peer = lax.rem(me + distance, groups)
        pl.semaphore_signal(barrier, inc=1, device_id=(peer, lat, lon), device_id_type=MESH)
    pl.semaphore_wait(barrier, groups - 1)

    def exchange(phase, source_of, target_of):
        copies = []
        for distance in range(1, groups):
            peer = lax.rem(me + distance, groups)
            copy = pltpu.make_async_remote_copy(
                src_ref=source_of(peer),
                dst_ref=target_of(me),
                send_sem=send_sems.at[phase, distance],
                recv_sem=recv_sems.at[phase, distance],
                device_id=(peer, lat, lon),
                device_id_type=MESH,
            )
            copy.start()
            copies.append(copy)
        local = pltpu.make_async_copy(source_of(me), target_of(me), local_sems.at[phase])
        local.start()
        return copies, local

    def wait_arrivals(phase, source_of, target_of):
        for distance in range(1, groups):
            sender = lax.rem(me + groups - distance, groups)
            pltpu.make_async_remote_copy(
                src_ref=source_of(sender),
                dst_ref=target_of(sender),
                send_sem=send_sems.at[phase, distance],
                recv_sem=recv_sems.at[phase, distance],
                device_id=(sender, lat, lon),
                device_id_type=MESH,
            ).wait_recv()

    sending = [exchange(0, lambda g: second_ref.at[g], lambda g: arrived.at[g])]
    table_t = table_t_ref[...]

    def compute(piece, flows_ref, stacked_in):
        stacked = stacked_in[...]

        def block(index, carry):
            offset = pl.multiple_of(index * width, width)
            drag_row = drag_ref[piece, :, pl.ds(offset, width)]
            east, north, rate = friction_block(
                groups, stacked, table_t, flows_ref, drag_row, offset, width, gather_ref, parts_ref
            )
            for group in range(groups):
                results[piece, group, 0:per, pl.ds(offset, width)] = east[
                    group * per : (group + 1) * per
                ]
                results[piece, group, per : 2 * per, pl.ds(offset, width)] = north[
                    group * per : (group + 1) * per
                ]
                results[piece, group, pl.ds(index, 1), pl.ds(cells, width)] = rate
            return carry

        lax.fori_loop(0, blocks, block, 0)

    compute(0, first_ref, stacked_first_ref)
    sending.append(exchange(1, lambda g: results.at[0, g], lambda g: landed.at[0, g]))
    wait_arrivals(0, lambda g: second_ref.at[g], lambda g: arrived.at[g])
    sending[0][1].wait()
    compute(1, arrived, stacked_ref)
    sending.append(exchange(2, lambda g: results.at[1, g], lambda g: landed.at[1, g]))
    for copies, local in sending:
        for copy in copies:
            copy.wait_send()
    sending[1][1].wait()
    sending[2][1].wait()
    wait_arrivals(1, lambda g: results.at[0, g], lambda g: landed.at[0, g])
    wait_arrivals(2, lambda g: results.at[1, g], lambda g: landed.at[1, g])
    back_first_ref[...] = landed[0]
    back_second_ref[...] = landed[1]


def stack_table(table):
    high = lax.reduce_precision(table, exponent_bits=8, mantissa_bits=7)
    rest = table - high
    middle = lax.reduce_precision(rest, exponent_bits=8, mantissa_bits=7)
    low = lax.reduce_precision(rest - middle, exponent_bits=8, mantissa_bits=7)
    stacked = jnp.concatenate([high, middle, middle, high, low, high], axis=1)
    return stacked.astype(jnp.bfloat16)


def exchange_friction(first, second, drag_band, table, width):
    groups, rows_in, cells = first.shape
    coefs = table.shape[1]
    per = coefs // groups
    table_t = jnp.transpose(table)
    member = lax.axis_index("freq")
    senders = lax.rem(member + groups - jnp.arange(groups, dtype=jnp.int32), groups)
    order = (senders[:, None] * per + jnp.arange(per, dtype=jnp.int32)[None, :]).reshape(coefs)
    stacked_first = stack_table(jnp.take(table, order, axis=1))
    stacked = stack_table(table)
    returned = (groups, 2 * per, cells + cells // (2 * per))
    vmem = pl.BlockSpec(memory_space=pltpu.VMEM)
    return pl.pallas_call(
        functools.partial(exchange_kernel, groups, width),
        in_specs=[vmem] * 6,
        out_specs=[vmem, vmem],
        out_shape=[jax.ShapeDtypeStruct(returned, jnp.float32)] * 2,
        scratch_shapes=[
            pltpu.VMEM(first.shape, jnp.float32),
            pltpu.VMEM((2,) + returned, jnp.float32),
            pltpu.VMEM((2,) + returned, jnp.float32),
            pltpu.VMEM((coefs, width), jnp.float32),
            pltpu.VMEM((6 * coefs, width), jnp.bfloat16),
            pltpu.SemaphoreType.DMA((3, groups)),
            pltpu.SemaphoreType.DMA((3, groups)),
            pltpu.SemaphoreType.DMA((3,)),
        ],
        compiler_params=pltpu.CompilerParams(
            collective_id=0, has_side_effects=True, vmem_limit_bytes=60 * 1024 * 1024
        ),
    )(stacked_first, stacked, table_t, first, second, drag_band)


def local(direction, base_flow, water_depth, drag_factor, wet_mask, pieces=2):
    local_coefs = direction.shape[1]
    tile_rows = direction.shape[2]
    tile_cols = direction.shape[3]
    groups = lax.axis_size("freq")
    member = lax.axis_index("freq")
    band_rows = tile_rows // groups
    piece_rows = band_rows // pieces
    piece_cells = piece_rows * tile_cols
    lat_place = lax.axis_index("lat")
    lat_count = lax.axis_size("lat")
    total_rows = tile_rows * lat_count
    wet_cells = wet_mask.astype(jnp.float32)
    height = direction[0] * wet_cells
    east = direction[1] * wet_cells
    north = direction[2] * wet_cells
    flows = jnp.concatenate([base_flow, jnp.stack([east, north])], axis=0)
    flows = flows.reshape(4 * local_coefs, groups, pieces, piece_rows, tile_cols)
    table = samples_table(NTIME, NCON)
    band_start = member * band_rows
    drag_band = lax.dynamic_slice_in_dim(drag_factor, band_start, band_rows, 0)
    drag_band = drag_band.reshape(pieces, 1, piece_cells)
    payloads = [
        jnp.moveaxis(flows[:, :, piece], 1, 0).reshape(groups, 4 * local_coefs, piece_cells)
        for piece in range(pieces)
    ]
    by_distance = [lax.dynamic_index_in_dim(payloads[0], member, 0, keepdims=False)]
    for distance in range(1, groups):
        target = lax.rem(member + distance, groups)
        piece = lax.dynamic_index_in_dim(payloads[0], target, 0, keepdims=False)
        pairs = [(source, (source + distance) % groups) for source in range(groups)]
        by_distance.append(lax.ppermute(piece, "freq", pairs))
    sent = [jnp.stack(by_distance)]
    planes = jnp.stack([height, east, north, water_depth * east, water_depth * north])
    extended = extended_2(planes, (("lat", 2), ("lon", 3)), 1)
    rim_keep = jnp.ones((tile_rows + 2,), jnp.float32)
    rim_keep = rim_keep.at[0].set(jnp.where(lat_place == 0, 0.0, 1.0))
    rim_keep = rim_keep.at[tile_rows + 1].set(jnp.where(lat_place == lat_count - 1, 0.0, 1.0))
    extended = extended * rim_keep[:, None]
    local_count = local_coefs // 2
    first_con = member * local_count
    angular_local = OMEGA_STEP * (first_con + jnp.arange(local_count, dtype=jnp.int32) + 1).astype(
        jnp.float32
    )
    row_global = lat_place * tile_rows + jnp.arange(tile_rows, dtype=jnp.int32)
    rotation = rotation_of(row_global, total_rows)
    linear_part = linear_residual(
        extended, tile_rows, tile_cols, angular_local[:, None, None], rotation[:, None]
    )
    later = lax.optimization_barrier((payloads[1], linear_part))
    linear_part = later[1]
    shape_piece = (groups, pieces, piece_rows, tile_cols)
    linear_part = linear_part.reshape(3, local_coefs, *shape_piece)
    wet_piece = wet_cells.reshape(shape_piece)
    rotation_piece = rotation.reshape(groups, pieces, piece_rows, 1)
    backs = exchange_friction(sent[0], later[0], drag_band, table, tile_cols)
    results = []
    for piece in range(pieces):
        back = backs[piece]
        friction = back[:, :, :piece_cells].reshape(groups, 2, local_coefs, piece_rows, tile_cols)
        friction = jnp.moveaxis(friction, 0, 2)
        drag_rate = back[:, :, piece_cells:].reshape(groups, piece_rows, tile_cols)
        linear_piece = linear_part[:, :, :, piece]
        residual = (
            linear_piece + jnp.concatenate([jnp.zeros_like(friction[:1]), friction], axis=0)
        ) * wet_piece[:, piece]
        results.append(
            precondition(
                residual,
                angular_local[:, None, None, None],
                rotation_piece[:, piece],
                drag_rate,
            )
        )
    return jnp.stack(results, axis=3).reshape(3, local_coefs, tile_rows, tile_cols)


def solution(mesh):
    placed = (
        P(None, "freq", "lat", "lon"),
        P(None, "freq", "lat", "lon"),
        P("lat", "lon"),
        P("lat", "lon"),
        P("lat", "lon"),
    )
    return jax.shard_map(
        local, mesh=mesh, in_specs=placed, out_specs=P(None, "freq", "lat", "lon"), check_vma=False
    )
```

```python
import functools
import math

import jax
import jax.numpy as jnp
from jax import lax
from jax.experimental import pallas as pl
from jax.experimental.pallas import tpu as pltpu
from jax.sharding import PartitionSpec as P

NCON = 16
NTIME = 256


LINEAR_DRAG = 0.5
GRAVITY = 1.0
OMEGA_STEP = 0.25
SPEED_SOFT = 0.01


def extended_2(block, sides, width):
    for axis, dim in sides:
        count = lax.axis_size(axis)
        forward = [(i, i + 1) for i in range(count - 1)]
        forward.append((count - 1, 0))
        backward = [(target, source) for source, target in forward]
        low = lax.ppermute(
            lax.slice_in_dim(block, block.shape[dim] - width, None, axis=dim), axis, forward
        )
        high = lax.ppermute(lax.slice_in_dim(block, 0, width, axis=dim), axis, backward)
        block = jnp.concatenate([low, block, high], axis=dim)
    return block


def samples_table(sample_count, constituents):
    sample_index = jnp.arange(sample_count, dtype=jnp.int32)
    harmonic = jnp.arange(1, constituents + 1, dtype=jnp.int32)
    wrapped_turns = sample_index[:, None] * harmonic[None, :] % sample_count
    phase_angle = wrapped_turns.astype(jnp.float32) * (2.0 * math.pi / sample_count)
    table = jnp.stack([jnp.cos(phase_angle), jnp.sin(phase_angle)], axis=2)
    return table.reshape(sample_count, 2 * constituents)


def rotation_of(row_index, total_rows):
    return 0.5 + (row_index.astype(jnp.float32) + 0.5) / total_rows


def tendency(values, angular):
    cos_sin = values.reshape((values.shape[0] // 2, 2) + values.shape[1:])
    moved = jnp.stack([angular * cos_sin[:, 1], -angular * cos_sin[:, 0]], axis=1)
    return moved.reshape(values.shape)


def linear_residual(extended, tile_rows, tile_cols, angular, rotation):

    def neighbour(plane, row_step, col_step):
        return extended[
            plane,
            :,
            1 + row_step : 1 + row_step + tile_rows,
            1 + col_step : 1 + col_step + tile_cols,
        ]

    height = neighbour(0, 0, 0)
    east = neighbour(1, 0, 0)
    north = neighbour(2, 0, 0)
    res_height = (
        tendency(height, angular)
        + neighbour(3, 0, 0)
        - neighbour(3, 0, -1)
        + neighbour(4, 0, 0)
        - neighbour(4, -1, 0)
    )
    north_mean = 0.25 * (north + neighbour(2, 0, 1) + neighbour(2, -1, 0) + neighbour(2, -1, 1))
    east_mean = 0.25 * (east + neighbour(1, 0, -1) + neighbour(1, 1, 0) + neighbour(1, 1, -1))
    res_east = (
        tendency(east, angular)
        + LINEAR_DRAG * east
        - rotation * north_mean
        + GRAVITY * (neighbour(0, 0, 1) - height)
    )
    res_north = (
        tendency(north, angular)
        + LINEAR_DRAG * north
        + rotation * east_mean
        + GRAVITY * (neighbour(0, 1, 0) - height)
    )
    return jnp.stack([res_height, res_east, res_north])


def friction_row(row_block, drag_row, table):
    highest = lax.Precision.HIGHEST
    series = jnp.einsum("tc,fcn->ftn", table, row_block, precision=highest)
    base_east, base_north, step_east, step_north = (series[0], series[1], series[2], series[3])
    magnitude = jnp.sqrt(base_east * base_east + base_north * base_north + SPEED_SOFT)
    projected = (base_east * step_east + base_north * step_north) / magnitude
    force_east = drag_row * (magnitude * step_east + base_east * projected)
    force_north = drag_row * (magnitude * step_north + base_north * projected)
    forces = jnp.stack([force_east, force_north])
    analysed = jnp.einsum("tc,ftn->fcn", table, forces, precision=highest) * (2.0 / table.shape[0])
    drag_rate = drag_row * jnp.mean(magnitude, axis=0)
    return (analysed, drag_rate)


def height_result(residual_height, angular):
    shaped = residual_height.reshape((residual_height.shape[0] // 2, 2) + residual_height.shape[1:])
    cos_part = shaped[:, 0]
    sin_part = shaped[:, 1]
    moved = jnp.stack([-sin_part / angular, cos_part / angular], axis=1)
    return moved.reshape(residual_height.shape)


def precondition(residual, angular, rotation, drag_rate):
    shaped = residual.reshape((3, residual.shape[1] // 2, 2) + residual.shape[2:])
    cos_part = shaped[:, :, 0]
    sin_part = shaped[:, :, 1]
    height_cos = -sin_part[0] / angular
    height_sin = cos_part[0] / angular
    real_rate = drag_rate + LINEAR_DRAG
    det_real = real_rate * real_rate - angular * angular + rotation * rotation
    det_imag = 2.0 * real_rate * angular
    det_norm = det_real * det_real + det_imag * det_imag
    inv_real = det_real / det_norm
    inv_imag = -det_imag / det_norm
    east_re = cos_part[1]
    east_im = -sin_part[1]
    north_re = cos_part[2]
    north_im = -sin_part[2]
    num_east_re = real_rate * east_re - angular * east_im + rotation * north_re
    num_east_im = real_rate * east_im + angular * east_re + rotation * north_im
    num_north_re = -rotation * east_re + real_rate * north_re - angular * north_im
    num_north_im = -rotation * east_im + real_rate * north_im + angular * north_re
    east_out_re = num_east_re * inv_real - num_east_im * inv_imag
    east_out_im = num_east_re * inv_imag + num_east_im * inv_real
    north_out_re = num_north_re * inv_real - num_north_im * inv_imag
    north_out_im = num_north_re * inv_imag + num_north_im * inv_real
    cosines = jnp.stack([height_cos, east_out_re, north_out_re])
    sines = jnp.stack([height_sin, -east_out_im, -north_out_im])
    return jnp.stack([cosines, sines], axis=2).reshape(residual.shape)


def split_three(values):
    high = values.astype(jnp.bfloat16)
    rest = values - high.astype(jnp.float32)
    middle = rest.astype(jnp.bfloat16)
    low = (rest - middle.astype(jnp.float32)).astype(jnp.bfloat16)
    return high, middle, low


def friction_kernel(
    groups, stacked_ref, table_t_ref, flows_ref, drag_ref, out_ref, rate_ref, gather_ref, parts_ref
):
    highest = lax.Precision.HIGHEST
    stacked = stacked_ref[...]
    coefs = gather_ref.shape[0]
    per = coefs // groups

    def synth(field):
        for source in range(groups):
            gather_ref[source * per : (source + 1) * per, :] = flows_ref[
                source, field * per : (field + 1) * per, :
            ]
        high, middle, low = split_three(gather_ref[...])
        for slot, part in enumerate((high, middle, high, low, high, middle)):
            parts_ref[slot * coefs : (slot + 1) * coefs, :] = part
        return jnp.dot(stacked, parts_ref[...], preferred_element_type=jnp.float32)

    base_east, base_north, step_east, step_north = synth(0), synth(1), synth(2), synth(3)
    drag_row = drag_ref[...]
    magnitude = jnp.sqrt(base_east * base_east + base_north * base_north + SPEED_SOFT)
    projected = (base_east * step_east + base_north * step_north) / magnitude
    force_east = drag_row * (magnitude * step_east + base_east * projected)
    force_north = drag_row * (magnitude * step_north + base_north * projected)
    table_t = table_t_ref[...]
    scale = 2.0 / stacked.shape[0]
    analysed_east = (
        jnp.dot(table_t, force_east, precision=highest, preferred_element_type=jnp.float32) * scale
    )
    analysed_north = (
        jnp.dot(table_t, force_north, precision=highest, preferred_element_type=jnp.float32)
        * scale
    )
    rate_ref[...] = drag_row * jnp.mean(magnitude, axis=0, keepdims=True)
    for group in range(groups):
        out_ref[group, 0:per, :] = analysed_east[group * per : (group + 1) * per]
        out_ref[group, per : 2 * per, :] = analysed_north[group * per : (group + 1) * per]


def friction_band(flows_band, drag_band, table, block):
    groups, rows_in, cells = flows_band.shape
    coefs = table.shape[1]
    per = coefs // groups
    table_t = jnp.transpose(table)
    high = lax.reduce_precision(table, exponent_bits=8, mantissa_bits=7)
    rest = table - high
    middle = lax.reduce_precision(rest, exponent_bits=8, mantissa_bits=7)
    low = lax.reduce_precision(rest - middle, exponent_bits=8, mantissa_bits=7)
    stacked = jnp.concatenate([high, middle, middle, high, low, high], axis=1)
    stacked = stacked.astype(jnp.bfloat16)
    steps = cells // block
    return pl.pallas_call(
        functools.partial(friction_kernel, groups),
        grid=(steps,),
        in_specs=[
            pl.BlockSpec(stacked.shape, lambda i: (0, 0)),
            pl.BlockSpec(table_t.shape, lambda i: (0, 0)),
            pl.BlockSpec((groups, rows_in, block), lambda i: (0, 0, i)),
            pl.BlockSpec((1, block), lambda i: (0, i)),
        ],
        out_specs=[
            pl.BlockSpec((groups, 2 * per, block), lambda i: (0, 0, i)),
            pl.BlockSpec((pl.Squeezed(), 1, block), lambda i: (i, 0, 0)),
        ],
        out_shape=[
            jax.ShapeDtypeStruct((groups, 2 * per, cells), jnp.float32),
            jax.ShapeDtypeStruct((steps, 1, block), jnp.float32),
        ],
        scratch_shapes=[
            pltpu.VMEM((coefs, block), jnp.float32),
            pltpu.VMEM((6 * coefs, block), jnp.bfloat16),
        ],
        compiler_params=pltpu.CompilerParams(vmem_limit_bytes=48 * 1024 * 1024),
    )(stacked, table_t, flows_band, drag_band)


MESH = pl.DeviceIdType.MESH


def friction_block(groups, stacked, table_t, flows_ref, drag_row, offset, width, gather_ref, parts_ref):
    coefs = gather_ref.shape[0]
    per = coefs // groups
    cells = pl.ds(offset, width)

    def synth(field):
        for source in range(groups):
            gather_ref[source * per : (source + 1) * per, :] = flows_ref[
                source, field * per : (field + 1) * per, cells
            ]
        high, middle, low = split_three(gather_ref[...])
        for slot, part in enumerate((high, middle, high, low, high, middle)):
            parts_ref[slot * coefs : (slot + 1) * coefs, :] = part
        return jnp.dot(stacked, parts_ref[...], preferred_element_type=jnp.float32)

    highest = lax.Precision.HIGHEST
    base_east, base_north, step_east, step_north = synth(0), synth(1), synth(2), synth(3)
    magnitude = jnp.sqrt(base_east * base_east + base_north * base_north + SPEED_SOFT)
    projected = (base_east * step_east + base_north * step_north) / magnitude
    force_east = drag_row * (magnitude * step_east + base_east * projected)
    force_north = drag_row * (magnitude * step_north + base_north * projected)
    scale = 2.0 / stacked.shape[0]
    analysed_east = (
        jnp.dot(table_t, force_east, precision=highest, preferred_element_type=jnp.float32) * scale
    )
    analysed_north = (
        jnp.dot(table_t, force_north, precision=highest, preferred_element_type=jnp.float32)
        * scale
    )
    drag_rate = drag_row * jnp.mean(magnitude, axis=0, keepdims=True)
    return analysed_east, analysed_north, drag_rate


def exchange_kernel(
    groups,
    width,
    stacked_ref,
    table_t_ref,
    first_ref,
    second_ref,
    drag_ref,
    back_first_ref,
    back_second_ref,
    arrived,
    results,
    landed,
    gather_ref,
    parts_ref,
    send_sems,
    recv_sems,
    local_sems,
):
    me = lax.axis_index("freq")
    lat = lax.axis_index("lat")
    lon = lax.axis_index("lon")
    cells = first_ref.shape[2]
    coefs = gather_ref.shape[0]
    per = coefs // groups
    blocks = cells // width

    barrier = pltpu.get_barrier_semaphore()
    for distance in range(1, groups):
        peer = lax.rem(me + distance, groups)
        pl.semaphore_signal(barrier, inc=1, device_id=(peer, lat, lon), device_id_type=MESH)
    pl.semaphore_wait(barrier, groups - 1)

    def exchange(phase, source_of, target_of):
        copies = []
        for distance in range(1, groups):
            peer = lax.rem(me + distance, groups)
            copy = pltpu.make_async_remote_copy(
                src_ref=source_of(peer),
                dst_ref=target_of(me),
                send_sem=send_sems.at[phase, distance],
                recv_sem=recv_sems.at[phase, distance],
                device_id=(peer, lat, lon),
                device_id_type=MESH,
            )
            copy.start()
            copies.append(copy)
        local = pltpu.make_async_copy(source_of(me), target_of(me), local_sems.at[phase])
        local.start()
        return copies, local

    def wait_arrivals(phase, source_of, target_of):
        for distance in range(1, groups):
            sender = lax.rem(me + groups - distance, groups)
            pltpu.make_async_remote_copy(
                src_ref=source_of(sender),
                dst_ref=target_of(sender),
                send_sem=send_sems.at[phase, distance],
                recv_sem=recv_sems.at[phase, distance],
                device_id=(sender, lat, lon),
                device_id_type=MESH,
            ).wait_recv()

    sending = [exchange(0, lambda g: second_ref.at[g], lambda g: arrived.at[g])]
    stacked = stacked_ref[...]
    table_t = table_t_ref[...]

    def compute(piece, flows_ref):
        def block(index, carry):
            offset = pl.multiple_of(index * width, width)
            drag_row = drag_ref[piece, :, pl.ds(offset, width)]
            east, north, rate = friction_block(
                groups, stacked, table_t, flows_ref, drag_row, offset, width, gather_ref, parts_ref
            )
            for group in range(groups):
                results[piece, group, 0:per, pl.ds(offset, width)] = east[
                    group * per : (group + 1) * per
                ]
                results[piece, group, per : 2 * per, pl.ds(offset, width)] = north[
                    group * per : (group + 1) * per
                ]
                results[piece, group, pl.ds(index, 1), pl.ds(cells, width)] = rate
            return carry

        lax.fori_loop(0, blocks, block, 0)

    compute(0, first_ref)
    sending.append(exchange(1, lambda g: results.at[0, g], lambda g: landed.at[0, g]))
    wait_arrivals(0, lambda g: second_ref.at[g], lambda g: arrived.at[g])
    sending[0][1].wait()
    compute(1, arrived)
    sending.append(exchange(2, lambda g: results.at[1, g], lambda g: landed.at[1, g]))
    for copies, local in sending:
        for copy in copies:
            copy.wait_send()
    sending[1][1].wait()
    sending[2][1].wait()
    wait_arrivals(1, lambda g: results.at[0, g], lambda g: landed.at[0, g])
    wait_arrivals(2, lambda g: results.at[1, g], lambda g: landed.at[1, g])
    back_first_ref[...] = landed[0]
    back_second_ref[...] = landed[1]


def exchange_friction(first, second, drag_band, table, width):
    groups, rows_in, cells = first.shape
    coefs = table.shape[1]
    per = coefs // groups
    table_t = jnp.transpose(table)
    high = lax.reduce_precision(table, exponent_bits=8, mantissa_bits=7)
    rest = table - high
    middle = lax.reduce_precision(rest, exponent_bits=8, mantissa_bits=7)
    low = lax.reduce_precision(rest - middle, exponent_bits=8, mantissa_bits=7)
    stacked = jnp.concatenate([high, middle, middle, high, low, high], axis=1)
    stacked = stacked.astype(jnp.bfloat16)
    returned = (groups, 2 * per, cells + cells // (2 * per))
    vmem = pl.BlockSpec(memory_space=pltpu.VMEM)
    return pl.pallas_call(
        functools.partial(exchange_kernel, groups, width),
        in_specs=[vmem] * 5,
        out_specs=[vmem, vmem],
        out_shape=[jax.ShapeDtypeStruct(returned, jnp.float32)] * 2,
        scratch_shapes=[
            pltpu.VMEM(first.shape, jnp.float32),
            pltpu.VMEM((2,) + returned, jnp.float32),
            pltpu.VMEM((2,) + returned, jnp.float32),
            pltpu.VMEM((coefs, width), jnp.float32),
            pltpu.VMEM((6 * coefs, width), jnp.bfloat16),
            pltpu.SemaphoreType.DMA((3, groups)),
            pltpu.SemaphoreType.DMA((3, groups)),
            pltpu.SemaphoreType.DMA((3,)),
        ],
        compiler_params=pltpu.CompilerParams(
            collective_id=0, has_side_effects=True, vmem_limit_bytes=60 * 1024 * 1024
        ),
    )(stacked, table_t, first, second, drag_band)


def local(direction, base_flow, water_depth, drag_factor, wet_mask, pieces=2):
    local_coefs = direction.shape[1]
    tile_rows = direction.shape[2]
    tile_cols = direction.shape[3]
    groups = lax.axis_size("freq")
    member = lax.axis_index("freq")
    band_rows = tile_rows // groups
    piece_rows = band_rows // pieces
    piece_cells = piece_rows * tile_cols
    lat_place = lax.axis_index("lat")
    lat_count = lax.axis_size("lat")
    total_rows = tile_rows * lat_count
    wet_cells = wet_mask.astype(jnp.float32)
    height = direction[0] * wet_cells
    east = direction[1] * wet_cells
    north = direction[2] * wet_cells
    flows = jnp.concatenate([base_flow, jnp.stack([east, north])], axis=0)
    flows = flows.reshape(4 * local_coefs, groups, pieces, piece_rows, tile_cols)
    table = samples_table(NTIME, NCON)
    band_start = member * band_rows
    drag_band = lax.dynamic_slice_in_dim(drag_factor, band_start, band_rows, 0)
    drag_band = drag_band.reshape(pieces, 1, piece_cells)
    payloads = [
        jnp.moveaxis(flows[:, :, piece], 1, 0).reshape(groups, 4 * local_coefs, piece_cells)
        for piece in range(pieces)
    ]
    sent = [lax.all_to_all(payloads[0], "freq", split_axis=0, concat_axis=0, tiled=True)]
    planes = jnp.stack([height, east, north, water_depth * east, water_depth * north])
    extended = extended_2(planes, (("lat", 2), ("lon", 3)), 1)
    rim_keep = jnp.ones((tile_rows + 2,), jnp.float32)
    rim_keep = rim_keep.at[0].set(jnp.where(lat_place == 0, 0.0, 1.0))
    rim_keep = rim_keep.at[tile_rows + 1].set(jnp.where(lat_place == lat_count - 1, 0.0, 1.0))
    extended = extended * rim_keep[:, None]
    local_count = local_coefs // 2
    first_con = member * local_count
    angular_local = OMEGA_STEP * (first_con + jnp.arange(local_count, dtype=jnp.int32) + 1).astype(
        jnp.float32
    )
    row_global = lat_place * tile_rows + jnp.arange(tile_rows, dtype=jnp.int32)
    rotation = rotation_of(row_global, total_rows)
    linear_part = linear_residual(
        extended, tile_rows, tile_cols, angular_local[:, None, None], rotation[:, None]
    )
    height_out = height_result(linear_part[0] * wet_cells, angular_local[:, None, None])
    later = lax.optimization_barrier((payloads[1], linear_part, height_out))
    linear_part = later[1]
    height_out = later[2]
    shape_piece = (groups, pieces, piece_rows, tile_cols)
    linear_part = linear_part.reshape(3, local_coefs, *shape_piece)
    wet_piece = wet_cells.reshape(shape_piece)
    rotation_piece = rotation.reshape(groups, pieces, piece_rows, 1)
    backs = exchange_friction(sent[0], later[0], drag_band, table, tile_cols)
    results = []
    for piece in range(pieces):
        back = backs[piece]
        friction = back[:, :, :piece_cells].reshape(groups, 2, local_coefs, piece_rows, tile_cols)
        friction = jnp.moveaxis(friction, 0, 2)
        drag_rate = back[:, :, piece_cells:].reshape(groups, piece_rows, tile_cols)
        linear_piece = linear_part[:, :, :, piece]
        residual = (
            linear_piece + jnp.concatenate([jnp.zeros_like(friction[:1]), friction], axis=0)
        ) * wet_piece[:, piece]
        results.append(
            precondition(
                residual,
                angular_local[:, None, None, None],
                rotation_piece[:, piece],
                drag_rate,
            )[1:]
        )
    moving = jnp.stack(results, axis=3).reshape(2, local_coefs, tile_rows, tile_cols)
    return jnp.concatenate([height_out[None], moving], axis=0)


def solution(mesh):
    placed = (
        P(None, "freq", "lat", "lon"),
        P(None, "freq", "lat", "lon"),
        P("lat", "lon"),
        P("lat", "lon"),
        P("lat", "lon"),
    )
    return jax.shard_map(
        local, mesh=mesh, in_specs=placed, out_specs=P(None, "freq", "lat", "lon"), check_vma=False
    )
```

```python
import functools
import math

import jax
import jax.numpy as jnp
from jax import lax
from jax.experimental import pallas as pl
from jax.experimental.pallas import tpu as pltpu
from jax.sharding import PartitionSpec as P

NCON = 16
NTIME = 256


LINEAR_DRAG = 0.5
GRAVITY = 1.0
OMEGA_STEP = 0.25
SPEED_SOFT = 0.01


def extended_2(block, sides, width):
    for axis, dim in sides:
        count = lax.axis_size(axis)
        forward = [(i, i + 1) for i in range(count - 1)]
        forward.append((count - 1, 0))
        backward = [(target, source) for source, target in forward]
        low = lax.ppermute(
            lax.slice_in_dim(block, block.shape[dim] - width, None, axis=dim), axis, forward
        )
        high = lax.ppermute(lax.slice_in_dim(block, 0, width, axis=dim), axis, backward)
        block = jnp.concatenate([low, block, high], axis=dim)
    return block


def samples_table(sample_count, constituents):
    sample_index = jnp.arange(sample_count, dtype=jnp.int32)
    harmonic = jnp.arange(1, constituents + 1, dtype=jnp.int32)
    wrapped_turns = sample_index[:, None] * harmonic[None, :] % sample_count
    phase_angle = wrapped_turns.astype(jnp.float32) * (2.0 * math.pi / sample_count)
    table = jnp.stack([jnp.cos(phase_angle), jnp.sin(phase_angle)], axis=2)
    return table.reshape(sample_count, 2 * constituents)


def rotation_of(row_index, total_rows):
    return 0.5 + (row_index.astype(jnp.float32) + 0.5) / total_rows


def tendency(values, angular):
    cos_sin = values.reshape((values.shape[0] // 2, 2) + values.shape[1:])
    moved = jnp.stack([angular * cos_sin[:, 1], -angular * cos_sin[:, 0]], axis=1)
    return moved.reshape(values.shape)


def linear_residual(extended, tile_rows, tile_cols, angular, rotation):

    def neighbour(plane, row_step, col_step):
        return extended[
            plane,
            :,
            1 + row_step : 1 + row_step + tile_rows,
            1 + col_step : 1 + col_step + tile_cols,
        ]

    height = neighbour(0, 0, 0)
    east = neighbour(1, 0, 0)
    north = neighbour(2, 0, 0)
    res_height = (
        tendency(height, angular)
        + neighbour(3, 0, 0)
        - neighbour(3, 0, -1)
        + neighbour(4, 0, 0)
        - neighbour(4, -1, 0)
    )
    north_mean = 0.25 * (north + neighbour(2, 0, 1) + neighbour(2, -1, 0) + neighbour(2, -1, 1))
    east_mean = 0.25 * (east + neighbour(1, 0, -1) + neighbour(1, 1, 0) + neighbour(1, 1, -1))
    res_east = (
        tendency(east, angular)
        + LINEAR_DRAG * east
        - rotation * north_mean
        + GRAVITY * (neighbour(0, 0, 1) - height)
    )
    res_north = (
        tendency(north, angular)
        + LINEAR_DRAG * north
        + rotation * east_mean
        + GRAVITY * (neighbour(0, 1, 0) - height)
    )
    return jnp.stack([res_height, res_east, res_north])


def friction_row(row_block, drag_row, table):
    highest = lax.Precision.HIGHEST
    series = jnp.einsum("tc,fcn->ftn", table, row_block, precision=highest)
    base_east, base_north, step_east, step_north = (series[0], series[1], series[2], series[3])
    magnitude = jnp.sqrt(base_east * base_east + base_north * base_north + SPEED_SOFT)
    projected = (base_east * step_east + base_north * step_north) / magnitude
    force_east = drag_row * (magnitude * step_east + base_east * projected)
    force_north = drag_row * (magnitude * step_north + base_north * projected)
    forces = jnp.stack([force_east, force_north])
    analysed = jnp.einsum("tc,ftn->fcn", table, forces, precision=highest) * (2.0 / table.shape[0])
    drag_rate = drag_row * jnp.mean(magnitude, axis=0)
    return (analysed, drag_rate)


def precondition(residual, angular, rotation, drag_rate):
    shaped = residual.reshape((3, residual.shape[1] // 2, 2) + residual.shape[2:])
    cos_part = shaped[:, :, 0]
    sin_part = shaped[:, :, 1]
    height_cos = -sin_part[0] / angular
    height_sin = cos_part[0] / angular
    real_rate = drag_rate + LINEAR_DRAG
    det_real = real_rate * real_rate - angular * angular + rotation * rotation
    det_imag = 2.0 * real_rate * angular
    det_norm = det_real * det_real + det_imag * det_imag
    inv_real = det_real / det_norm
    inv_imag = -det_imag / det_norm
    east_re = cos_part[1]
    east_im = -sin_part[1]
    north_re = cos_part[2]
    north_im = -sin_part[2]
    num_east_re = real_rate * east_re - angular * east_im + rotation * north_re
    num_east_im = real_rate * east_im + angular * east_re + rotation * north_im
    num_north_re = -rotation * east_re + real_rate * north_re - angular * north_im
    num_north_im = -rotation * east_im + real_rate * north_im + angular * north_re
    east_out_re = num_east_re * inv_real - num_east_im * inv_imag
    east_out_im = num_east_re * inv_imag + num_east_im * inv_real
    north_out_re = num_north_re * inv_real - num_north_im * inv_imag
    north_out_im = num_north_re * inv_imag + num_north_im * inv_real
    cosines = jnp.stack([height_cos, east_out_re, north_out_re])
    sines = jnp.stack([height_sin, -east_out_im, -north_out_im])
    return jnp.stack([cosines, sines], axis=2).reshape(residual.shape)


def split_three(values):
    high = values.astype(jnp.bfloat16)
    rest = values - high.astype(jnp.float32)
    middle = rest.astype(jnp.bfloat16)
    low = (rest - middle.astype(jnp.float32)).astype(jnp.bfloat16)
    return high, middle, low


def friction_kernel(
    groups, stacked_ref, table_t_ref, flows_ref, drag_ref, out_ref, rate_ref, gather_ref, parts_ref
):
    highest = lax.Precision.HIGHEST
    stacked = stacked_ref[...]
    coefs = gather_ref.shape[0]
    per = coefs // groups

    def synth(field):
        for source in range(groups):
            gather_ref[source * per : (source + 1) * per, :] = flows_ref[
                source, field * per : (field + 1) * per, :
            ]
        high, middle, low = split_three(gather_ref[...])
        for slot, part in enumerate((high, middle, high, low, high, middle)):
            parts_ref[slot * coefs : (slot + 1) * coefs, :] = part
        return jnp.dot(stacked, parts_ref[...], preferred_element_type=jnp.float32)

    base_east, base_north, step_east, step_north = synth(0), synth(1), synth(2), synth(3)
    drag_row = drag_ref[...]
    magnitude = jnp.sqrt(base_east * base_east + base_north * base_north + SPEED_SOFT)
    projected = (base_east * step_east + base_north * step_north) / magnitude
    force_east = drag_row * (magnitude * step_east + base_east * projected)
    force_north = drag_row * (magnitude * step_north + base_north * projected)
    table_t = table_t_ref[...]
    scale = 2.0 / stacked.shape[0]
    analysed_east = (
        jnp.dot(table_t, force_east, precision=highest, preferred_element_type=jnp.float32) * scale
    )
    analysed_north = (
        jnp.dot(table_t, force_north, precision=highest, preferred_element_type=jnp.float32)
        * scale
    )
    rate_ref[...] = drag_row * jnp.mean(magnitude, axis=0, keepdims=True)
    for group in range(groups):
        out_ref[group, 0:per, :] = analysed_east[group * per : (group + 1) * per]
        out_ref[group, per : 2 * per, :] = analysed_north[group * per : (group + 1) * per]


def friction_band(flows_band, drag_band, table, block):
    groups, rows_in, cells = flows_band.shape
    coefs = table.shape[1]
    per = coefs // groups
    table_t = jnp.transpose(table)
    high = lax.reduce_precision(table, exponent_bits=8, mantissa_bits=7)
    rest = table - high
    middle = lax.reduce_precision(rest, exponent_bits=8, mantissa_bits=7)
    low = lax.reduce_precision(rest - middle, exponent_bits=8, mantissa_bits=7)
    stacked = jnp.concatenate([high, middle, middle, high, low, high], axis=1)
    stacked = stacked.astype(jnp.bfloat16)
    steps = cells // block
    return pl.pallas_call(
        functools.partial(friction_kernel, groups),
        grid=(steps,),
        in_specs=[
            pl.BlockSpec(stacked.shape, lambda i: (0, 0)),
            pl.BlockSpec(table_t.shape, lambda i: (0, 0)),
            pl.BlockSpec((groups, rows_in, block), lambda i: (0, 0, i)),
            pl.BlockSpec((1, block), lambda i: (0, i)),
        ],
        out_specs=[
            pl.BlockSpec((groups, 2 * per, block), lambda i: (0, 0, i)),
            pl.BlockSpec((pl.Squeezed(), 1, block), lambda i: (i, 0, 0)),
        ],
        out_shape=[
            jax.ShapeDtypeStruct((groups, 2 * per, cells), jnp.float32),
            jax.ShapeDtypeStruct((steps, 1, block), jnp.float32),
        ],
        scratch_shapes=[
            pltpu.VMEM((coefs, block), jnp.float32),
            pltpu.VMEM((6 * coefs, block), jnp.bfloat16),
        ],
        compiler_params=pltpu.CompilerParams(vmem_limit_bytes=48 * 1024 * 1024),
    )(stacked, table_t, flows_band, drag_band)


MESH = pl.DeviceIdType.MESH


def friction_block(groups, stacked, table_t, flows_ref, drag_row, offset, width, gather_ref, parts_ref):
    coefs = gather_ref.shape[0]
    per = coefs // groups
    cells = pl.ds(offset, width)

    def synth(field):
        for source in range(groups):
            gather_ref[source * per : (source + 1) * per, :] = flows_ref[
                source, field * per : (field + 1) * per, cells
            ]
        high, middle, low = split_three(gather_ref[...])
        for slot, part in enumerate((high, middle, high, low, high, middle)):
            parts_ref[slot * coefs : (slot + 1) * coefs, :] = part
        return jnp.dot(stacked, parts_ref[...], preferred_element_type=jnp.float32)

    highest = lax.Precision.HIGHEST
    base_east, base_north, step_east, step_north = synth(0), synth(1), synth(2), synth(3)
    magnitude = jnp.sqrt(base_east * base_east + base_north * base_north + SPEED_SOFT)
    projected = (base_east * step_east + base_north * step_north) / magnitude
    force_east = drag_row * (magnitude * step_east + base_east * projected)
    force_north = drag_row * (magnitude * step_north + base_north * projected)
    scale = 2.0 / stacked.shape[0]
    analysed_east = (
        jnp.dot(table_t, force_east, precision=highest, preferred_element_type=jnp.float32) * scale
    )
    analysed_north = (
        jnp.dot(table_t, force_north, precision=highest, preferred_element_type=jnp.float32)
        * scale
    )
    drag_rate = drag_row * jnp.mean(magnitude, axis=0, keepdims=True)
    return analysed_east, analysed_north, drag_rate


def exchange_kernel(
    groups,
    width,
    stacked_ref,
    table_t_ref,
    first_ref,
    second_ref,
    drag_ref,
    friction_first_ref,
    friction_second_ref,
    rate_first_ref,
    rate_second_ref,
    arrived,
    results,
    landed,
    gather_ref,
    parts_ref,
    send_sems,
    recv_sems,
    local_sems,
):
    me = lax.axis_index("freq")
    lat = lax.axis_index("lat")
    lon = lax.axis_index("lon")
    cells = first_ref.shape[2]
    coefs = gather_ref.shape[0]
    per = coefs // groups
    blocks = cells // width

    barrier = pltpu.get_barrier_semaphore()
    for distance in range(1, groups):
        peer = lax.rem(me + distance, groups)
        pl.semaphore_signal(barrier, inc=1, device_id=(peer, lat, lon), device_id_type=MESH)
    pl.semaphore_wait(barrier, groups - 1)

    def exchange(phase, source_of, target_of):
        copies = []
        for distance in range(1, groups):
            peer = lax.rem(me + distance, groups)
            copy = pltpu.make_async_remote_copy(
                src_ref=source_of(peer),
                dst_ref=target_of(me),
                send_sem=send_sems.at[phase, distance],
                recv_sem=recv_sems.at[phase, distance],
                device_id=(peer, lat, lon),
                device_id_type=MESH,
            )
            copy.start()
            copies.append(copy)
        local = pltpu.make_async_copy(source_of(me), target_of(me), local_sems.at[phase])
        local.start()
        return copies, local

    def wait_arrivals(phase, source_of, target_of):
        for distance in range(1, groups):
            sender = lax.rem(me + groups - distance, groups)
            pltpu.make_async_remote_copy(
                src_ref=source_of(sender),
                dst_ref=target_of(sender),
                send_sem=send_sems.at[phase, distance],
                recv_sem=recv_sems.at[phase, distance],
                device_id=(sender, lat, lon),
                device_id_type=MESH,
            ).wait_recv()

    sending = [exchange(0, lambda g: second_ref.at[g], lambda g: arrived.at[g])]
    stacked = stacked_ref[...]
    table_t = table_t_ref[...]

    def compute(piece, flows_ref):
        def block(index, carry):
            offset = pl.multiple_of(index * width, width)
            drag_row = drag_ref[piece, :, pl.ds(offset, width)]
            east, north, rate = friction_block(
                groups, stacked, table_t, flows_ref, drag_row, offset, width, gather_ref, parts_ref
            )
            for group in range(groups):
                results[piece, group, 0:per, pl.ds(offset, width)] = east[
                    group * per : (group + 1) * per
                ]
                results[piece, group, per : 2 * per, pl.ds(offset, width)] = north[
                    group * per : (group + 1) * per
                ]
                results[piece, group, pl.ds(index, 1), pl.ds(cells, width)] = rate
            return carry

        lax.fori_loop(0, blocks, block, 0)

    compute(0, first_ref)
    sending.append(exchange(1, lambda g: results.at[0, g], lambda g: landed.at[0, g]))
    wait_arrivals(0, lambda g: second_ref.at[g], lambda g: arrived.at[g])
    sending[0][1].wait()
    compute(1, arrived)
    sending.append(exchange(2, lambda g: results.at[1, g], lambda g: landed.at[1, g]))
    for copies, local in sending:
        for copy in copies:
            copy.wait_send()
    sending[1][1].wait()
    sending[2][1].wait()
    wait_arrivals(1, lambda g: results.at[0, g], lambda g: landed.at[0, g])
    wait_arrivals(2, lambda g: results.at[1, g], lambda g: landed.at[1, g])
    friction_first_ref[...] = landed[0, :, :, 0:cells]
    friction_second_ref[...] = landed[1, :, :, 0:cells]
    rate_first_ref[...] = landed[0, :, :, cells:]
    rate_second_ref[...] = landed[1, :, :, cells:]


def exchange_friction(first, second, drag_band, table, width):
    groups, rows_in, cells = first.shape
    coefs = table.shape[1]
    per = coefs // groups
    table_t = jnp.transpose(table)
    high = lax.reduce_precision(table, exponent_bits=8, mantissa_bits=7)
    rest = table - high
    middle = lax.reduce_precision(rest, exponent_bits=8, mantissa_bits=7)
    low = lax.reduce_precision(rest - middle, exponent_bits=8, mantissa_bits=7)
    stacked = jnp.concatenate([high, middle, middle, high, low, high], axis=1)
    stacked = stacked.astype(jnp.bfloat16)
    returned = (groups, 2 * per, cells + cells // (2 * per))
    vmem = pl.BlockSpec(memory_space=pltpu.VMEM)
    return pl.pallas_call(
        functools.partial(exchange_kernel, groups, width),
        in_specs=[vmem] * 5,
        out_specs=[vmem] * 4,
        out_shape=[jax.ShapeDtypeStruct((groups, 2 * per, cells), jnp.float32)] * 2
        + [jax.ShapeDtypeStruct((groups, 2 * per, cells // (2 * per)), jnp.float32)] * 2,
        scratch_shapes=[
            pltpu.VMEM(first.shape, jnp.float32),
            pltpu.VMEM((2,) + returned, jnp.float32),
            pltpu.VMEM((2,) + returned, jnp.float32),
            pltpu.VMEM((coefs, width), jnp.float32),
            pltpu.VMEM((6 * coefs, width), jnp.bfloat16),
            pltpu.SemaphoreType.DMA((3, groups)),
            pltpu.SemaphoreType.DMA((3, groups)),
            pltpu.SemaphoreType.DMA((3,)),
        ],
        compiler_params=pltpu.CompilerParams(
            collective_id=0, has_side_effects=True, vmem_limit_bytes=60 * 1024 * 1024
        ),
    )(stacked, table_t, first, second, drag_band)


def local(direction, base_flow, water_depth, drag_factor, wet_mask, pieces=2):
    local_coefs = direction.shape[1]
    tile_rows = direction.shape[2]
    tile_cols = direction.shape[3]
    groups = lax.axis_size("freq")
    member = lax.axis_index("freq")
    band_rows = tile_rows // groups
    piece_rows = band_rows // pieces
    piece_cells = piece_rows * tile_cols
    lat_place = lax.axis_index("lat")
    lat_count = lax.axis_size("lat")
    total_rows = tile_rows * lat_count
    wet_cells = wet_mask.astype(jnp.float32)
    height = direction[0] * wet_cells
    east = direction[1] * wet_cells
    north = direction[2] * wet_cells
    flows = jnp.concatenate([base_flow, jnp.stack([east, north])], axis=0)
    flows = flows.reshape(4 * local_coefs, groups, pieces, piece_rows, tile_cols)
    table = samples_table(NTIME, NCON)
    band_start = member * band_rows
    drag_band = lax.dynamic_slice_in_dim(drag_factor, band_start, band_rows, 0)
    drag_band = drag_band.reshape(pieces, 1, piece_cells)
    payloads = [
        jnp.moveaxis(flows[:, :, piece], 1, 0).reshape(groups, 4 * local_coefs, piece_cells)
        for piece in range(pieces)
    ]
    sent = [lax.all_to_all(payloads[0], "freq", split_axis=0, concat_axis=0, tiled=True)]
    planes = jnp.stack([height, east, north, water_depth * east, water_depth * north])
    extended = extended_2(planes, (("lat", 2), ("lon", 3)), 1)
    rim_keep = jnp.ones((tile_rows + 2,), jnp.float32)
    rim_keep = rim_keep.at[0].set(jnp.where(lat_place == 0, 0.0, 1.0))
    rim_keep = rim_keep.at[tile_rows + 1].set(jnp.where(lat_place == lat_count - 1, 0.0, 1.0))
    extended = extended * rim_keep[:, None]
    local_count = local_coefs // 2
    first_con = member * local_count
    angular_local = OMEGA_STEP * (first_con + jnp.arange(local_count, dtype=jnp.int32) + 1).astype(
        jnp.float32
    )
    row_global = lat_place * tile_rows + jnp.arange(tile_rows, dtype=jnp.int32)
    rotation = rotation_of(row_global, total_rows)
    linear_part = linear_residual(
        extended, tile_rows, tile_cols, angular_local[:, None, None], rotation[:, None]
    )
    later = lax.optimization_barrier((payloads[1], linear_part))
    linear_part = later[1]
    shape_piece = (groups, pieces, piece_rows, tile_cols)
    linear_part = linear_part.reshape(3, local_coefs, *shape_piece)
    wet_piece = wet_cells.reshape(shape_piece)
    rotation_piece = rotation.reshape(groups, pieces, piece_rows, 1)
    backs = exchange_friction(sent[0], later[0], drag_band, table, tile_cols)
    results = []
    for piece in range(pieces):
        friction = backs[piece].reshape(groups, 2, local_coefs, piece_rows, tile_cols)
        friction = jnp.moveaxis(friction, 0, 2)
        drag_rate = backs[pieces + piece].reshape(groups, piece_rows, tile_cols)
        linear_piece = linear_part[:, :, :, piece]
        residual = (
            linear_piece + jnp.concatenate([jnp.zeros_like(friction[:1]), friction], axis=0)
        ) * wet_piece[:, piece]
        results.append(
            precondition(
                residual,
                angular_local[:, None, None, None],
                rotation_piece[:, piece],
                drag_rate,
            )
        )
    return jnp.stack(results, axis=3).reshape(3, local_coefs, tile_rows, tile_cols)


def solution(mesh):
    placed = (
        P(None, "freq", "lat", "lon"),
        P(None, "freq", "lat", "lon"),
        P("lat", "lon"),
        P("lat", "lon"),
        P("lat", "lon"),
    )
    return jax.shard_map(
        local, mesh=mesh, in_specs=placed, out_specs=P(None, "freq", "lat", "lon"), check_vma=False
    )
```

```python
import functools
import math

import jax
import jax.numpy as jnp
from jax import lax
from jax.experimental import pallas as pl
from jax.experimental.pallas import tpu as pltpu
from jax.sharding import PartitionSpec as P

NCON = 16
NTIME = 256


LINEAR_DRAG = 0.5
GRAVITY = 1.0
OMEGA_STEP = 0.25
SPEED_SOFT = 0.01


def extended_2(block, sides, width):
    for axis, dim in sides:
        count = lax.axis_size(axis)
        forward = [(i, i + 1) for i in range(count - 1)]
        forward.append((count - 1, 0))
        backward = [(target, source) for source, target in forward]
        sent = 128 if dim == block.ndim - 1 else width
        low = lax.ppermute(
            lax.slice_in_dim(block, block.shape[dim] - sent, None, axis=dim), axis, forward
        )
        high = lax.ppermute(lax.slice_in_dim(block, 0, sent, axis=dim), axis, backward)
        low = lax.slice_in_dim(low, sent - width, None, axis=dim)
        high = lax.slice_in_dim(high, 0, width, axis=dim)
        block = jnp.concatenate([low, block, high], axis=dim)
    return block


def samples_table(sample_count, constituents):
    sample_index = jnp.arange(sample_count, dtype=jnp.int32)
    harmonic = jnp.arange(1, constituents + 1, dtype=jnp.int32)
    wrapped_turns = sample_index[:, None] * harmonic[None, :] % sample_count
    phase_angle = wrapped_turns.astype(jnp.float32) * (2.0 * math.pi / sample_count)
    table = jnp.stack([jnp.cos(phase_angle), jnp.sin(phase_angle)], axis=2)
    return table.reshape(sample_count, 2 * constituents)


def rotation_of(row_index, total_rows):
    return 0.5 + (row_index.astype(jnp.float32) + 0.5) / total_rows


def tendency(values, angular):
    cos_sin = values.reshape((values.shape[0] // 2, 2) + values.shape[1:])
    moved = jnp.stack([angular * cos_sin[:, 1], -angular * cos_sin[:, 0]], axis=1)
    return moved.reshape(values.shape)


def linear_residual(extended, tile_rows, tile_cols, angular, rotation):

    def neighbour(plane, row_step, col_step):
        return extended[
            plane,
            :,
            1 + row_step : 1 + row_step + tile_rows,
            1 + col_step : 1 + col_step + tile_cols,
        ]

    height = neighbour(0, 0, 0)
    east = neighbour(1, 0, 0)
    north = neighbour(2, 0, 0)
    res_height = (
        tendency(height, angular)
        + neighbour(3, 0, 0)
        - neighbour(3, 0, -1)
        + neighbour(4, 0, 0)
        - neighbour(4, -1, 0)
    )
    north_mean = 0.25 * (north + neighbour(2, 0, 1) + neighbour(2, -1, 0) + neighbour(2, -1, 1))
    east_mean = 0.25 * (east + neighbour(1, 0, -1) + neighbour(1, 1, 0) + neighbour(1, 1, -1))
    res_east = (
        tendency(east, angular)
        + LINEAR_DRAG * east
        - rotation * north_mean
        + GRAVITY * (neighbour(0, 0, 1) - height)
    )
    res_north = (
        tendency(north, angular)
        + LINEAR_DRAG * north
        + rotation * east_mean
        + GRAVITY * (neighbour(0, 1, 0) - height)
    )
    return jnp.stack([res_height, res_east, res_north])


def friction_row(row_block, drag_row, table):
    highest = lax.Precision.HIGHEST
    series = jnp.einsum("tc,fcn->ftn", table, row_block, precision=highest)
    base_east, base_north, step_east, step_north = (series[0], series[1], series[2], series[3])
    magnitude = jnp.sqrt(base_east * base_east + base_north * base_north + SPEED_SOFT)
    projected = (base_east * step_east + base_north * step_north) / magnitude
    force_east = drag_row * (magnitude * step_east + base_east * projected)
    force_north = drag_row * (magnitude * step_north + base_north * projected)
    forces = jnp.stack([force_east, force_north])
    analysed = jnp.einsum("tc,ftn->fcn", table, forces, precision=highest) * (2.0 / table.shape[0])
    drag_rate = drag_row * jnp.mean(magnitude, axis=0)
    return (analysed, drag_rate)


def precondition(residual, angular, rotation, drag_rate):
    shaped = residual.reshape((3, residual.shape[1] // 2, 2) + residual.shape[2:])
    cos_part = shaped[:, :, 0]
    sin_part = shaped[:, :, 1]
    height_cos = -sin_part[0] / angular
    height_sin = cos_part[0] / angular
    real_rate = drag_rate + LINEAR_DRAG
    det_real = real_rate * real_rate - angular * angular + rotation * rotation
    det_imag = 2.0 * real_rate * angular
    det_norm = det_real * det_real + det_imag * det_imag
    inv_real = det_real / det_norm
    inv_imag = -det_imag / det_norm
    east_re = cos_part[1]
    east_im = -sin_part[1]
    north_re = cos_part[2]
    north_im = -sin_part[2]
    num_east_re = real_rate * east_re - angular * east_im + rotation * north_re
    num_east_im = real_rate * east_im + angular * east_re + rotation * north_im
    num_north_re = -rotation * east_re + real_rate * north_re - angular * north_im
    num_north_im = -rotation * east_im + real_rate * north_im + angular * north_re
    east_out_re = num_east_re * inv_real - num_east_im * inv_imag
    east_out_im = num_east_re * inv_imag + num_east_im * inv_real
    north_out_re = num_north_re * inv_real - num_north_im * inv_imag
    north_out_im = num_north_re * inv_imag + num_north_im * inv_real
    cosines = jnp.stack([height_cos, east_out_re, north_out_re])
    sines = jnp.stack([height_sin, -east_out_im, -north_out_im])
    return jnp.stack([cosines, sines], axis=2).reshape(residual.shape)


def split_three(values):
    high = values.astype(jnp.bfloat16)
    rest = values - high.astype(jnp.float32)
    middle = rest.astype(jnp.bfloat16)
    low = (rest - middle.astype(jnp.float32)).astype(jnp.bfloat16)
    return high, middle, low


def friction_kernel(
    groups, stacked_ref, table_t_ref, flows_ref, drag_ref, out_ref, rate_ref, gather_ref, parts_ref
):
    highest = lax.Precision.HIGHEST
    stacked = stacked_ref[...]
    coefs = gather_ref.shape[0]
    per = coefs // groups

    def synth(field):
        for source in range(groups):
            gather_ref[source * per : (source + 1) * per, :] = flows_ref[
                source, field * per : (field + 1) * per, :
            ]
        high, middle, low = split_three(gather_ref[...])
        for slot, part in enumerate((high, middle, high, low, high, middle)):
            parts_ref[slot * coefs : (slot + 1) * coefs, :] = part
        return jnp.dot(stacked, parts_ref[...], preferred_element_type=jnp.float32)

    base_east, base_north, step_east, step_north = synth(0), synth(1), synth(2), synth(3)
    drag_row = drag_ref[...]
    magnitude = jnp.sqrt(base_east * base_east + base_north * base_north + SPEED_SOFT)
    projected = (base_east * step_east + base_north * step_north) / magnitude
    force_east = drag_row * (magnitude * step_east + base_east * projected)
    force_north = drag_row * (magnitude * step_north + base_north * projected)
    table_t = table_t_ref[...]
    scale = 2.0 / stacked.shape[0]
    analysed_east = (
        jnp.dot(table_t, force_east, precision=highest, preferred_element_type=jnp.float32) * scale
    )
    analysed_north = (
        jnp.dot(table_t, force_north, precision=highest, preferred_element_type=jnp.float32)
        * scale
    )
    rate_ref[...] = drag_row * jnp.mean(magnitude, axis=0, keepdims=True)
    for group in range(groups):
        out_ref[group, 0:per, :] = analysed_east[group * per : (group + 1) * per]
        out_ref[group, per : 2 * per, :] = analysed_north[group * per : (group + 1) * per]


def friction_band(flows_band, drag_band, table, block):
    groups, rows_in, cells = flows_band.shape
    coefs = table.shape[1]
    per = coefs // groups
    table_t = jnp.transpose(table)
    high = lax.reduce_precision(table, exponent_bits=8, mantissa_bits=7)
    rest = table - high
    middle = lax.reduce_precision(rest, exponent_bits=8, mantissa_bits=7)
    low = lax.reduce_precision(rest - middle, exponent_bits=8, mantissa_bits=7)
    stacked = jnp.concatenate([high, middle, middle, high, low, high], axis=1)
    stacked = stacked.astype(jnp.bfloat16)
    steps = cells // block
    return pl.pallas_call(
        functools.partial(friction_kernel, groups),
        grid=(steps,),
        in_specs=[
            pl.BlockSpec(stacked.shape, lambda i: (0, 0)),
            pl.BlockSpec(table_t.shape, lambda i: (0, 0)),
            pl.BlockSpec((groups, rows_in, block), lambda i: (0, 0, i)),
            pl.BlockSpec((1, block), lambda i: (0, i)),
        ],
        out_specs=[
            pl.BlockSpec((groups, 2 * per, block), lambda i: (0, 0, i)),
            pl.BlockSpec((pl.Squeezed(), 1, block), lambda i: (i, 0, 0)),
        ],
        out_shape=[
            jax.ShapeDtypeStruct((groups, 2 * per, cells), jnp.float32),
            jax.ShapeDtypeStruct((steps, 1, block), jnp.float32),
        ],
        scratch_shapes=[
            pltpu.VMEM((coefs, block), jnp.float32),
            pltpu.VMEM((6 * coefs, block), jnp.bfloat16),
        ],
        compiler_params=pltpu.CompilerParams(vmem_limit_bytes=48 * 1024 * 1024),
    )(stacked, table_t, flows_band, drag_band)


MESH = pl.DeviceIdType.MESH


def friction_block(groups, stacked, table_t, flows_ref, drag_row, offset, width, gather_ref, parts_ref):
    coefs = gather_ref.shape[0]
    per = coefs // groups
    cells = pl.ds(offset, width)

    def synth(field):
        for source in range(groups):
            gather_ref[source * per : (source + 1) * per, :] = flows_ref[
                source, field * per : (field + 1) * per, cells
            ]
        high, middle, low = split_three(gather_ref[...])
        for slot, part in enumerate((high, middle, high, low, high, middle)):
            parts_ref[slot * coefs : (slot + 1) * coefs, :] = part
        return jnp.dot(stacked, parts_ref[...], preferred_element_type=jnp.float32)

    highest = lax.Precision.HIGHEST
    base_east, base_north, step_east, step_north = synth(0), synth(1), synth(2), synth(3)
    magnitude = jnp.sqrt(base_east * base_east + base_north * base_north + SPEED_SOFT)
    projected = (base_east * step_east + base_north * step_north) / magnitude
    force_east = drag_row * (magnitude * step_east + base_east * projected)
    force_north = drag_row * (magnitude * step_north + base_north * projected)
    scale = 2.0 / stacked.shape[0]
    analysed_east = (
        jnp.dot(table_t, force_east, precision=highest, preferred_element_type=jnp.float32) * scale
    )
    analysed_north = (
        jnp.dot(table_t, force_north, precision=highest, preferred_element_type=jnp.float32)
        * scale
    )
    drag_rate = drag_row * jnp.mean(magnitude, axis=0, keepdims=True)
    return analysed_east, analysed_north, drag_rate


def exchange_kernel(
    groups,
    width,
    stacked_ref,
    table_t_ref,
    first_ref,
    second_ref,
    drag_ref,
    friction_first_ref,
    friction_second_ref,
    rate_first_ref,
    rate_second_ref,
    arrived,
    results,
    landed,
    gather_ref,
    parts_ref,
    send_sems,
    recv_sems,
    local_sems,
):
    me = lax.axis_index("freq")
    lat = lax.axis_index("lat")
    lon = lax.axis_index("lon")
    cells = first_ref.shape[2]
    coefs = gather_ref.shape[0]
    per = coefs // groups
    blocks = cells // width

    barrier = pltpu.get_barrier_semaphore()
    for distance in range(1, groups):
        peer = lax.rem(me + distance, groups)
        pl.semaphore_signal(barrier, inc=1, device_id=(peer, lat, lon), device_id_type=MESH)
    pl.semaphore_wait(barrier, groups - 1)

    def exchange(phase, source_of, target_of):
        copies = []
        for distance in range(1, groups):
            peer = lax.rem(me + distance, groups)
            copy = pltpu.make_async_remote_copy(
                src_ref=source_of(peer),
                dst_ref=target_of(me),
                send_sem=send_sems.at[phase, distance],
                recv_sem=recv_sems.at[phase, distance],
                device_id=(peer, lat, lon),
                device_id_type=MESH,
            )
            copy.start()
            copies.append(copy)
        local = pltpu.make_async_copy(source_of(me), target_of(me), local_sems.at[phase])
        local.start()
        return copies, local

    def wait_arrivals(phase, source_of, target_of):
        for distance in range(1, groups):
            sender = lax.rem(me + groups - distance, groups)
            pltpu.make_async_remote_copy(
                src_ref=source_of(sender),
                dst_ref=target_of(sender),
                send_sem=send_sems.at[phase, distance],
                recv_sem=recv_sems.at[phase, distance],
                device_id=(sender, lat, lon),
                device_id_type=MESH,
            ).wait_recv()

    sending = [exchange(0, lambda g: second_ref.at[g], lambda g: arrived.at[g])]
    stacked = stacked_ref[...]
    table_t = table_t_ref[...]

    def compute(piece, flows_ref):
        def block(index, carry):
            offset = pl.multiple_of(index * width, width)
            drag_row = drag_ref[piece, :, pl.ds(offset, width)]
            east, north, rate = friction_block(
                groups, stacked, table_t, flows_ref, drag_row, offset, width, gather_ref, parts_ref
            )
            for group in range(groups):
                results[piece, group, 0:per, pl.ds(offset, width)] = east[
                    group * per : (group + 1) * per
                ]
                results[piece, group, per : 2 * per, pl.ds(offset, width)] = north[
                    group * per : (group + 1) * per
                ]
                results[piece, group, pl.ds(index, 1), pl.ds(cells, width)] = rate
            return carry

        lax.fori_loop(0, blocks, block, 0)

    compute(0, first_ref)
    sending.append(exchange(1, lambda g: results.at[0, g], lambda g: landed.at[0, g]))
    wait_arrivals(0, lambda g: second_ref.at[g], lambda g: arrived.at[g])
    sending[0][1].wait()
    compute(1, arrived)
    sending.append(exchange(2, lambda g: results.at[1, g], lambda g: landed.at[1, g]))
    for copies, local in sending:
        for copy in copies:
            copy.wait_send()
    sending[1][1].wait()
    sending[2][1].wait()
    wait_arrivals(1, lambda g: results.at[0, g], lambda g: landed.at[0, g])
    wait_arrivals(2, lambda g: results.at[1, g], lambda g: landed.at[1, g])
    friction_first_ref[...] = landed[0, :, :, 0:cells]
    friction_second_ref[...] = landed[1, :, :, 0:cells]
    rate_first_ref[...] = landed[0, :, :, cells:]
    rate_second_ref[...] = landed[1, :, :, cells:]


def exchange_friction(first, second, drag_band, table, width):
    groups, rows_in, cells = first.shape
    coefs = table.shape[1]
    per = coefs // groups
    table_t = jnp.transpose(table)
    high = lax.reduce_precision(table, exponent_bits=8, mantissa_bits=7)
    rest = table - high
    middle = lax.reduce_precision(rest, exponent_bits=8, mantissa_bits=7)
    low = lax.reduce_precision(rest - middle, exponent_bits=8, mantissa_bits=7)
    stacked = jnp.concatenate([high, middle, middle, high, low, high], axis=1)
    stacked = stacked.astype(jnp.bfloat16)
    returned = (groups, 2 * per, cells + cells // (2 * per))
    vmem = pl.BlockSpec(memory_space=pltpu.VMEM)
    return pl.pallas_call(
        functools.partial(exchange_kernel, groups, width),
        in_specs=[vmem] * 5,
        out_specs=[vmem] * 4,
        out_shape=[jax.ShapeDtypeStruct((groups, 2 * per, cells), jnp.float32)] * 2
        + [jax.ShapeDtypeStruct((groups, 2 * per, cells // (2 * per)), jnp.float32)] * 2,
        scratch_shapes=[
            pltpu.VMEM(first.shape, jnp.float32),
            pltpu.VMEM((2,) + returned, jnp.float32),
            pltpu.VMEM((2,) + returned, jnp.float32),
            pltpu.VMEM((coefs, width), jnp.float32),
            pltpu.VMEM((6 * coefs, width), jnp.bfloat16),
            pltpu.SemaphoreType.DMA((3, groups)),
            pltpu.SemaphoreType.DMA((3, groups)),
            pltpu.SemaphoreType.DMA((3,)),
        ],
        compiler_params=pltpu.CompilerParams(
            collective_id=0, has_side_effects=True, vmem_limit_bytes=60 * 1024 * 1024
        ),
    )(stacked, table_t, first, second, drag_band)


def local(direction, base_flow, water_depth, drag_factor, wet_mask, pieces=2):
    local_coefs = direction.shape[1]
    tile_rows = direction.shape[2]
    tile_cols = direction.shape[3]
    groups = lax.axis_size("freq")
    member = lax.axis_index("freq")
    band_rows = tile_rows // groups
    piece_rows = band_rows // pieces
    piece_cells = piece_rows * tile_cols
    lat_place = lax.axis_index("lat")
    lat_count = lax.axis_size("lat")
    total_rows = tile_rows * lat_count
    wet_cells = wet_mask.astype(jnp.float32)
    height = direction[0] * wet_cells
    east = direction[1] * wet_cells
    north = direction[2] * wet_cells
    flows = jnp.concatenate([base_flow, jnp.stack([east, north])], axis=0)
    flows = flows.reshape(4 * local_coefs, groups, pieces, piece_rows, tile_cols)
    table = samples_table(NTIME, NCON)
    band_start = member * band_rows
    drag_band = lax.dynamic_slice_in_dim(drag_factor, band_start, band_rows, 0)
    drag_band = drag_band.reshape(pieces, 1, piece_cells)
    payloads = [
        jnp.moveaxis(flows[:, :, piece], 1, 0).reshape(groups, 4 * local_coefs, piece_cells)
        for piece in range(pieces)
    ]
    sent = [lax.all_to_all(payloads[0], "freq", split_axis=0, concat_axis=0, tiled=True)]
    planes = jnp.stack([height, east, north, water_depth * east, water_depth * north])
    extended = extended_2(planes, (("lat", 2), ("lon", 3)), 1)
    rim_keep = jnp.ones((tile_rows + 2,), jnp.float32)
    rim_keep = rim_keep.at[0].set(jnp.where(lat_place == 0, 0.0, 1.0))
    rim_keep = rim_keep.at[tile_rows + 1].set(jnp.where(lat_place == lat_count - 1, 0.0, 1.0))
    extended = extended * rim_keep[:, None]
    local_count = local_coefs // 2
    first_con = member * local_count
    angular_local = OMEGA_STEP * (first_con + jnp.arange(local_count, dtype=jnp.int32) + 1).astype(
        jnp.float32
    )
    row_global = lat_place * tile_rows + jnp.arange(tile_rows, dtype=jnp.int32)
    rotation = rotation_of(row_global, total_rows)
    linear_part = linear_residual(
        extended, tile_rows, tile_cols, angular_local[:, None, None], rotation[:, None]
    )
    later = lax.optimization_barrier((payloads[1], linear_part))
    linear_part = later[1]
    shape_piece = (groups, pieces, piece_rows, tile_cols)
    linear_part = linear_part.reshape(3, local_coefs, *shape_piece)
    wet_piece = wet_cells.reshape(shape_piece)
    rotation_piece = rotation.reshape(groups, pieces, piece_rows, 1)
    backs = exchange_friction(sent[0], later[0], drag_band, table, tile_cols)
    results = []
    for piece in range(pieces):
        friction = backs[piece].reshape(groups, 2, local_coefs, piece_rows, tile_cols)
        friction = jnp.moveaxis(friction, 0, 2)
        drag_rate = backs[pieces + piece].reshape(groups, piece_rows, tile_cols)
        linear_piece = linear_part[:, :, :, piece]
        residual = (
            linear_piece + jnp.concatenate([jnp.zeros_like(friction[:1]), friction], axis=0)
        ) * wet_piece[:, piece]
        results.append(
            precondition(
                residual,
                angular_local[:, None, None, None],
                rotation_piece[:, piece],
                drag_rate,
            )
        )
    return jnp.stack(results, axis=3).reshape(3, local_coefs, tile_rows, tile_cols)


def solution(mesh):
    placed = (
        P(None, "freq", "lat", "lon"),
        P(None, "freq", "lat", "lon"),
        P("lat", "lon"),
        P("lat", "lon"),
        P("lat", "lon"),
    )
    return jax.shard_map(
        local, mesh=mesh, in_specs=placed, out_specs=P(None, "freq", "lat", "lon"), check_vma=False
    )
```

```python
import functools
import math

import jax
import jax.numpy as jnp
from jax import lax
from jax.experimental import pallas as pl
from jax.experimental.pallas import tpu as pltpu
from jax.sharding import PartitionSpec as P

NCON = 16
NTIME = 256


LINEAR_DRAG = 0.5
GRAVITY = 1.0
OMEGA_STEP = 0.25
SPEED_SOFT = 0.01


def extended_2(block, sides, width):
    for axis, dim in sides:
        count = lax.axis_size(axis)
        forward = [(i, i + 1) for i in range(count - 1)]
        forward.append((count - 1, 0))
        backward = [(target, source) for source, target in forward]
        low = lax.ppermute(
            lax.slice_in_dim(block, block.shape[dim] - width, None, axis=dim), axis, forward
        )
        high = lax.ppermute(lax.slice_in_dim(block, 0, width, axis=dim), axis, backward)
        block = jnp.concatenate([low, block, high], axis=dim)
    return block


def samples_table(sample_count, constituents):
    sample_index = jnp.arange(sample_count, dtype=jnp.int32)
    harmonic = jnp.arange(1, constituents + 1, dtype=jnp.int32)
    wrapped_turns = sample_index[:, None] * harmonic[None, :] % sample_count
    phase_angle = wrapped_turns.astype(jnp.float32) * (2.0 * math.pi / sample_count)
    table = jnp.stack([jnp.cos(phase_angle), jnp.sin(phase_angle)], axis=2)
    return table.reshape(sample_count, 2 * constituents)


def rotation_of(row_index, total_rows):
    return 0.5 + (row_index.astype(jnp.float32) + 0.5) / total_rows


def tendency(values, angular):
    cos_sin = values.reshape((values.shape[0] // 2, 2) + values.shape[1:])
    moved = jnp.stack([angular * cos_sin[:, 1], -angular * cos_sin[:, 0]], axis=1)
    return moved.reshape(values.shape)


def linear_residual(extended, tile_rows, tile_cols, angular, rotation):

    def neighbour(plane, row_step, col_step):
        return extended[
            plane,
            :,
            1 + row_step : 1 + row_step + tile_rows,
            1 + col_step : 1 + col_step + tile_cols,
        ]

    height = neighbour(0, 0, 0)
    east = neighbour(1, 0, 0)
    north = neighbour(2, 0, 0)
    res_height = (
        tendency(height, angular)
        + neighbour(3, 0, 0)
        - neighbour(3, 0, -1)
        + neighbour(4, 0, 0)
        - neighbour(4, -1, 0)
    )
    north_mean = 0.25 * (north + neighbour(2, 0, 1) + neighbour(2, -1, 0) + neighbour(2, -1, 1))
    east_mean = 0.25 * (east + neighbour(1, 0, -1) + neighbour(1, 1, 0) + neighbour(1, 1, -1))
    res_east = (
        tendency(east, angular)
        + LINEAR_DRAG * east
        - rotation * north_mean
        + GRAVITY * (neighbour(0, 0, 1) - height)
    )
    res_north = (
        tendency(north, angular)
        + LINEAR_DRAG * north
        + rotation * east_mean
        + GRAVITY * (neighbour(0, 1, 0) - height)
    )
    return jnp.stack([res_height, res_east, res_north])


def friction_row(row_block, drag_row, table):
    highest = lax.Precision.HIGHEST
    series = jnp.einsum("tc,fcn->ftn", table, row_block, precision=highest)
    base_east, base_north, step_east, step_north = (series[0], series[1], series[2], series[3])
    magnitude = jnp.sqrt(base_east * base_east + base_north * base_north + SPEED_SOFT)
    projected = (base_east * step_east + base_north * step_north) / magnitude
    force_east = drag_row * (magnitude * step_east + base_east * projected)
    force_north = drag_row * (magnitude * step_north + base_north * projected)
    forces = jnp.stack([force_east, force_north])
    analysed = jnp.einsum("tc,ftn->fcn", table, forces, precision=highest) * (2.0 / table.shape[0])
    drag_rate = drag_row * jnp.mean(magnitude, axis=0)
    return (analysed, drag_rate)


def precondition(residual, angular, rotation, drag_rate):
    shaped = residual.reshape((3, residual.shape[1] // 2, 2) + residual.shape[2:])
    cos_part = shaped[:, :, 0]
    sin_part = shaped[:, :, 1]
    height_cos = -sin_part[0] / angular
    height_sin = cos_part[0] / angular
    real_rate = drag_rate + LINEAR_DRAG
    det_real = real_rate * real_rate - angular * angular + rotation * rotation
    det_imag = 2.0 * real_rate * angular
    det_norm = det_real * det_real + det_imag * det_imag
    inv_real = det_real / det_norm
    inv_imag = -det_imag / det_norm
    east_re = cos_part[1]
    east_im = -sin_part[1]
    north_re = cos_part[2]
    north_im = -sin_part[2]
    num_east_re = real_rate * east_re - angular * east_im + rotation * north_re
    num_east_im = real_rate * east_im + angular * east_re + rotation * north_im
    num_north_re = -rotation * east_re + real_rate * north_re - angular * north_im
    num_north_im = -rotation * east_im + real_rate * north_im + angular * north_re
    east_out_re = num_east_re * inv_real - num_east_im * inv_imag
    east_out_im = num_east_re * inv_imag + num_east_im * inv_real
    north_out_re = num_north_re * inv_real - num_north_im * inv_imag
    north_out_im = num_north_re * inv_imag + num_north_im * inv_real
    cosines = jnp.stack([height_cos, east_out_re, north_out_re])
    sines = jnp.stack([height_sin, -east_out_im, -north_out_im])
    return jnp.stack([cosines, sines], axis=2).reshape(residual.shape)


def split_three(values):
    high = values.astype(jnp.bfloat16)
    rest = values - high.astype(jnp.float32)
    middle = rest.astype(jnp.bfloat16)
    low = (rest - middle.astype(jnp.float32)).astype(jnp.bfloat16)
    return high, middle, low


def friction_kernel(
    groups, stacked_ref, table_t_ref, flows_ref, drag_ref, out_ref, rate_ref, gather_ref, parts_ref
):
    highest = lax.Precision.HIGHEST
    stacked = stacked_ref[...]
    coefs = gather_ref.shape[0]
    per = coefs // groups

    def synth(field):
        for source in range(groups):
            gather_ref[source * per : (source + 1) * per, :] = flows_ref[
                source, field * per : (field + 1) * per, :
            ]
        high, middle, low = split_three(gather_ref[...])
        for slot, part in enumerate((high, middle, high, low, high, middle)):
            parts_ref[slot * coefs : (slot + 1) * coefs, :] = part
        return jnp.dot(stacked, parts_ref[...], preferred_element_type=jnp.float32)

    base_east, base_north, step_east, step_north = synth(0), synth(1), synth(2), synth(3)
    drag_row = drag_ref[...]
    magnitude = jnp.sqrt(base_east * base_east + base_north * base_north + SPEED_SOFT)
    projected = (base_east * step_east + base_north * step_north) / magnitude
    force_east = drag_row * (magnitude * step_east + base_east * projected)
    force_north = drag_row * (magnitude * step_north + base_north * projected)
    table_t = table_t_ref[...]
    scale = 2.0 / stacked.shape[0]
    analysed_east = (
        jnp.dot(table_t, force_east, precision=highest, preferred_element_type=jnp.float32) * scale
    )
    analysed_north = (
        jnp.dot(table_t, force_north, precision=highest, preferred_element_type=jnp.float32)
        * scale
    )
    rate_ref[...] = drag_row * jnp.mean(magnitude, axis=0, keepdims=True)
    for group in range(groups):
        out_ref[group, 0:per, :] = analysed_east[group * per : (group + 1) * per]
        out_ref[group, per : 2 * per, :] = analysed_north[group * per : (group + 1) * per]


def friction_band(flows_band, drag_band, table, block):
    groups, rows_in, cells = flows_band.shape
    coefs = table.shape[1]
    per = coefs // groups
    table_t = jnp.transpose(table)
    high = lax.reduce_precision(table, exponent_bits=8, mantissa_bits=7)
    rest = table - high
    middle = lax.reduce_precision(rest, exponent_bits=8, mantissa_bits=7)
    low = lax.reduce_precision(rest - middle, exponent_bits=8, mantissa_bits=7)
    stacked = jnp.concatenate([high, middle, middle, high, low, high], axis=1)
    stacked = stacked.astype(jnp.bfloat16)
    steps = cells // block
    return pl.pallas_call(
        functools.partial(friction_kernel, groups),
        grid=(steps,),
        in_specs=[
            pl.BlockSpec(stacked.shape, lambda i: (0, 0)),
            pl.BlockSpec(table_t.shape, lambda i: (0, 0)),
            pl.BlockSpec((groups, rows_in, block), lambda i: (0, 0, i)),
            pl.BlockSpec((1, block), lambda i: (0, i)),
        ],
        out_specs=[
            pl.BlockSpec((groups, 2 * per, block), lambda i: (0, 0, i)),
            pl.BlockSpec((pl.Squeezed(), 1, block), lambda i: (i, 0, 0)),
        ],
        out_shape=[
            jax.ShapeDtypeStruct((groups, 2 * per, cells), jnp.float32),
            jax.ShapeDtypeStruct((steps, 1, block), jnp.float32),
        ],
        scratch_shapes=[
            pltpu.VMEM((coefs, block), jnp.float32),
            pltpu.VMEM((6 * coefs, block), jnp.bfloat16),
        ],
        compiler_params=pltpu.CompilerParams(vmem_limit_bytes=48 * 1024 * 1024),
    )(stacked, table_t, flows_band, drag_band)


MESH = pl.DeviceIdType.MESH


def friction_block(groups, stacked, table_t, flows_ref, drag_row, offset, width, gather_ref, parts_ref):
    coefs = gather_ref.shape[0]
    per = coefs // groups
    cells = pl.ds(offset, width)

    def synth(field):
        for source in range(groups):
            gather_ref[source * per : (source + 1) * per, :] = flows_ref[
                source, field * per : (field + 1) * per, cells
            ]
        high, middle, low = split_three(gather_ref[...])
        for slot, part in enumerate((high, middle, high, low, high, middle)):
            parts_ref[slot * coefs : (slot + 1) * coefs, :] = part
        return jnp.dot(stacked, parts_ref[...], preferred_element_type=jnp.float32)

    highest = lax.Precision.HIGHEST
    base_east, base_north, step_east, step_north = synth(0), synth(1), synth(2), synth(3)
    magnitude = jnp.sqrt(base_east * base_east + base_north * base_north + SPEED_SOFT)
    projected = (base_east * step_east + base_north * step_north) / magnitude
    force_east = drag_row * (magnitude * step_east + base_east * projected)
    force_north = drag_row * (magnitude * step_north + base_north * projected)
    scale = 2.0 / stacked.shape[0]
    analysed_east = (
        jnp.dot(table_t, force_east, precision=highest, preferred_element_type=jnp.float32) * scale
    )
    analysed_north = (
        jnp.dot(table_t, force_north, precision=highest, preferred_element_type=jnp.float32)
        * scale
    )
    drag_rate = drag_row * jnp.mean(magnitude, axis=0, keepdims=True)
    return analysed_east, analysed_north, drag_rate


def exchange_kernel(
    groups,
    width,
    stacked_ref,
    table_t_ref,
    first_ref,
    second_ref,
    drag_ref,
    friction_first_ref,
    friction_second_ref,
    rate_first_ref,
    rate_second_ref,
    arrived,
    results,
    landed,
    gather_ref,
    parts_ref,
    send_sems,
    recv_sems,
    local_sems,
):
    me = lax.axis_index("freq")
    lat = lax.axis_index("lat")
    lon = lax.axis_index("lon")
    cells = first_ref.shape[2]
    coefs = gather_ref.shape[0]
    per = coefs // groups
    blocks = cells // width

    barrier = pltpu.get_barrier_semaphore()
    for distance in range(1, groups):
        peer = lax.rem(me + distance, groups)
        pl.semaphore_signal(barrier, inc=1, device_id=(peer, lat, lon), device_id_type=MESH)
    pl.semaphore_wait(barrier, groups - 1)

    def exchange(phase, source_of, target_of):
        copies = []
        for distance in range(1, groups):
            peer = lax.rem(me + distance, groups)
            copy = pltpu.make_async_remote_copy(
                src_ref=source_of(peer),
                dst_ref=target_of(me),
                send_sem=send_sems.at[phase, distance],
                recv_sem=recv_sems.at[phase, distance],
                device_id=(peer, lat, lon),
                device_id_type=MESH,
            )
            copy.start()
            copies.append(copy)
        local = pltpu.make_async_copy(source_of(me), target_of(me), local_sems.at[phase])
        local.start()
        return copies, local

    def wait_arrivals(phase, source_of, target_of):
        for distance in range(1, groups):
            sender = lax.rem(me + groups - distance, groups)
            pltpu.make_async_remote_copy(
                src_ref=source_of(sender),
                dst_ref=target_of(sender),
                send_sem=send_sems.at[phase, distance],
                recv_sem=recv_sems.at[phase, distance],
                device_id=(sender, lat, lon),
                device_id_type=MESH,
            ).wait_recv()

    sending = [exchange(0, lambda g: second_ref.at[g], lambda g: arrived.at[g])]
    stacked = stacked_ref[...]
    table_t = table_t_ref[...]

    def compute(piece, flows_ref):
        def block(index, carry):
            offset = pl.multiple_of(index * width, width)
            drag_row = drag_ref[piece, :, pl.ds(offset, width)]
            east, north, rate = friction_block(
                groups, stacked, table_t, flows_ref, drag_row, offset, width, gather_ref, parts_ref
            )
            for group in range(groups):
                results[piece, group, 0:per, pl.ds(offset, width)] = east[
                    group * per : (group + 1) * per
                ]
                results[piece, group, per : 2 * per, pl.ds(offset, width)] = north[
                    group * per : (group + 1) * per
                ]
                results[piece, group, pl.ds(index, 1), pl.ds(cells, width)] = rate
            return carry

        lax.fori_loop(0, blocks, block, 0)

    compute(0, first_ref)
    wait_arrivals(0, lambda g: second_ref.at[g], lambda g: arrived.at[g])
    sending[0][1].wait()
    sending.append(exchange(1, lambda g: results.at[0, g], lambda g: landed.at[0, g]))
    compute(1, arrived)
    sending.append(exchange(2, lambda g: results.at[1, g], lambda g: landed.at[1, g]))
    for copies, local in sending:
        for copy in copies:
            copy.wait_send()
    sending[1][1].wait()
    sending[2][1].wait()
    wait_arrivals(1, lambda g: results.at[0, g], lambda g: landed.at[0, g])
    wait_arrivals(2, lambda g: results.at[1, g], lambda g: landed.at[1, g])
    friction_first_ref[...] = landed[0, :, :, 0:cells]
    friction_second_ref[...] = landed[1, :, :, 0:cells]
    rate_first_ref[...] = landed[0, :, :, cells:]
    rate_second_ref[...] = landed[1, :, :, cells:]


def exchange_friction(first, second, drag_band, table, width):
    groups, rows_in, cells = first.shape
    coefs = table.shape[1]
    per = coefs // groups
    table_t = jnp.transpose(table)
    high = lax.reduce_precision(table, exponent_bits=8, mantissa_bits=7)
    rest = table - high
    middle = lax.reduce_precision(rest, exponent_bits=8, mantissa_bits=7)
    low = lax.reduce_precision(rest - middle, exponent_bits=8, mantissa_bits=7)
    stacked = jnp.concatenate([high, middle, middle, high, low, high], axis=1)
    stacked = stacked.astype(jnp.bfloat16)
    returned = (groups, 2 * per, cells + cells // (2 * per))
    vmem = pl.BlockSpec(memory_space=pltpu.VMEM)
    return pl.pallas_call(
        functools.partial(exchange_kernel, groups, width),
        in_specs=[vmem] * 5,
        out_specs=[vmem] * 4,
        out_shape=[jax.ShapeDtypeStruct((groups, 2 * per, cells), jnp.float32)] * 2
        + [jax.ShapeDtypeStruct((groups, 2 * per, cells // (2 * per)), jnp.float32)] * 2,
        scratch_shapes=[
            pltpu.VMEM(first.shape, jnp.float32),
            pltpu.VMEM((2,) + returned, jnp.float32),
            pltpu.VMEM((2,) + returned, jnp.float32),
            pltpu.VMEM((coefs, width), jnp.float32),
            pltpu.VMEM((6 * coefs, width), jnp.bfloat16),
            pltpu.SemaphoreType.DMA((3, groups)),
            pltpu.SemaphoreType.DMA((3, groups)),
            pltpu.SemaphoreType.DMA((3,)),
        ],
        compiler_params=pltpu.CompilerParams(
            collective_id=0, has_side_effects=True, vmem_limit_bytes=60 * 1024 * 1024
        ),
    )(stacked, table_t, first, second, drag_band)


def local(direction, base_flow, water_depth, drag_factor, wet_mask, pieces=2):
    local_coefs = direction.shape[1]
    tile_rows = direction.shape[2]
    tile_cols = direction.shape[3]
    groups = lax.axis_size("freq")
    member = lax.axis_index("freq")
    band_rows = tile_rows // groups
    piece_rows = band_rows // pieces
    piece_cells = piece_rows * tile_cols
    lat_place = lax.axis_index("lat")
    lat_count = lax.axis_size("lat")
    total_rows = tile_rows * lat_count
    wet_cells = wet_mask.astype(jnp.float32)
    height = direction[0] * wet_cells
    east = direction[1] * wet_cells
    north = direction[2] * wet_cells
    flows = jnp.concatenate([base_flow, jnp.stack([east, north])], axis=0)
    flows = flows.reshape(4 * local_coefs, groups, pieces, piece_rows, tile_cols)
    table = samples_table(NTIME, NCON)
    band_start = member * band_rows
    drag_band = lax.dynamic_slice_in_dim(drag_factor, band_start, band_rows, 0)
    drag_band = drag_band.reshape(pieces, 1, piece_cells)
    payloads = [
        jnp.moveaxis(flows[:, :, piece], 1, 0).reshape(groups, 4 * local_coefs, piece_cells)
        for piece in range(pieces)
    ]
    sent = [lax.all_to_all(payloads[0], "freq", split_axis=0, concat_axis=0, tiled=True)]
    planes = jnp.stack([height, east, north, water_depth * east, water_depth * north])
    extended = extended_2(planes, (("lat", 2), ("lon", 3)), 1)
    rim_keep = jnp.ones((tile_rows + 2,), jnp.float32)
    rim_keep = rim_keep.at[0].set(jnp.where(lat_place == 0, 0.0, 1.0))
    rim_keep = rim_keep.at[tile_rows + 1].set(jnp.where(lat_place == lat_count - 1, 0.0, 1.0))
    extended = extended * rim_keep[:, None]
    local_count = local_coefs // 2
    first_con = member * local_count
    angular_local = OMEGA_STEP * (first_con + jnp.arange(local_count, dtype=jnp.int32) + 1).astype(
        jnp.float32
    )
    row_global = lat_place * tile_rows + jnp.arange(tile_rows, dtype=jnp.int32)
    rotation = rotation_of(row_global, total_rows)
    linear_part = linear_residual(
        extended, tile_rows, tile_cols, angular_local[:, None, None], rotation[:, None]
    )
    later = lax.optimization_barrier((payloads[1], linear_part))
    linear_part = later[1]
    shape_piece = (groups, pieces, piece_rows, tile_cols)
    linear_part = linear_part.reshape(3, local_coefs, *shape_piece)
    wet_piece = wet_cells.reshape(shape_piece)
    rotation_piece = rotation.reshape(groups, pieces, piece_rows, 1)
    backs = exchange_friction(sent[0], later[0], drag_band, table, tile_cols)
    results = []
    for piece in range(pieces):
        friction = backs[piece].reshape(groups, 2, local_coefs, piece_rows, tile_cols)
        friction = jnp.moveaxis(friction, 0, 2)
        drag_rate = backs[pieces + piece].reshape(groups, piece_rows, tile_cols)
        linear_piece = linear_part[:, :, :, piece]
        residual = (
            linear_piece + jnp.concatenate([jnp.zeros_like(friction[:1]), friction], axis=0)
        ) * wet_piece[:, piece]
        results.append(
            precondition(
                residual,
                angular_local[:, None, None, None],
                rotation_piece[:, piece],
                drag_rate,
            )
        )
    return jnp.stack(results, axis=3).reshape(3, local_coefs, tile_rows, tile_cols)


def solution(mesh):
    placed = (
        P(None, "freq", "lat", "lon"),
        P(None, "freq", "lat", "lon"),
        P("lat", "lon"),
        P("lat", "lon"),
        P("lat", "lon"),
    )
    return jax.shard_map(
        local, mesh=mesh, in_specs=placed, out_specs=P(None, "freq", "lat", "lon"), check_vma=False
    )
```
